256 devices in a mesh: box: 16 (over z, core), agg: 16 (over y, x).
Axes of the slice: x: 4, y: 4, z: 8, core: 2. Of those that a mesh axis runs over, the one named last changes fastest.
Arguments:
- source: float32 [512, 512, 128], P('box', 'agg'), may hold values from -6 to 6
- guess: float32 [512, 512, 128], P('box', 'agg'), may hold values from -6 to 6
- reaction: float32 [512, 512, 128], P('box', 'agg'), may hold values from 0.001 to 0.02
- flags: int32 [16, 16, 4], P('box', 'agg'), may hold values from 0 to 1, as said below
Outputs:
- iterate: float32 [512, 512, 128], P('box', 'agg')
- level_one: float32 [256, 256, 64], P('box', 'agg')
- level_two: float32 [128, 128, 32], P('box', 'agg')
- level_three: float32 [64, 64, 16], P('box', 'agg')
- level_four: float32 [32, 32, 8], P('box', 'agg')
- bottom_residual: float32 [32, 32, 8], P('box', 'agg')
The draws below stay inside these ranges and needn't reach their ends.
Inputs may be any that keep to these rules, and one draw needn't show every extreme that they name: `flags`: flags are 0 or 1; the share of refined boxes differs from device block to device block, and some blocks have none.
All inputs are finite; a program needn't handle non-finite values.
Results may differ from the reference program's by a relative error of at most 0.00018.
Values sent between devices are 32-bit elements; how exact they have to be, the bound alone decides.
No kernel may reach another device: no remote copies, remote signals or barrier semaphores. Data moves between devices by JAX's collectives and lax.ppermute only.
A program may use at most 128 MiB of HBM per device.

```python
import math
import jax
import jax.numpy as jnp

CX = 32
CY = 32
CZ = 128
PATCH = 32
LEVELS = 4
NX = 512
NY = 512


def draw_flags(key, part):
    key_device = jax.random.fold_in(key, 11)
    key_boxes = jax.random.fold_in(key, 12)
    refine_level = jax.random.randint(key_device, (NX // CX, NY // CY, 1), 0, 4)
    refine_level = jnp.repeat(jnp.repeat(refine_level, CX // PATCH, axis=0), CY // PATCH, axis=1)
    chance = jax.random.randint(key_boxes, (NX // PATCH, NY // PATCH, CZ // PATCH), 0, 4)
    return (chance < refine_level).astype(jnp.int32)


def block_levels(rng, shape, pieces, smallest, high):
    level, own = 1.0, jax.random.fold_in(rng, 6)
    for dim, blocks in pieces:
        draws = jnp.exp(jax.random.uniform(jax.random.fold_in(own, dim), (blocks,), jnp.float32, smallest / len(pieces), high / len(pieces)))
        level = level * jnp.repeat(draws, shape[dim] // blocks).reshape([-1 if axis == dim else 1 for axis in range(len(shape))])
    return level


def gaussian(own_key, dims, width, most, pieces=(), held_as=jnp.bfloat16):
    entries = jax.random.normal(own_key, dims, jnp.float32) * width
    if len(pieces) > 0:
        entries = block_levels(own_key, dims, pieces, -0.22, 0.18) * entries
    return jnp.clip(entries, min=-most, max=most).astype(held_as)


def setup_inputs(seed: int = 0) -> dict:
    arg_keys = jax.random.split(jax.random.key(seed), 5)
    return {
        "source": gaussian(arg_keys[0], (NX, NY, CZ), 1.0, 6.0, ((0, 16), (1, 16)), jnp.float32),
        "guess": gaussian(arg_keys[1], (NX, NY, CZ), 1.0, 6.0, ((0, 16), (1, 16)), jnp.float32),
        "reaction": jnp.clip(jnp.exp(math.log(0.02) - 2.9957322 * jax.random.uniform(arg_keys[2], (NX, NY, CZ), jnp.float32) ** block_levels(arg_keys[2], (NX, NY, CZ), ((0, 16), (1, 16)), -0.2, 0.2)), 0.001, 0.02),
        "flags": draw_flags(jax.random.fold_in(arg_keys[4], 71), 0),
    }


def neighbours(padded):
    count_x = padded.shape[0] - 2
    count_y = padded.shape[1] - 2
    count_z = padded.shape[2] - 2
    face_sum = jnp.zeros((count_x, count_y, count_z), jnp.float32)
    edge_sum = jnp.zeros((count_x, count_y, count_z), jnp.float32)
    corner_sum = jnp.zeros((count_x, count_y, count_z), jnp.float32)
    for step_x in (-1, 0, 1):
        for step_y in (-1, 0, 1):
            for step_z in (-1, 0, 1):
                moved = abs(step_x) + abs(step_y) + abs(step_z)
                if moved == 0:
                    continue
                window = padded[1 + step_x:1 + step_x + count_x, 1 + step_y:1 + step_y + count_y, 1 + step_z:1 + step_z + count_z]
                if moved == 1:
                    face_sum = face_sum + window
                elif moved == 2:
                    edge_sum = edge_sum + window
                else:
                    corner_sum = corner_sum + window
    return (face_sum + 0.5 * edge_sum + 0.25 * corner_sum) / 14.0


def operate(values, coefficient):
    padded = jnp.pad(values, 1)
    return values - neighbours(padded) + coefficient * values


def restrict(values):
    size_a, size_b, size_c = values.shape
    return values.reshape(size_a // 2, 2, size_b // 2, 2, size_c // 2, 2).sum(axis=(1, 3, 5)) * 0.5


def cell_mask(flags, shape):
    boxes_x, boxes_y, boxes_z = flags.shape
    spread = jnp.broadcast_to(flags.astype(jnp.float32)[:, None, :, None, :, None], (boxes_x, shape[0] // boxes_x, boxes_y, shape[1] // boxes_y, boxes_z, shape[2] // boxes_z))
    return spread.reshape(shape)


def coefficients(level_index):
    upper_edge = 1.1 * (2.0 + 0.02 * 4.0 ** level_index)
    lower_edge = upper_edge / 8.0
    midpoint = (upper_edge + lower_edge) / 2.0
    half_span = (upper_edge - lower_edge) / 2.0
    sigma_value = midpoint / half_span
    rho_first = 1.0 / sigma_value
    rho_second = 1.0 / (2.0 * sigma_value - rho_first)
    return midpoint, rho_second * rho_first, 2.0 * rho_second / half_span


def reference(source, guess, reaction, flags):
    refined = cell_mask(flags, source.shape)
    midpoint, factor_one, factor_two = coefficients(0)
    first_residual = refined * (source - operate(guess, reaction))
    first_step = first_residual / midpoint
    current = guess + first_step
    mid_residual = refined * (source - operate(current, reaction))
    second_step = factor_one * first_step + factor_two * mid_residual
    current = current + second_step
    residual = refined * (source - operate(current, reaction))
    results = [current]
    coarse_reaction = reaction
    for level_index in range(1, LEVELS + 1):
        coarse_source = restrict(residual)
        coarse_reaction = restrict(coarse_reaction)
        midpoint, factor_one, factor_two = coefficients(level_index)
        first_step = coarse_source / midpoint
        mid_residual = coarse_source - operate(first_step, coarse_reaction)
        second_step = factor_one * first_step + factor_two * mid_residual
        correction = first_step + second_step
        residual = coarse_source - operate(correction, coarse_reaction)
        results.append(correction)
    return (results[0], results[1], results[2], results[3], results[4], residual)
```

```python
import functools

import jax
import jax.numpy as jnp
from jax import lax
from jax.experimental import pallas as pl
from jax.experimental.pallas import tpu as pltpu
from jax.sharding import PartitionSpec as P

F32 = jnp.float32
LANES = 128
FAR = 14


def coefficients(level_index):
    upper_edge = 1.1 * (2.0 + 0.02 * 4.0**level_index)
    lower_edge = upper_edge / 8.0
    midpoint = (upper_edge + lower_edge) / 2.0
    half_span = (upper_edge - lower_edge) / 2.0
    sigma_value = midpoint / half_span
    rho_first = 1.0 / sigma_value
    rho_second = 1.0 / (2.0 * sigma_value - rho_first)
    return (midpoint, rho_second * rho_first, 2.0 * rho_second / half_span)


def iota(shape, dim):
    return lax.broadcasted_iota(jnp.int32, shape, dim)


def edges(axis):
    here = lax.axis_index(axis)
    before = jnp.where(here > 0, 1.0, 0.0).astype(F32)
    after = jnp.where(here < lax.axis_size(axis) - 1, 1.0, 0.0).astype(F32)
    return before, after


def blur_xy(below, here, above):
    rows = here.shape[0]
    total = (below + here) + (here + above)
    part = total + pltpu.roll(total, 1, 0)
    return part + pltpu.roll(part, rows - 1, 0)


def blur_z_full(values):
    lane = iota(values.shape, 1)
    part = values + jnp.where(lane == 0, 0.0, pltpu.roll(values, 1, 1))
    return part + jnp.where(lane == LANES - 1, values, pltpu.roll(part, LANES - 1, 1))


def blur_z_part(values):
    part = values + pltpu.roll(values, 1, 1)
    return part + pltpu.roll(part, LANES - 1, 1)


def pair_rows(values):
    return values + pltpu.roll(values, values.shape[0] - 1, 0)


def pair_matrix(first, count):
    source = iota((LANES, LANES), 0)
    target = iota((LANES, LANES), 1)
    hit = ((source - first) >> 1 == target) & (source >= first) & (target < count)
    return jnp.where(hit, 0.5, 0.0).astype(F32)


def exact_dot(a, b):
    return jnp.dot(a, b, precision=lax.Precision.HIGHEST, preferred_element_type=F32)


def flag_rows(flags_ref, rows):
    boxes = flags_ref.shape[2]
    lane = iota((rows, LANES), 1)
    out = jnp.zeros((rows, LANES), F32)
    for i in range(boxes):
        out = jnp.where(lane // (LANES // boxes) == i, flags_ref[0, 0, i].astype(F32), out)
    return out


def pack_rows(flags_ref, guess_lo, guess_hi, source_lo, source_hi, reaction_lo, reaction_hi, up, down):
    shape = up.shape
    row = iota(shape, 1)
    flag = flag_rows(flags_ref, 8)[None]
    up[...] = jnp.where(
        row >= 5,
        guess_hi[...],
        jnp.where(
            row >= 3,
            pltpu.roll(source_hi[...], 5, 1),
            jnp.where(row >= 1, pltpu.roll(reaction_hi[...], 3, 1), flag),
        ),
    )
    down[...] = jnp.where(
        row < 3,
        guess_lo[...],
        jnp.where(
            row < 5,
            pltpu.roll(source_lo[...], 3, 1),
            jnp.where(row < 7, pltpu.roll(reaction_lo[...], 5, 1), flag),
        ),
    )


def halo_tiles(from_before, from_after, before, after):
    row = iota(from_before.shape, 1)
    first = row < 4
    guess = jnp.where(first, from_after * after, from_before * before)
    source = jnp.where(first, pltpu.roll(from_after, 5, 1), pltpu.roll(from_before, 3, 1))
    reaction = jnp.where(first, pltpu.roll(from_after, 3, 1), pltpu.roll(from_before, 5, 1))
    return guess, source, reaction


def mask_plane(flags_ref, from_before, from_after, before, after):
    tile = from_before[0].shape
    row = iota(tile, 0)
    lo = jnp.broadcast_to(from_before[0][0:1] * before, tile)
    hi = jnp.broadcast_to(from_after[0][7:8] * after, tile)
    return flag_rows(flags_ref, 32), jnp.where(row < 4, hi, lo)


def pack_planes(
    flags_ref, from_before, from_after, guess_lo, guess_hi, source_lo, source_hi, reaction_lo, reaction_hi, up, down
):
    before, after = edges("agg")
    own_mask, halo_mask = mask_plane(flags_ref, from_before, from_after, before, after)
    planes = from_before.shape[0]
    for target, first, fields, local in (
        (up, planes - 4, (guess_hi, source_hi, reaction_hi), (1, 2, 2)),
        (down, 0, (guess_lo, source_lo, reaction_lo), (0, 0, 0)),
    ):
        tiles = halo_tiles(from_before[first : first + 4], from_after[first : first + 4], before, after)
        at = 0
        for field, tile, start, count in zip(fields, tiles, local, (3, 2, 2)):
            for i in range(count):
                target[at, 0:32, :] = field[start + i]
                target[at, 32:40, :] = tile[start + i]
                at += 1
        target[at, 0:32, :] = own_mask
        target[at, 32:40, :] = halo_mask


def fine_kernel(
    flags_ref, from_before, from_after, x_before, x_after, guess, source, reaction,
    iterate, coarse, g, s, k, d, u, w, m, pairs, kpairs,
):
    before, after = edges("agg")
    xbefore, xafter = edges("box")
    own_mask, halo_mask = mask_plane(flags_ref, from_before, from_after, before, after)
    m[0] = x_before[7] * xbefore
    m[1, 0:32, :] = own_mask
    m[1, 32:40, :] = halo_mask
    m[2] = x_after[7] * xafter
    g[0:3] = x_before[0:3] * xbefore
    g[35:38] = x_after[0:3] * xafter
    s[1:3] = x_before[3:5]
    s[35:37] = x_after[3:5]
    shift = 8.0 / 7.0
    k[1:3] = x_before[5:7] + shift
    k[35:37] = x_after[5:7] + shift

    def assemble(i, carry):
        tiles = halo_tiles(from_before[pl.ds(i * 4, 4)], from_after[pl.ds(i * 4, 4)], before, after)
        at = pl.ds(3 + i * 4, 4)
        mine = pl.ds(i * 4, 4)
        g[at, 0:32, :] = guess[mine]
        g[at, 32:40, :] = tiles[0]
        s[at, 0:32, :] = source[mine]
        s[at, 32:40, :] = tiles[1]
        k[at, 0:32, :] = reaction[mine] + shift
        k[at, 32:40, :] = tiles[2] + shift
        return carry

    lax.fori_loop(0, 8, assemble, 0)
    theta, c1, c2 = coefficients(0)

    def remainder(field, x):
        region = jnp.where(x < 3, 0, jnp.where(x < 35, 1, 2))
        middle = field[x]
        q = blur_z_full(blur_xy(field[x - 1], middle, field[x + 1]))
        return m[region] * (s[x] - k[x] * middle + q * (1.0 / 56.0)), middle

    def first(x, carry):
        r, middle = remainder(g, x)
        step = r * (1.0 / theta)
        d[x] = step
        u[x] = middle + step
        return carry

    lax.fori_loop(1, 37, first, 0)

    def second(x, carry):
        r, middle = remainder(u, x)
        w[x] = middle + (c1 * d[x] + c2 * r)
        return carry

    lax.fori_loop(2, 36, second, 0)

    def third(i, carry):
        x = 3 + 2 * i
        r0, middle0 = remainder(w, x)
        r1, middle1 = remainder(w, x + 1)
        iterate[2 * i] = middle0[0:32]
        iterate[2 * i + 1] = middle1[0:32]
        pairs[i] = pair_rows(r0 + r1)
        kpairs[i] = pair_rows(reaction[2 * i] + reaction[2 * i + 1])
        return carry

    lax.fori_loop(0, 16, third, 0)
    rf = jnp.concatenate([pairs[i, pl.ds(0, 16, stride=2), :] for i in range(16)], axis=0)
    rk = jnp.concatenate([kpairs[i, pl.ds(0, 16, stride=2), :] for i in range(16)], axis=0)
    to_low = pair_matrix(0, 64)
    to_high = pltpu.roll(to_low, 64, 1)
    coarse[...] = (exact_dot(rf, to_low) + exact_dot(rk, to_high)).reshape(16, 16, LANES)


def level_constants(level):
    theta, c1, c2 = coefficients(level)
    return (1.0 + c1) / theta + c2, c2 / theta


def coarse_kernel(
    y_before, own, y_after, x_before, x_after, e1, e2, e3, f4, k4,
    f, k, e, m, pairs, kpairs, fb, kb, eb, mb, fc, kc, ec, mc,
):
    before, after = edges("agg")
    xbefore, xafter = edges("box")
    shift = 8.0 / 7.0

    def masks(ref, rows, lo, hi, lanes):
        shape = (rows, LANES)
        row = iota(shape, 0)
        inside = jnp.where(row < lo, before, jnp.where(row >= hi, after, 1.0))
        inside = jnp.where(iota(shape, 1) < lanes, inside, 0.0)
        ref[0] = inside * xbefore
        ref[1] = inside
        ref[2] = inside * xafter

    masks(m, 48, 16, 32, 64)
    masks(mb, 32, 8, 16, 32)
    masks(mc, 16, 4, 8, 16)

    def take(x, block, region):
        f[x] = block * m[region]
        k[x] = pltpu.roll(block, 64, 1)

    def take_before(i, carry):
        take(i, x_before[i], 0)
        take(30 + i, x_after[i], 2)
        return carry

    lax.fori_loop(0, FAR, take_before, 0)

    def take_own(i, carry):
        take(FAR + i, jnp.concatenate([y_before[i], own[i], y_after[i]], axis=0), 1)
        return carry

    lax.fori_loop(0, 16, take_own, 0)

    def correct(level, f, k, e, m, x, lo, hi):
        alpha, beta = level_constants(level)
        region = jnp.where(x < lo, 0, jnp.where(x < hi, 1, 2))
        middle = f[x]
        q = blur_z_part(blur_xy(f[x - 1], middle, f[x + 1]))
        kk = k[x] + shift
        e[x] = m[region] * (middle * (alpha - beta * kk) + q * (beta / 56.0))

    def remainder(f, k, e, x):
        middle = e[x]
        q = blur_z_part(blur_xy(e[x - 1], middle, e[x + 1]))
        return f[x] - (k[x] + shift) * middle + q * (1.0 / 56.0)

    def one(x, carry):
        correct(1, f, k, e, m, x, 14, 30)
        return carry

    lax.fori_loop(1, 43, one, 0)

    def two(i, carry):
        x = 2 + 2 * i
        pairs[i, 0:48, :] = pair_rows(remainder(f, k, e, x) + remainder(f, k, e, x + 1))
        kpairs[i, 0:48, :] = pair_rows(k[x] + k[x + 1])
        return carry

    lax.fori_loop(0, 20, two, 0)
    e1[...] = e[14:30, 16:32, 0:64]
    to_low = pair_matrix(0, 32)
    rf = jnp.concatenate([pairs[i, pl.ds(0, 24, stride=2), :] for i in range(20)], axis=0)
    rk = jnp.concatenate([kpairs[i, pl.ds(0, 24, stride=2), :] for i in range(20)], axis=0)
    rf = exact_dot(rf, to_low).reshape(20, 24, LANES)
    rk = exact_dot(rk, to_low).reshape(20, 24, LANES)
    for region, start, stop in ((0, 0, 6), (1, 6, 14), (2, 14, 20)):
        fb[start:stop, 0:24, :] = rf[start:stop] * mb[region, 0:24, :]
    kb[:, 0:24, :] = rk
    fb[:, 24:32, :] = jnp.zeros((20, 8, LANES), F32)
    kb[:, 24:32, :] = jnp.zeros((20, 8, LANES), F32)

    def three(x, carry):
        correct(2, fb, kb, eb, mb, x, 6, 14)
        return carry

    lax.fori_loop(1, 19, three, 0)
    e2[...] = eb[6:14, 8:16, 0:32]

    def four(i, carry):
        x = 2 + 2 * i
        pairs[i, 0:32, :] = pair_rows(remainder(fb, kb, eb, x) + remainder(fb, kb, eb, x + 1))
        kpairs[i, 0:32, :] = pair_rows(kb[x] + kb[x + 1])
        return carry

    lax.fori_loop(0, 8, four, 0)
    to_low = pair_matrix(0, 16)
    rf = jnp.concatenate([pairs[i, pl.ds(0, 16, stride=2), :] for i in range(8)], axis=0)
    rk = jnp.concatenate([kpairs[i, pl.ds(0, 16, stride=2), :] for i in range(8)], axis=0)
    rf = exact_dot(rf, to_low).reshape(8, 16, LANES)
    rk = exact_dot(rk, to_low).reshape(8, 16, LANES)
    for region, start, stop in ((0, 0, 2), (1, 2, 6), (2, 6, 8)):
        fc[start:stop] = rf[start:stop] * mc[region]
    kc[...] = rk
    for x in range(1, 7):
        correct(3, fc, kc, ec, mc, x, 2, 6)
    e3[...] = ec[2:6, 4:8, 0:16]
    for i in range(2):
        x = 2 + 2 * i
        pairs[i, 0:16, :] = pair_rows(remainder(fc, kc, ec, x) + remainder(fc, kc, ec, x + 1))
    for i in range(4):
        kpairs[i, 0:16, :] = pair_rows(kc[2 * i] + kc[2 * i + 1])
    to_low = pair_matrix(0, 8)
    rf = jnp.concatenate([pairs[i, pl.ds(0, 8, stride=2), :] for i in range(2)], axis=0)
    rk = jnp.concatenate([kpairs[i, pl.ds(0, 8, stride=2), :] for i in range(4)], axis=0)
    f4[...] = exact_dot(rf, to_low).reshape(2, 8, LANES)
    k4[...] = exact_dot(rk, to_low).reshape(4, 8, LANES)


def pack_last(y_before, own, y_after, out):
    before, after = edges("agg")
    row = iota(own.shape, 1)
    lo = pltpu.roll(y_before[...], 6, 1) * before
    hi = pltpu.roll(y_after[...], 2, 1) * after
    out[...] = jnp.where(row < 2, lo, jnp.where(row < 4, own[...], jnp.where(row < 6, hi, 0.0)))


def last_kernel(own, x_before, x_after, k4, e4, rest, f, e):
    before, after = edges("agg")
    xbefore, xafter = edges("box")
    shift = 8.0 / 7.0
    alpha, beta = level_constants(4)
    f[0:2] = x_before[...] * xbefore
    f[2:4] = own[...]
    f[4:6] = x_after[...] * xafter
    shape = (8, LANES)
    row = iota(shape, 0)
    inside = jnp.where(row < 2, before, jnp.where(row >= 4, after, 1.0))
    inside = jnp.where((iota(shape, 1) < 8) & (row < 6), inside, 0.0)
    for x in range(1, 5):
        middle = f[x]
        q = blur_z_part(blur_xy(f[x - 1], middle, f[x + 1]))
        value = inside * (middle * (alpha - beta * (k4[x - 1] + shift)) + q * (beta / 56.0))
        e[x] = value * xbefore if x == 1 else value * xafter if x == 4 else value
    for x in (2, 3):
        middle = e[x]
        q = blur_z_part(blur_xy(e[x - 1], middle, e[x + 1]))
        left = f[x] - (k4[x - 1] + shift) * middle + q * (1.0 / 56.0)
        e4[x - 2] = middle[2:4, 0:8]
        rest[x - 2] = left[2:4, 0:8]


def neighbours_of(up, down, axis):
    count = lax.axis_size(axis)
    ahead = [(i, (i + 1) % count) for i in range(count)]
    back = [(i, (i - 1) % count) for i in range(count)]
    return lax.ppermute(up, axis, ahead), lax.ppermute(down, axis, back)


def shaped(*dims):
    return jax.ShapeDtypeStruct(dims, F32)


def call(body, out_shape, scratch=(), in_specs=None, grid=None, out_specs=None, name=None):
    extra = {}
    if in_specs is not None:
        extra["in_specs"] = in_specs
    if grid is not None:
        extra["grid"] = grid
        extra["out_specs"] = out_specs
    return pl.pallas_call(
        body,
        out_shape=out_shape,
        scratch_shapes=[pltpu.VMEM(dims, F32) for dims in scratch],
        compiler_params=pltpu.CompilerParams(vmem_limit_bytes=40 * 1024 * 1024),
        name=name,
        **extra,
    )


def per_device(source, guess, reaction, flags):
    smem = pl.BlockSpec(memory_space=pltpu.SMEM)
    vmem = pl.BlockSpec(memory_space=pltpu.VMEM)
    rows_lo = pl.BlockSpec((32, 8, LANES), lambda i: (0, 0, 0))
    rows_hi = pl.BlockSpec((32, 8, LANES), lambda i: (0, 3, 0))
    whole = pl.BlockSpec((32, 8, LANES), lambda i: (0, 0, 0))
    up, down = call(
        pack_rows,
        (shaped(32, 8, LANES), shaped(32, 8, LANES)),
        in_specs=[smem, rows_lo, rows_hi, rows_lo, rows_hi, rows_lo, rows_hi],
        grid=(1,),
        out_specs=(whole, whole),
        name="pack_rows",
    )(flags, guess, guess, source, source, reaction, reaction)
    y_before, y_after = neighbours_of(up, down, "agg")
    planes_lo = pl.BlockSpec((4, 32, LANES), lambda i: (0, 0, 0))
    planes_hi = pl.BlockSpec((4, 32, LANES), lambda i: (7, 0, 0))
    strip = pl.BlockSpec((8, 40, LANES), lambda i: (0, 0, 0))
    up, down = call(
        pack_planes,
        (shaped(8, 40, LANES), shaped(8, 40, LANES)),
        in_specs=[smem, whole, whole, planes_lo, planes_hi, planes_lo, planes_hi, planes_lo, planes_hi],
        grid=(1,),
        out_specs=(strip, strip),
        name="pack_planes",
    )(flags, y_before, y_after, guess, guess, source, source, reaction, reaction)
    x_before, x_after = neighbours_of(up, down, "box")
    big = (38, 40, LANES)
    iterate, coarse = call(
        fine_kernel,
        (shaped(32, 32, LANES), shaped(16, 16, LANES)),
        scratch=[big] * 6 + [(3, 40, LANES), (16, 40, LANES), (16, 32, LANES)],
        in_specs=[smem] + [vmem] * 7,
        name="fine",
    )(flags, y_before, y_after, x_before, x_after, guess, source, reaction)
    y_before, y_after = neighbours_of(coarse, coarse, "agg")
    extended = jnp.concatenate([y_before, coarse, y_after], axis=1)
    x_before, x_after = neighbours_of(extended[16 - FAR :], extended[:FAR], "box")
    e1, e2, e3, f4, k4 = call(
        coarse_kernel,
        (shaped(16, 16, 64), shaped(8, 8, 32), shaped(4, 4, 16), shaped(2, 8, LANES), shaped(4, 8, LANES)),
        scratch=[(44, 48, LANES)] * 3 + [(3, 48, LANES), (20, 48, LANES), (20, 48, LANES)]
        + [(20, 32, LANES)] * 3 + [(3, 32, LANES)] + [(8, 16, LANES)] * 3 + [(3, 16, LANES)],
        name="coarse",
    )(y_before, coarse, y_after, x_before, x_after)
    y_before, y_after = neighbours_of(f4, f4, "agg")
    last = call(pack_last, shaped(2, 8, LANES), name="pack_last")(y_before, f4, y_after)
    x_before, x_after = neighbours_of(last, last, "box")
    e4, rest = call(
        last_kernel,
        (shaped(2, 2, 8), shaped(2, 2, 8)),
        scratch=[(6, 8, LANES), (6, 8, LANES)],
        name="last",
    )(last, x_before, x_after, k4)
    return iterate, e1, e2, e3, e4, rest


def solution(mesh):
    spec = P("box", "agg", None)
    return jax.shard_map(
        per_device, mesh=mesh, in_specs=(spec,) * 4, out_specs=(spec,) * 6, check_vma=False
    )
```

```python
import functools

import jax
import jax.numpy as jnp
from jax import lax
from jax.experimental import pallas as pl
from jax.experimental.pallas import tpu as pltpu
from jax.sharding import PartitionSpec as P

F32 = jnp.float32
LANES = 128
FAR = 14


def coefficients(level_index):
    upper_edge = 1.1 * (2.0 + 0.02 * 4.0**level_index)
    lower_edge = upper_edge / 8.0
    midpoint = (upper_edge + lower_edge) / 2.0
    half_span = (upper_edge - lower_edge) / 2.0
    sigma_value = midpoint / half_span
    rho_first = 1.0 / sigma_value
    rho_second = 1.0 / (2.0 * sigma_value - rho_first)
    return (midpoint, rho_second * rho_first, 2.0 * rho_second / half_span)


def iota(shape, dim):
    return lax.broadcasted_iota(jnp.int32, shape, dim)


def edges(axis):
    here = lax.axis_index(axis)
    before = jnp.where(here > 0, 1.0, 0.0).astype(F32)
    after = jnp.where(here < lax.axis_size(axis) - 1, 1.0, 0.0).astype(F32)
    return before, after


def blurred(planes, blur_z):
    sums = [a + b for a, b in zip(planes[:-1], planes[1:])]
    out = []
    for low, high in zip(sums[:-1], sums[1:]):
        total = low + high
        part = total + pltpu.roll(total, 1, 0)
        out.append(blur_z(part + pltpu.roll(part, part.shape[0] - 1, 0)))
    return out


def blur_z_full(values):
    lane = iota(values.shape, 1)
    part = values + jnp.where(lane == 0, 0.0, pltpu.roll(values, 1, 1))
    return part + jnp.where(lane == LANES - 1, values, pltpu.roll(part, LANES - 1, 1))


def blur_z_halves(values):
    lane = iota(values.shape, 1) & 63
    part = values + jnp.where(lane == 0, 0.0, pltpu.roll(values, 1, 1))
    return part + jnp.where(lane == 63, values, pltpu.roll(part, LANES - 1, 1))


def blur_z_part(values):
    part = values + pltpu.roll(values, 1, 1)
    return part + pltpu.roll(part, LANES - 1, 1)


def pair_rows(values):
    return values + pltpu.roll(values, values.shape[0] - 1, 0)


def pair_matrix():
    source = iota((LANES, LANES), 0)
    target = iota((LANES, LANES), 1)
    return jnp.where(source >> 1 == target, 0.5, 0.0).astype(F32)


def pair_matrix_halves():
    source = iota((LANES, LANES), 0)
    target = iota((LANES, LANES), 1)
    hit = ((source & 64) == (target & 64)) & ((source & 63) >> 1 == (target & 63))
    return jnp.where(hit, 0.5, 0.0).astype(F32)


def exact_dot(a, b):
    return jnp.dot(a, b, precision=lax.Precision.HIGHEST, preferred_element_type=F32)


def loop(first, stop, size, body):
    count = (stop - first) // size

    def step(i, carry):
        body(first + i * size)
        return carry

    lax.fori_loop(0, count, step, 0)


def copy_all(sems, *pairs):
    copies = [pltpu.make_async_copy(a, b, sems.at[i]) for i, (a, b) in enumerate(pairs)]
    for copy in copies:
        copy.start()
    return copies


def pack_rows(
    flags, guess, source, reaction, up, down, strip_up, strip_down,
    flag_smem, guess_lo, guess_hi, source_lo, source_hi, reaction_lo, reaction_hi, sems,
):
    lo, hi = pl.ds(0, 8), pl.ds(24, 8)
    copies = copy_all(
        sems,
        (flags, flag_smem),
        (guess.at[:, lo, :], guess_lo),
        (guess.at[:, hi, :], guess_hi),
        (source.at[:, lo, :], source_lo),
        (source.at[:, hi, :], source_hi),
        (reaction.at[:, lo, :], reaction_lo),
        (reaction.at[:, hi, :], reaction_hi),
        (guess.at[29:32], strip_up.at[0:3]),
        (source.at[30:32], strip_up.at[3:5]),
        (reaction.at[30:32], strip_up.at[5:7]),
        (guess.at[0:3], strip_down.at[0:3]),
        (source.at[0:2], strip_down.at[3:5]),
        (reaction.at[0:2], strip_down.at[5:7]),
    )
    for copy in copies[:7]:
        copy.wait()
    boxes = flags.shape[2]
    lane = iota((8, LANES), 1)
    flag = jnp.zeros((8, LANES), F32)
    for i in range(boxes):
        flag = jnp.where(lane // (LANES // boxes) == i, flag_smem[0, 0, i].astype(F32), flag)
    flag = flag[None]
    row = iota(up.shape, 1)
    up[...] = jnp.where(
        row >= 5,
        guess_hi[...],
        jnp.where(
            row >= 3,
            pltpu.roll(source_hi[...], 5, 1),
            jnp.where(row >= 1, pltpu.roll(reaction_hi[...], 3, 1), flag),
        ),
    )
    down[...] = jnp.where(
        row < 3,
        guess_lo[...],
        jnp.where(
            row < 5,
            pltpu.roll(source_lo[...], 3, 1),
            jnp.where(row < 7, pltpu.roll(reaction_lo[...], 5, 1), flag),
        ),
    )
    for copy in copies[7:]:
        copy.wait()


def halo_tiles(from_before, from_after, before, after):
    row = iota(from_before.shape, 1)
    first = row < 4
    guess = jnp.where(first, from_after * after, from_before * before)
    source = jnp.where(first, pltpu.roll(from_after, 5, 1), pltpu.roll(from_before, 3, 1))
    reaction = jnp.where(first, pltpu.roll(from_after, 3, 1), pltpu.roll(from_before, 5, 1))
    return guess, source, reaction


def pack_planes(own, from_before, from_after, strip_up, strip_down, up, down):
    before, after = edges("agg")
    tile = (8, LANES)
    own_mask = jnp.broadcast_to(own[0, 0:1, :], (32, LANES))
    lo_mask = jnp.broadcast_to(from_before[0, 0:1, :] * before, tile)
    hi_mask = jnp.broadcast_to(from_after[0, 7:8, :] * after, tile)
    halo_mask = jnp.where(iota(tile, 0) < 4, hi_mask, lo_mask)
    planes = from_before.shape[0]
    for target, strip, first, local in (
        (up, strip_up, planes - 4, (1, 2, 2)),
        (down, strip_down, 0, (0, 0, 0)),
    ):
        tiles = halo_tiles(from_before[first : first + 4], from_after[first : first + 4], before, after)
        target[0:7, 0:32, :] = strip[...]
        at = 0
        for tile, start, count in zip(tiles, local, (3, 2, 2)):
            target[at : at + count, 32:40, :] = tile[start : start + count]
            at += count
        target[7, 0:32, :] = own_mask
        target[7, 32:40, :] = halo_mask


SHIFT = 8.0 / 7.0


def compact(values, ref, rows):
    return jnp.concatenate([ref[i, pl.ds(0, rows, stride=2), :] for i in values], axis=0)


def fine_inner(
    packed, from_before, from_after, guess, source, reaction,
    g, s, k, d, u, w, coarse, pairs, kpairs, sems,
):
    rows = pl.ds(0, 32)
    copies = copy_all(
        sems, (guess, g.at[:, rows, :]), (source, s.at[:, rows, :]), (reaction, k.at[:, rows, :])
    )
    before, after = edges("agg")
    theta, c1, c2 = coefficients(0)

    def assemble(x):
        at = pl.ds(x, 8)
        tiles = halo_tiles(from_before[at], from_after[at], before, after)
        g[at, 32:40, :] = tiles[0]
        s[at, 32:40, :] = tiles[1]
        k[at, 32:40, :] = tiles[2]

    loop(0, 32, 8, assemble)
    for copy in copies:
        copy.wait()

    def remainders(field, x, size):
        planes = [field[x + i] for i in range(-1, size + 1)]
        mask = packed[7]
        out = []
        for i, q in enumerate(blurred(planes, blur_z_full)):
            r = mask * (s[x + i] - (k[x + i] + SHIFT) * planes[i + 1] + q * (1.0 / 56.0))
            out.append((r, planes[i + 1]))
        return out

    def first(x):
        out = remainders(g, x, 3)
        for i, (r, middle) in enumerate(out):
            step = r * (1.0 / theta)
            d[x + i] = step
            u[x + i] = middle + step

    loop(1, 31, 3, first)

    def second(x):
        out = [m + (c1 * d[x + i] + c2 * r) for i, (r, m) in enumerate(remainders(u, x, 4))]
        for i, value in enumerate(out):
            w[x + i] = value

    loop(2, 30, 4, second)

    def third(x):
        out = [r for r, _ in remainders(w, x, 4)]
        at = (x - 4) // 2
        pairs[at] = pair_rows(out[0] + out[1])
        pairs[at + 1] = pair_rows(out[2] + out[3])

    loop(4, 28, 4, third)

    def fourth(i):
        out = [pair_rows(k[2 * i + 2 * j, 0:32, :] + k[2 * i + 2 * j + 1, 0:32, :]) for j in range(4)]
        for j, value in enumerate(out):
            kpairs[i + j] = value

    loop(0, 16, 4, fourth)
    to_low = pair_matrix()
    rk = exact_dot(compact(range(16), kpairs, 16), pltpu.roll(to_low, 64, 1)).reshape(16, 16, LANES)
    rf = exact_dot(compact(range(12), pairs, 16), to_low).reshape(12, 16, LANES)
    coarse[0:2] = rk[0:2]
    coarse[2:14] = rk[2:14] + rf
    coarse[14:16] = rk[14:16]


def fine_outer(packed, x_before, x_after, g, s, k, d, u, w, inner, coarse, edge, pairs):
    xbefore, xafter = edges("box")
    theta, c1, c2 = coefficients(0)
    new_d, new_u, new_w = {}, {}, {}

    def side(x, before, after, own):
        return before(x + 3) if x < 0 else after(x - 32) if x > 31 else own(x)

    def guess_at(x):
        return side(x, lambda i: x_before[i] * xbefore, lambda i: x_after[i] * xafter, lambda i: g[i])

    def source_at(x):
        return side(x, lambda i: x_before[i + 2], lambda i: x_after[i + 3], lambda i: s[i])

    def reaction_at(x):
        return side(x, lambda i: x_before[i + 4], lambda i: x_after[i + 5], lambda i: k[i])

    def mask_at(x):
        return side(x, lambda i: x_before[7] * xbefore, lambda i: x_after[7] * xafter, lambda i: packed[7])

    def remainders(field, first, size):
        planes = [field(x) for x in range(first - 1, first + size + 1)]
        out = []
        for i, q in enumerate(blurred(planes, blur_z_full)):
            x = first + i
            r = mask_at(x) * (source_at(x) - (reaction_at(x) + SHIFT) * planes[i + 1] + q * (1.0 / 56.0))
            out.append((x, r, planes[i + 1]))
        return out

    for first in (-2, 31):
        for x, r, middle in remainders(guess_at, first, 3):
            new_d[x] = r * (1.0 / theta)
            new_u[x] = middle + new_d[x]
    for first in (-1, 30):
        for x, r, middle in remainders(lambda i: new_u[i] if i in new_u else u[i], first, 3):
            step = new_d[x] if x in new_d else d[x]
            new_w[x] = middle + (c1 * step + c2 * r)
    for at, x in enumerate((0, 1, 30, 31)):
        edge[at] = new_w[x][0:32]
    for at, first in enumerate((0, 28)):
        out = [r for _, r, _ in remainders(lambda i: new_w[i] if i in new_w else w[i], first, 4)]
        pairs[2 * at] = pair_rows(out[0] + out[1])
        pairs[2 * at + 1] = pair_rows(out[2] + out[3])
    rf = exact_dot(compact(range(4), pairs, 16), pair_matrix()).reshape(4, 16, LANES)
    coarse[0:2] = inner[0:2] + rf[0:2]
    coarse[2:14] = inner[2:14]
    coarse[14:16] = inner[14:16] + rf[2:4]


def level_constants(level):
    theta, c1, c2 = coefficients(level)
    return (1.0 + c1) / theta + c2, c2 / theta


def low_half(shape):
    return iota(shape, len(shape) - 1) < 64


def masks_of(rows, lo, hi, lanes):
    before, after = edges("agg")
    xbefore, xafter = edges("box")
    shape = (rows, LANES)
    row = iota(shape, 0)
    inside = jnp.where(row < lo, before, jnp.where(row >= hi, after, 1.0))
    inside = jnp.where((iota(shape, 1) & 63) < lanes, inside, 0.0)
    return inside * jnp.where(low_half(shape), xbefore, xafter), inside


def corrections(level, planes, reactions, masks, blur_z):
    alpha, beta = level_constants(level)
    return [
        m * (f * (alpha - beta * (k + SHIFT)) + q * (beta / 56.0))
        for f, k, m, q in zip(planes[1:-1], reactions, masks, blurred(planes, blur_z))
    ]


def coarse_remainders(planes, fields, reactions, blur_z):
    return [
        f - (k + SHIFT) * e + q * (1.0 / 56.0)
        for f, k, e, q in zip(fields, reactions, planes[1:-1], blurred(planes, blur_z))
    ]


def swap(values):
    return pltpu.roll(values, 64, 1)


def coarse_inner(y_before, own, y_after, f, k, e, f2, k2, pairs, kpairs):
    _, inside = masks_of(48, 16, 32, 64)
    low = low_half((48, LANES))
    for j in range(8):
        lo = jnp.concatenate([y_before[j], own[j], y_after[j]], axis=0)
        hi = jnp.concatenate([y_before[15 - j], own[15 - j], y_after[15 - j]], axis=0)
        f[j] = jnp.where(low, lo, swap(hi)) * inside
        k[j] = jnp.where(low, swap(lo), hi)
    fields = [f[j] for j in range(8)]
    reactions = [k[j] for j in range(8)]
    value = corrections(1, fields + [swap(fields[7])], reactions[1:], [inside] * 7, blur_z_halves)
    for j in range(7):
        e[j + 1] = value[j]
    rest = coarse_remainders(value + [swap(value[6])], fields[2:], reactions[2:], blur_z_halves)
    for j in range(3):
        pairs[j] = pair_rows(rest[2 * j] + rest[2 * j + 1])
        kpairs[j] = pair_rows(reactions[2 * j + 2] + reactions[2 * j + 3])
    halve = pair_matrix_halves()
    _, inside = masks_of(24, 8, 16, 32)
    rf = exact_dot(compact(range(3), pairs, 24), halve).reshape(3, 24, LANES)
    for j in range(3):
        f2[j] = rf[j] * inside
    k2[...] = exact_dot(compact(range(3), kpairs, 24), halve).reshape(3, 24, LANES)


def coarse_outer(
    x_before, x_after, f_in, k_in, e_in, f2_in, k2_in, e1, e2, e3, f4, k4,
    f, k, e, pairs, kpairs,
):
    outside, inside = masks_of(48, 16, 32, 64)
    low = low_half((48, LANES))

    def take(j):
        out = []
        for i in range(2):
            lo, hi = x_before[j + i], x_after[13 - j - i]
            out.append((jnp.where(low, lo, swap(hi)) * outside, jnp.where(low, swap(lo), hi)))
        for i in range(2):
            f[j + i], k[j + i] = out[i]

    loop(0, 14, 2, take)
    for j in (0, 1):
        f[14 + j] = f_in[j]
        k[14 + j] = k_in[j]

    def one(j):
        out = corrections(
            1,
            [f[j + i] for i in range(-1, 4)],
            [k[j + i] for i in range(3)],
            [outside] * 3,
            blur_z_halves,
        )
        for i in range(3):
            e[j + i] = out[i]

    loop(1, 13, 3, one)
    value = corrections(1, [f[j] for j in range(12, 16)], [k[13], k[14]], [outside, inside], blur_z_halves)
    e[13], e[14] = value
    e[15] = e_in[1]
    e[16] = e_in[2]

    def two(j):
        out = coarse_remainders(
            [e[j + i] for i in range(-1, 3)],
            [f[j + i] for i in range(2)],
            [k[j + i] for i in range(2)],
            blur_z_halves,
        )
        p = (j - 2) // 2
        pairs[p] = pair_rows(out[0] + out[1])
        kpairs[p] = pair_rows(k[j] + k[j + 1])

    loop(2, 16, 2, two)
    half = slice(16, 32)
    e1[0] = e[14, half, 0:64]
    e1[15] = swap(e[14, half, :])[:, 0:64]
    for j in range(1, 8):
        value = e_in[j, half, :]
        e1[j] = value[:, 0:64]
        e1[15 - j] = swap(value)[:, 0:64]
    halve = pair_matrix_halves()
    rf = exact_dot(compact(range(7), pairs, 24), halve).reshape(7, 24, LANES)
    rk = exact_dot(compact(range(7), kpairs, 24), halve).reshape(7, 24, LANES)
    outside, inside = masks_of(24, 8, 16, 32)
    fields = [rf[j] * (outside if j < 6 else inside) for j in range(7)] + [f2_in[j] for j in range(3)]
    reactions = [rk[j] for j in range(7)] + [k2_in[j] for j in range(3)]
    value = corrections(
        2, fields + [swap(fields[9])], reactions[1:], [outside] * 5 + [inside] * 4, blur_z_part
    )
    for j in range(4):
        own = value[5 + j][8:16]
        e2[j] = own[:, 0:32]
        e2[7 - j] = swap(own)[:, 0:32]
    rest = coarse_remainders(value + [swap(value[8])], fields[2:], reactions[2:], blur_z_part)
    for p in range(4):
        pairs[p, 0:24, :] = pair_rows(rest[2 * p] + rest[2 * p + 1])
        kpairs[p, 0:24, :] = pair_rows(reactions[2 * p + 2] + reactions[2 * p + 3])
    rf = exact_dot(compact(range(4), pairs, 16), halve).reshape(4, 16, LANES)
    rk = exact_dot(compact(range(4), kpairs, 16), halve).reshape(4, 16, LANES)
    outside, inside = masks_of(16, 4, 8, 16)
    fields = [rf[0] * outside, rf[1] * outside, rf[2] * inside, rf[3] * inside]
    reactions = [rk[j] for j in range(4)]
    value = corrections(3, fields + [swap(fields[3])], reactions[1:], [outside, inside, inside], blur_z_part)
    for j in range(2):
        own = value[1 + j][0:8]
        e3[j] = own[4:8, 0:16]
        e3[3 - j] = swap(own)[4:8, 0:16]
    rest = coarse_remainders(value + [swap(value[2])], fields[2:], reactions[2:], blur_z_part)
    pairs[0, 0:16, :] = pair_rows(rest[0] + rest[1])
    for p in range(2):
        kpairs[p, 0:16, :] = pair_rows(reactions[2 * p] + reactions[2 * p + 1])
    f4[...] = exact_dot(compact(range(1), pairs, 8), halve)
    k4[...] = exact_dot(compact(range(2), kpairs, 8), halve).reshape(2, 8, LANES)


def pack_last(y_before, own, y_after, out):
    before, after = edges("agg")
    row = iota(own.shape, 0)
    lo = pltpu.roll(y_before[...], 6, 0) * before
    hi = pltpu.roll(y_after[...], 2, 0) * after
    out[...] = jnp.where(row < 2, lo, jnp.where(row < 4, own[...], jnp.where(row < 6, hi, 0.0)))


def last_kernel(own, x_before, x_after, k4, e4, rest):
    outside, inside = masks_of(8, 2, 4, 8)
    low = low_half(own.shape)
    inside = jnp.where(iota(own.shape, 0) < 6, inside, 0.0)
    outside = jnp.where(iota(own.shape, 0) < 6, outside, 0.0)
    middle = own[...] * inside
    fields = [
        jnp.where(low, x_before[...], x_after[...]) * outside,
        swap(jnp.where(low, x_after[...], x_before[...])) * outside,
        middle,
        swap(middle),
    ]
    value = corrections(4, fields, [k4[0], k4[1]], [outside, inside], blur_z_part)
    left = coarse_remainders(value + [swap(value[1])], [middle], [k4[1]], blur_z_part)[0]
    for out, here in ((e4, value[1]), (rest, left)):
        out[0] = here[2:4, 0:8]
        out[1] = swap(here)[2:4, 0:8]


def neighbours_of(up, down, axis):
    count = lax.axis_size(axis)
    ahead = [(i, (i + 1) % count) for i in range(count)]
    back = [(i, (i - 1) % count) for i in range(count)]
    return lax.ppermute(up, axis, ahead), lax.ppermute(down, axis, back)


VMEM = pl.BlockSpec(memory_space=pltpu.VMEM)
HBM = pl.BlockSpec(memory_space=pltpu.HBM)


def call(body, outs, ins, scratch=(), copies=0, flops=0, name=None):
    sems = [pltpu.SemaphoreType.DMA((copies,))] if copies else []
    return pl.pallas_call(
        body,
        out_shape=[jax.ShapeDtypeStruct(dims, F32) for dims in outs],
        in_specs=ins,
        out_specs=[VMEM] * len(outs),
        scratch_shapes=[s if not isinstance(s, tuple) else pltpu.VMEM(s, F32) for s in scratch] + sems,
        compiler_params=pltpu.CompilerParams(vmem_limit_bytes=40 * 1024 * 1024),
        cost_estimate=pl.CostEstimate(flops=flops, transcendentals=0, bytes_accessed=flops),
        name=name,
    )


def per_device(source, guess, reaction, flags):
    tile = (32, 8, LANES)
    own, down, strip_up, strip_down = call(
        pack_rows,
        [tile, tile, (7, 32, LANES), (7, 32, LANES)],
        [HBM] * 4,
        scratch=[pltpu.SMEM((1, 1, flags.shape[2]), jnp.int32)] + [tile] * 6,
        copies=13,
        name="pack_rows",
    )(flags, guess, source, reaction)
    y_before, y_after = neighbours_of(own, down, "agg")
    packed, down = call(
        pack_planes, [(8, 40, LANES)] * 2, [VMEM] * 5, name="pack_planes"
    )(own, y_before, y_after, strip_up, strip_down)
    x_before, x_after = neighbours_of(packed, down, "box")
    big = (32, 40, LANES)
    *fields, inner = call(
        fine_inner,
        [big] * 6 + [(16, 16, LANES)],
        [VMEM] * 3 + [HBM] * 3,
        scratch=[(12, 40, LANES), (16, 32, LANES)],
        copies=3,
        flops=8000000,
        name="fine_inner",
    )(packed, y_before, y_after, guess, source, reaction)
    coarse, edge = call(
        fine_outer,
        [(16, 16, LANES), (4, 32, LANES)],
        [VMEM] * 10,
        scratch=[(4, 40, LANES)],
        name="fine_outer",
    )(packed, x_before, x_after, *fields, inner)
    iterate = jnp.concatenate([edge[0:2], fields[5][2:30, 0:32], edge[2:4]], axis=0)
    y_before, y_after = neighbours_of(coarse, coarse, "agg")
    extended = jnp.concatenate([y_before, coarse, y_after], axis=1)
    x_before, x_after = neighbours_of(extended[16 - FAR :], extended[:FAR], "box")
    plane = (48, LANES)
    inner = call(
        coarse_inner,
        [(8,) + plane] * 3 + [(3, 24, LANES)] * 2,
        [VMEM] * 3,
        scratch=[(3,) + plane] * 2,
        flops=4000000,
        name="coarse_inner",
    )(y_before, coarse, y_after)
    e1, e2, e3, f4, k4 = call(
        coarse_outer,
        [(16, 16, 64), (8, 8, 32), (4, 4, 16), (8, LANES), (2, 8, LANES)],
        [VMEM] * 7,
        scratch=[(16,) + plane] * 2 + [(17,) + plane] + [(7,) + plane] * 2,
        name="coarse_outer",
    )(x_before, x_after, *inner)
    y_before, y_after = neighbours_of(f4, f4, "agg")
    (last,) = call(pack_last, [(8, LANES)], [VMEM] * 3, name="pack_last")(y_before, f4, y_after)
    x_before, x_after = neighbours_of(last, last, "box")
    e4, rest = call(
        last_kernel, [(2, 2, 8), (2, 2, 8)], [VMEM] * 4, name="last"
    )(last, x_before, x_after, k4)
    return iterate, e1, e2, e3, e4, rest


def solution(mesh):
    spec = P("box", "agg", None)
    return jax.shard_map(
        per_device, mesh=mesh, in_specs=(spec,) * 4, out_specs=(spec,) * 6, check_vma=False
    )
```

```python
import functools

import jax
import jax.numpy as jnp
from jax import lax
from jax.experimental import pallas as pl
from jax.experimental.pallas import tpu as pltpu
from jax.sharding import PartitionSpec as P

F32 = jnp.float32
LANES = 128
FAR = 14


def coefficients(level_index):
    upper_edge = 1.1 * (2.0 + 0.02 * 4.0**level_index)
    lower_edge = upper_edge / 8.0
    midpoint = (upper_edge + lower_edge) / 2.0
    half_span = (upper_edge - lower_edge) / 2.0
    sigma_value = midpoint / half_span
    rho_first = 1.0 / sigma_value
    rho_second = 1.0 / (2.0 * sigma_value - rho_first)
    return (midpoint, rho_second * rho_first, 2.0 * rho_second / half_span)


def iota(shape, dim):
    return lax.broadcasted_iota(jnp.int32, shape, dim)


def edges(axis):
    here = lax.axis_index(axis)
    before = jnp.where(here > 0, 1.0, 0.0).astype(F32)
    after = jnp.where(here < lax.axis_size(axis) - 1, 1.0, 0.0).astype(F32)
    return before, after


def blurred(planes, blur_z):
    sums = [a + b for a, b in zip(planes[:-1], planes[1:])]
    out = []
    for low, high in zip(sums[:-1], sums[1:]):
        total = low + high
        part = total + pltpu.roll(total, 1, 0)
        out.append(blur_z(part + pltpu.roll(part, part.shape[0] - 1, 0)))
    return out


def blur_z_full(values):
    lane = iota(values.shape, 1)
    part = values + jnp.where(lane == 0, 0.0, pltpu.roll(values, 1, 1))
    return part + jnp.where(lane == LANES - 1, values, pltpu.roll(part, LANES - 1, 1))


def blur_z_halves(values):
    lane = iota(values.shape, 1) & 63
    part = values + jnp.where(lane == 0, 0.0, pltpu.roll(values, 1, 1))
    return part + jnp.where(lane == 63, values, pltpu.roll(part, LANES - 1, 1))


def blur_z_part(values):
    part = values + pltpu.roll(values, 1, 1)
    return part + pltpu.roll(part, LANES - 1, 1)


def pair_rows(values):
    return values + pltpu.roll(values, values.shape[0] - 1, 0)


def pair_matrix(first):
    source = iota((2 * LANES, LANES), 0) & (LANES - 1)
    target = iota((2 * LANES, LANES), 1)
    return jnp.where((source >> 1) + first == target, 0.5, 0.0).astype(jnp.bfloat16)


def pair_matrix_halves():
    source = iota((2 * LANES, LANES), 0) & (LANES - 1)
    target = iota((2 * LANES, LANES), 1)
    hit = ((source & 64) == (target & 64)) & ((source & 63) >> 1 == (target & 63))
    return jnp.where(hit, 0.5, 0.0).astype(jnp.bfloat16)


def paired(values, matrix):
    coarse = values.astype(jnp.bfloat16)
    fine = (values - coarse.astype(F32)).astype(jnp.bfloat16)
    return jnp.dot(jnp.concatenate([coarse, fine], axis=1), matrix, preferred_element_type=F32)


def loop(first, stop, size, body):
    count = (stop - first) // size

    def step(i, carry):
        body(first + i * size)
        return carry

    lax.fori_loop(0, count, step, 0)


def copy_all(sems, *pairs):
    copies = [pltpu.make_async_copy(a, b, sems.at[i]) for i, (a, b) in enumerate(pairs)]
    for copy in copies:
        copy.start()
    return copies


def row_messages(source, guess, reaction, flags):
    depth = source.shape[2]
    boxes = flags.shape[2]
    flag = jnp.repeat(flags[0, 0].astype(F32), depth // boxes)
    flag = jnp.broadcast_to(flag, (source.shape[0], 1, depth))
    up = jnp.concatenate([flag, reaction[:, -2:], source[:, -2:], guess[:, -3:]], axis=1)
    down = jnp.concatenate([guess[:, :3], source[:, :2], reaction[:, :2], flag], axis=1)
    return up, down


def halo_tiles(from_before, from_after, before, after):
    row = iota(from_before.shape, 1)
    first = row < 4
    guess = jnp.where(first, from_after * after, from_before * before)
    source = jnp.where(first, pltpu.roll(from_after, 5, 1), pltpu.roll(from_before, 3, 1))
    reaction = jnp.where(first, pltpu.roll(from_after, 3, 1), pltpu.roll(from_before, 5, 1))
    return guess, source, reaction


def pack_planes(own, from_before, from_after, strip_up, strip_down, up, down):
    before, after = edges("agg")
    tile = (8, LANES)
    own_mask = jnp.broadcast_to(own[0, 0:1, :], (32, LANES))
    lo_mask = jnp.broadcast_to(from_before[0, 0:1, :] * before, tile)
    hi_mask = jnp.broadcast_to(from_after[0, 7:8, :] * after, tile)
    halo_mask = jnp.where(iota(tile, 0) < 4, hi_mask, lo_mask)
    planes = from_before.shape[0]
    for target, strip, first, local in (
        (up, strip_up, planes - 4, (1, 2, 2)),
        (down, strip_down, 0, (0, 0, 0)),
    ):
        tiles = halo_tiles(from_before[first : first + 4], from_after[first : first + 4], before, after)
        target[0:7, 0:32, :] = strip[...]
        at = 0
        for tile, start, count in zip(tiles, local, (3, 2, 2)):
            target[at : at + count, 32:40, :] = tile[start : start + count]
            at += count
        target[7, 0:32, :] = own_mask
        target[7, 32:40, :] = halo_mask


SHIFT = 8.0 / 7.0


def compact(values, ref, rows):
    return jnp.concatenate([ref[i, pl.ds(0, rows, stride=2), :] for i in values], axis=0)


def fine_inner(
    packed, from_before, from_after, guess, source, reaction,
    g, s, k, d, u, w, coarse, pairs, kpairs, sems,
):
    rows = pl.ds(0, 32)
    copies = copy_all(
        sems, (guess, g.at[:, rows, :]), (source, s.at[:, rows, :]), (reaction, k.at[:, rows, :])
    )
    before, after = edges("agg")
    theta, c1, c2 = coefficients(0)

    def assemble(x):
        at = pl.ds(x, 8)
        tiles = halo_tiles(from_before[at], from_after[at], before, after)
        g[at, 32:40, :] = tiles[0]
        s[at, 32:40, :] = tiles[1]
        k[at, 32:40, :] = tiles[2]

    loop(0, 32, 8, assemble)
    for copy in copies:
        copy.wait()

    def remainders(field, x, size):
        planes = [field[x + i] for i in range(-1, size + 1)]
        mask = packed[7]
        out = []
        for i, q in enumerate(blurred(planes, blur_z_full)):
            r = mask * (s[x + i] - (k[x + i] + SHIFT) * planes[i + 1] + q * (1.0 / 56.0))
            out.append((r, planes[i + 1]))
        return out

    def first(x):
        out = remainders(g, x, 3)
        for i, (r, middle) in enumerate(out):
            step = r * (1.0 / theta)
            d[x + i] = step
            u[x + i] = middle + step

    loop(1, 31, 3, first)

    def second(x):
        out = [m + (c1 * d[x + i] + c2 * r) for i, (r, m) in enumerate(remainders(u, x, 4))]
        for i, value in enumerate(out):
            w[x + i] = value

    loop(2, 30, 4, second)

    def third(x):
        out = [r for r, _ in remainders(w, x, 4)]
        at = (x - 4) // 2
        pairs[at] = pair_rows(out[0] + out[1])
        pairs[at + 1] = pair_rows(out[2] + out[3])

    loop(4, 28, 4, third)

    def fourth(i):
        out = [pair_rows(k[2 * i + 2 * j, 0:32, :] + k[2 * i + 2 * j + 1, 0:32, :]) for j in range(4)]
        for j, value in enumerate(out):
            kpairs[i + j] = value

    loop(0, 16, 4, fourth)
    rk = paired(compact(range(16), kpairs, 16), pair_matrix(64)).reshape(16, 16, LANES)
    rf = paired(compact(range(12), pairs, 16), pair_matrix(0)).reshape(12, 16, LANES)
    coarse[0:2] = rk[0:2]
    coarse[2:14] = rk[2:14] + rf
    coarse[14:16] = rk[14:16]


def fine_outer(packed, x_before, x_after, g, s, k, d, u, w, inner, coarse, edge, pairs):
    xbefore, xafter = edges("box")
    theta, c1, c2 = coefficients(0)
    new_d, new_u, new_w = {}, {}, {}

    def side(x, before, after, own):
        return before(x + 3) if x < 0 else after(x - 32) if x > 31 else own(x)

    def guess_at(x):
        return side(x, lambda i: x_before[i] * xbefore, lambda i: x_after[i] * xafter, lambda i: g[i])

    def source_at(x):
        return side(x, lambda i: x_before[i + 2], lambda i: x_after[i + 3], lambda i: s[i])

    def reaction_at(x):
        return side(x, lambda i: x_before[i + 4], lambda i: x_after[i + 5], lambda i: k[i])

    def mask_at(x):
        return side(x, lambda i: x_before[7] * xbefore, lambda i: x_after[7] * xafter, lambda i: packed[7])

    def remainders(field, first, size):
        planes = [field(x) for x in range(first - 1, first + size + 1)]
        out = []
        for i, q in enumerate(blurred(planes, blur_z_full)):
            x = first + i
            r = mask_at(x) * (source_at(x) - (reaction_at(x) + SHIFT) * planes[i + 1] + q * (1.0 / 56.0))
            out.append((x, r, planes[i + 1]))
        return out

    for first in (-2, 31):
        for x, r, middle in remainders(guess_at, first, 3):
            new_d[x] = r * (1.0 / theta)
            new_u[x] = middle + new_d[x]
    for first in (-1, 30):
        for x, r, middle in remainders(lambda i: new_u[i] if i in new_u else u[i], first, 3):
            step = new_d[x] if x in new_d else d[x]
            new_w[x] = middle + (c1 * step + c2 * r)
    for at, x in enumerate((0, 1, 30, 31)):
        edge[at] = new_w[x][0:32]
    for at, first in enumerate((0, 28)):
        out = [r for _, r, _ in remainders(lambda i: new_w[i] if i in new_w else w[i], first, 4)]
        pairs[2 * at] = pair_rows(out[0] + out[1])
        pairs[2 * at + 1] = pair_rows(out[2] + out[3])
    rf = paired(compact(range(4), pairs, 16), pair_matrix(0)).reshape(4, 16, LANES)
    coarse[0:2] = inner[0:2] + rf[0:2]
    coarse[2:14] = inner[2:14]
    coarse[14:16] = inner[14:16] + rf[2:4]


def level_constants(level):
    theta, c1, c2 = coefficients(level)
    return (1.0 + c1) / theta + c2, c2 / theta


def low_half(shape):
    return iota(shape, len(shape) - 1) < 64


def masks_of(rows, lo, hi, lanes):
    before, after = edges("agg")
    xbefore, xafter = edges("box")
    shape = (rows, LANES)
    row = iota(shape, 0)
    inside = jnp.where(row < lo, before, jnp.where(row >= hi, after, 1.0))
    inside = jnp.where((iota(shape, 1) & 63) < lanes, inside, 0.0)
    return inside * jnp.where(low_half(shape), xbefore, xafter), inside


def corrections(level, planes, reactions, masks, blur_z):
    alpha, beta = level_constants(level)
    return [
        m * (f * (alpha - beta * (k + SHIFT)) + q * (beta / 56.0))
        for f, k, m, q in zip(planes[1:-1], reactions, masks, blurred(planes, blur_z))
    ]


def coarse_remainders(planes, fields, reactions, blur_z):
    return [
        f - (k + SHIFT) * e + q * (1.0 / 56.0)
        for f, k, e, q in zip(fields, reactions, planes[1:-1], blurred(planes, blur_z))
    ]


def swap(values):
    return pltpu.roll(values, 64, 1)


def coarse_inner(y_before, own, y_after, f, k, e, f2, k2, pairs, kpairs):
    _, inside = masks_of(48, 16, 32, 64)
    low = low_half((48, LANES))
    for j in range(8):
        lo = jnp.concatenate([y_before[j], own[j], y_after[j]], axis=0)
        hi = jnp.concatenate([y_before[15 - j], own[15 - j], y_after[15 - j]], axis=0)
        f[j] = jnp.where(low, lo, swap(hi)) * inside
        k[j] = jnp.where(low, swap(lo), hi)
    fields = [f[j] for j in range(8)]
    reactions = [k[j] for j in range(8)]
    value = corrections(1, fields + [swap(fields[7])], reactions[1:], [inside] * 7, blur_z_halves)
    for j in range(7):
        e[j + 1] = value[j]
    rest = coarse_remainders(value + [swap(value[6])], fields[2:], reactions[2:], blur_z_halves)
    for j in range(3):
        pairs[j] = pair_rows(rest[2 * j] + rest[2 * j + 1])
        kpairs[j] = pair_rows(reactions[2 * j + 2] + reactions[2 * j + 3])
    halve = pair_matrix_halves()
    _, inside = masks_of(24, 8, 16, 32)
    both = jnp.concatenate([compact(range(3), pairs, 24), compact(range(3), kpairs, 24)], axis=0)
    both = paired(both, halve).reshape(6, 24, LANES)
    for j in range(3):
        f2[j] = both[j] * inside
    k2[...] = both[3:6]


def coarse_outer(
    x_before, x_after, f_in, k_in, e_in, f2_in, k2_in, e1, e2, e3, f4, k4,
    f, k, e, pairs, kpairs,
):
    outside, inside = masks_of(48, 16, 32, 64)
    low = low_half((48, LANES))

    def take(j):
        out = []
        for i in range(2):
            lo, hi = x_before[j + i], x_after[13 - j - i]
            out.append((jnp.where(low, lo, swap(hi)) * outside, jnp.where(low, swap(lo), hi)))
        for i in range(2):
            f[j + i], k[j + i] = out[i]

    loop(0, 14, 2, take)
    for j in (0, 1):
        f[14 + j] = f_in[j]
        k[14 + j] = k_in[j]

    def one(j):
        out = corrections(
            1,
            [f[j + i] for i in range(-1, 4)],
            [k[j + i] for i in range(3)],
            [outside] * 3,
            blur_z_halves,
        )
        for i in range(3):
            e[j + i] = out[i]

    loop(1, 13, 3, one)
    value = corrections(1, [f[j] for j in range(12, 16)], [k[13], k[14]], [outside, inside], blur_z_halves)
    e[13], e[14] = value
    e[15] = e_in[1]
    e[16] = e_in[2]

    def two(j):
        out = coarse_remainders(
            [e[j + i] for i in range(-1, 3)],
            [f[j + i] for i in range(2)],
            [k[j + i] for i in range(2)],
            blur_z_halves,
        )
        p = (j - 2) // 2
        pairs[p] = pair_rows(out[0] + out[1])
        kpairs[p] = pair_rows(k[j] + k[j + 1])

    loop(2, 16, 2, two)
    half = slice(16, 32)
    halve = pair_matrix_halves()

    def both(fields, reactions, rows):
        values = [compact(range(fields), pairs, rows), compact(range(reactions), kpairs, rows)]
        out = paired(jnp.concatenate(values, axis=0), halve).reshape(fields + reactions, rows, LANES)
        return out[:fields], out[fields:]

    e1[0] = e[14, half, 0:64]
    e1[15] = swap(e[14, half, :])[:, 0:64]
    for j in range(1, 8):
        value = e_in[j, half, :]
        e1[j] = value[:, 0:64]
        e1[15 - j] = swap(value)[:, 0:64]
    rf, rk = both(7, 7, 24)
    outside, inside = masks_of(24, 8, 16, 32)
    fields = [rf[j] * (outside if j < 6 else inside) for j in range(7)] + [f2_in[j] for j in range(3)]
    reactions = [rk[j] for j in range(7)] + [k2_in[j] for j in range(3)]
    value = corrections(
        2, fields + [swap(fields[9])], reactions[1:], [outside] * 5 + [inside] * 4, blur_z_part
    )
    for j in range(4):
        own = value[5 + j][8:16]
        e2[j] = own[:, 0:32]
        e2[7 - j] = swap(own)[:, 0:32]
    rest = coarse_remainders(value + [swap(value[8])], fields[2:], reactions[2:], blur_z_part)
    for p in range(4):
        pairs[p, 0:24, :] = pair_rows(rest[2 * p] + rest[2 * p + 1])
        kpairs[p, 0:24, :] = pair_rows(reactions[2 * p + 2] + reactions[2 * p + 3])
    rf, rk = both(4, 4, 16)
    outside, inside = masks_of(16, 4, 8, 16)
    fields = [rf[0] * outside, rf[1] * outside, rf[2] * inside, rf[3] * inside]
    reactions = [rk[j] for j in range(4)]
    value = corrections(3, fields + [swap(fields[3])], reactions[1:], [outside, inside, inside], blur_z_part)
    for j in range(2):
        own = value[1 + j][0:8]
        e3[j] = own[4:8, 0:16]
        e3[3 - j] = swap(own)[4:8, 0:16]
    rest = coarse_remainders(value + [swap(value[2])], fields[2:], reactions[2:], blur_z_part)
    pairs[0, 0:16, :] = pair_rows(rest[0] + rest[1])
    for p in range(2):
        kpairs[p, 0:16, :] = pair_rows(reactions[2 * p] + reactions[2 * p + 1])
    rf, rk = both(1, 2, 8)
    f4[...] = rf[0]
    k4[...] = rk


def pack_last(y_before, own, y_after, out):
    before, after = edges("agg")
    row = iota(own.shape, 0)
    lo = pltpu.roll(y_before[...], 6, 0) * before
    hi = pltpu.roll(y_after[...], 2, 0) * after
    out[...] = jnp.where(row < 2, lo, jnp.where(row < 4, own[...], jnp.where(row < 6, hi, 0.0)))


def last_kernel(own, x_before, x_after, k4, e4, rest):
    outside, inside = masks_of(8, 2, 4, 8)
    low = low_half(own.shape)
    inside = jnp.where(iota(own.shape, 0) < 6, inside, 0.0)
    outside = jnp.where(iota(own.shape, 0) < 6, outside, 0.0)
    middle = own[...] * inside
    fields = [
        jnp.where(low, x_before[...], x_after[...]) * outside,
        swap(jnp.where(low, x_after[...], x_before[...])) * outside,
        middle,
        swap(middle),
    ]
    value = corrections(4, fields, [k4[0], k4[1]], [outside, inside], blur_z_part)
    left = coarse_remainders(value + [swap(value[1])], [middle], [k4[1]], blur_z_part)[0]
    for out, here in ((e4, value[1]), (rest, left)):
        out[0] = here[2:4, 0:8]
        out[1] = swap(here)[2:4, 0:8]


def neighbours_of(up, down, axis):
    count = lax.axis_size(axis)
    ahead = [(i, (i + 1) % count) for i in range(count)]
    back = [(i, (i - 1) % count) for i in range(count)]
    return lax.ppermute(up, axis, ahead), lax.ppermute(down, axis, back)


VMEM = pl.BlockSpec(memory_space=pltpu.VMEM)
HBM = pl.BlockSpec(memory_space=pltpu.HBM)


def call(body, outs, ins, scratch=(), copies=0, flops=0, name=None):
    sems = [pltpu.SemaphoreType.DMA((copies,))] if copies else []
    return pl.pallas_call(
        body,
        out_shape=[jax.ShapeDtypeStruct(dims, F32) for dims in outs],
        in_specs=ins,
        out_specs=[VMEM] * len(outs),
        scratch_shapes=[s if not isinstance(s, tuple) else pltpu.VMEM(s, F32) for s in scratch] + sems,
        compiler_params=pltpu.CompilerParams(vmem_limit_bytes=40 * 1024 * 1024),
        cost_estimate=pl.CostEstimate(flops=flops, transcendentals=0, bytes_accessed=flops),
        name=name,
    )


def per_device(source, guess, reaction, flags):
    own, down = row_messages(source, guess, reaction, flags)
    y_before, y_after = neighbours_of(own, down, "agg")
    strip_up = jnp.concatenate([guess[-3:], source[-2:], reaction[-2:]], axis=0)
    strip_down = jnp.concatenate([guess[:3], source[:2], reaction[:2]], axis=0)
    packed, down = call(
        pack_planes, [(8, 40, LANES)] * 2, [VMEM] * 5, name="pack_planes"
    )(own, y_before, y_after, strip_up, strip_down)
    x_before, x_after = neighbours_of(packed, down, "box")
    big = (32, 40, LANES)
    *fields, inner = call(
        fine_inner,
        [big] * 6 + [(16, 16, LANES)],
        [VMEM] * 3 + [HBM] * 3,
        scratch=[(12, 40, LANES), (16, 32, LANES)],
        copies=3,
        flops=8000000,
        name="fine_inner",
    )(packed, y_before, y_after, guess, source, reaction)
    coarse, edge = call(
        fine_outer,
        [(16, 16, LANES), (4, 32, LANES)],
        [VMEM] * 10,
        scratch=[(4, 40, LANES)],
        name="fine_outer",
    )(packed, x_before, x_after, *fields, inner)
    iterate = jnp.concatenate([edge[0:2], fields[5][2:30, 0:32], edge[2:4]], axis=0)
    y_before, y_after = neighbours_of(coarse, coarse, "agg")
    extended = jnp.concatenate([y_before, coarse, y_after], axis=1)
    x_before, x_after = neighbours_of(extended[16 - FAR :], extended[:FAR], "box")
    plane = (48, LANES)
    inner = call(
        coarse_inner,
        [(8,) + plane] * 3 + [(3, 24, LANES)] * 2,
        [VMEM] * 3,
        scratch=[(3,) + plane] * 2,
        flops=4000000,
        name="coarse_inner",
    )(y_before, coarse, y_after)
    e1, e2, e3, f4, k4 = call(
        coarse_outer,
        [(16, 16, 64), (8, 8, 32), (4, 4, 16), (8, LANES), (2, 8, LANES)],
        [VMEM] * 7,
        scratch=[(16,) + plane] * 2 + [(17,) + plane] + [(7,) + plane] * 2,
        name="coarse_outer",
    )(x_before, x_after, *inner)
    y_before, y_after = neighbours_of(f4, f4, "agg")
    (last,) = call(pack_last, [(8, LANES)], [VMEM] * 3, name="pack_last")(y_before, f4, y_after)
    x_before, x_after = neighbours_of(last, last, "box")
    e4, rest = call(
        last_kernel, [(2, 2, 8), (2, 2, 8)], [VMEM] * 4, name="last"
    )(last, x_before, x_after, k4)
    return iterate, e1, e2, e3, e4, rest


def solution(mesh):
    spec = P("box", "agg", None)
    return jax.shard_map(
        per_device, mesh=mesh, in_specs=(spec,) * 4, out_specs=(spec,) * 6, check_vma=False
    )
```

```python
import functools

import jax
import jax.numpy as jnp
from jax import lax
from jax.experimental import pallas as pl
from jax.experimental.pallas import tpu as pltpu
from jax.sharding import PartitionSpec as P

F32 = jnp.float32
LANES = 128
FAR = 14


def coefficients(level_index):
    upper_edge = 1.1 * (2.0 + 0.02 * 4.0**level_index)
    lower_edge = upper_edge / 8.0
    midpoint = (upper_edge + lower_edge) / 2.0
    half_span = (upper_edge - lower_edge) / 2.0
    sigma_value = midpoint / half_span
    rho_first = 1.0 / sigma_value
    rho_second = 1.0 / (2.0 * sigma_value - rho_first)
    return (midpoint, rho_second * rho_first, 2.0 * rho_second / half_span)


def iota(shape, dim):
    return lax.broadcasted_iota(jnp.int32, shape, dim)


def edges(axis):
    here = lax.axis_index(axis)
    before = jnp.where(here > 0, 1.0, 0.0).astype(F32)
    after = jnp.where(here < lax.axis_size(axis) - 1, 1.0, 0.0).astype(F32)
    return before, after


def blurred(planes, blur_z):
    sums = [a + b for a, b in zip(planes[:-1], planes[1:])]
    out = []
    for low, high in zip(sums[:-1], sums[1:]):
        total = low + high
        part = total + pltpu.roll(total, 1, 0)
        out.append(blur_z(part + pltpu.roll(part, part.shape[0] - 1, 0)))
    return out


def blur_z_full(values):
    lane = iota(values.shape, 1)
    part = values + jnp.where(lane == 0, 0.0, pltpu.roll(values, 1, 1))
    return part + jnp.where(lane == LANES - 1, values, pltpu.roll(part, LANES - 1, 1))


def blur_z_halves(values):
    lane = iota(values.shape, 1) & 63
    part = values + jnp.where(lane == 0, 0.0, pltpu.roll(values, 1, 1))
    return part + jnp.where(lane == 63, values, pltpu.roll(part, LANES - 1, 1))


def blur_z_part(values):
    part = values + pltpu.roll(values, 1, 1)
    return part + pltpu.roll(part, LANES - 1, 1)


def pair_rows(values):
    return values + pltpu.roll(values, values.shape[0] - 1, 0)


def pair_matrix(first):
    source = iota((2 * LANES, LANES), 0) & (LANES - 1)
    target = iota((2 * LANES, LANES), 1)
    return jnp.where((source >> 1) + first == target, 0.5, 0.0).astype(jnp.bfloat16)


def pair_matrix_halves():
    source = iota((2 * LANES, LANES), 0) & (LANES - 1)
    target = iota((2 * LANES, LANES), 1)
    hit = ((source & 64) == (target & 64)) & ((source & 63) >> 1 == (target & 63))
    return jnp.where(hit, 0.5, 0.0).astype(jnp.bfloat16)


def paired(values, matrix):
    coarse = values.astype(jnp.bfloat16)
    fine = (values - coarse.astype(F32)).astype(jnp.bfloat16)
    return jnp.dot(jnp.concatenate([coarse, fine], axis=1), matrix, preferred_element_type=F32)


def loop(first, stop, size, body):
    count = (stop - first) // size
    if count == 1:
        body(first)
        return

    def step(i, carry):
        body(first + i * size)
        return carry

    lax.fori_loop(0, count, step, 0)


def copy_all(sems, *pairs):
    copies = [pltpu.make_async_copy(a, b, sems.at[i]) for i, (a, b) in enumerate(pairs)]
    for copy in copies:
        copy.start()
    return copies


def pack_rows(
    flags, guess, source, reaction, up, down, strip_up, strip_down,
    flag_smem, guess_lo, guess_hi, source_lo, source_hi, reaction_lo, reaction_hi, sems,
):
    lo, hi = pl.ds(0, 8), pl.ds(24, 8)
    copies = copy_all(
        sems,
        (flags, flag_smem),
        (guess.at[:, lo, :], guess_lo),
        (guess.at[:, hi, :], guess_hi),
        (source.at[:, lo, :], source_lo),
        (source.at[:, hi, :], source_hi),
        (reaction.at[:, lo, :], reaction_lo),
        (reaction.at[:, hi, :], reaction_hi),
        (guess.at[29:32], strip_up.at[0:3]),
        (source.at[30:32], strip_up.at[3:5]),
        (reaction.at[30:32], strip_up.at[5:7]),
        (guess.at[0:3], strip_down.at[0:3]),
        (source.at[0:2], strip_down.at[3:5]),
        (reaction.at[0:2], strip_down.at[5:7]),
    )
    for copy in copies[:7]:
        copy.wait()
    boxes = flags.shape[2]
    lane = iota((8, LANES), 1)
    flag = jnp.zeros((8, LANES), F32)
    for i in range(boxes):
        flag = jnp.where(lane // (LANES // boxes) == i, flag_smem[0, 0, i].astype(F32), flag)
    flag = flag[None]
    row = iota(up.shape, 1)
    up[...] = jnp.where(
        row >= 5,
        guess_hi[...],
        jnp.where(
            row >= 3,
            pltpu.roll(source_hi[...], 5, 1),
            jnp.where(row >= 1, pltpu.roll(reaction_hi[...], 3, 1), flag),
        ),
    )
    down[...] = jnp.where(
        row < 3,
        guess_lo[...],
        jnp.where(
            row < 5,
            pltpu.roll(source_lo[...], 3, 1),
            jnp.where(row < 7, pltpu.roll(reaction_lo[...], 5, 1), flag),
        ),
    )
    for copy in copies[7:]:
        copy.wait()


def halo_tiles(from_before, from_after, before, after):
    row = iota(from_before.shape, 1)
    first = row < 4
    guess = jnp.where(first, from_after * after, from_before * before)
    source = jnp.where(first, pltpu.roll(from_after, 5, 1), pltpu.roll(from_before, 3, 1))
    reaction = jnp.where(first, pltpu.roll(from_after, 3, 1), pltpu.roll(from_before, 5, 1))
    return guess, source, reaction


def pack_planes(own, from_before, from_after, strip_up, strip_down, up, down):
    before, after = edges("agg")
    tile = (8, LANES)
    own_mask = jnp.broadcast_to(own[0, 0:1, :], (32, LANES))
    lo_mask = jnp.broadcast_to(from_before[0, 0:1, :] * before, tile)
    hi_mask = jnp.broadcast_to(from_after[0, 7:8, :] * after, tile)
    halo_mask = jnp.where(iota(tile, 0) < 4, hi_mask, lo_mask)
    planes = from_before.shape[0]
    for target, strip, first, local in (
        (up, strip_up, planes - 4, (1, 2, 2)),
        (down, strip_down, 0, (0, 0, 0)),
    ):
        tiles = halo_tiles(from_before[first : first + 4], from_after[first : first + 4], before, after)
        target[0:7, 0:32, :] = strip[...]
        at = 0
        for tile, start, count in zip(tiles, local, (3, 2, 2)):
            target[at : at + count, 32:40, :] = tile[start : start + count]
            at += count
        target[7, 0:32, :] = own_mask
        target[7, 32:40, :] = halo_mask


SHIFT = 8.0 / 7.0


def compact(values, ref, rows):
    return jnp.concatenate([ref[i, pl.ds(0, rows, stride=2), :] for i in values], axis=0)


def fine_inner(
    packed, from_before, from_after, guess, source, reaction,
    g, s, k, d, u, w, coarse, pairs, kpairs, sems,
):
    rows = pl.ds(0, 32)
    copies = copy_all(
        sems, (guess, g.at[:, rows, :]), (source, s.at[:, rows, :]), (reaction, k.at[:, rows, :])
    )
    before, after = edges("agg")
    theta, c1, c2 = coefficients(0)

    def assemble(x):
        at = pl.ds(x, 32)
        tiles = halo_tiles(from_before[at], from_after[at], before, after)
        g[at, 32:40, :] = tiles[0]
        s[at, 32:40, :] = tiles[1]
        k[at, 32:40, :] = tiles[2]

    loop(0, 32, 32, assemble)
    for copy in copies:
        copy.wait()

    def remainders(field, x, size):
        planes = [field[x + i] for i in range(-1, size + 1)]
        mask = packed[7]
        out = []
        for i, q in enumerate(blurred(planes, blur_z_full)):
            r = mask * (s[x + i] - (k[x + i] + SHIFT) * planes[i + 1] + q * (1.0 / 56.0))
            out.append((r, planes[i + 1]))
        return out

    def first(x):
        out = remainders(g, x, 10)
        for i, (r, middle) in enumerate(out):
            step = r * (1.0 / theta)
            d[x + i] = step
            u[x + i] = middle + step

    loop(1, 31, 10, first)

    def second(x):
        out = [m + (c1 * d[x + i] + c2 * r) for i, (r, m) in enumerate(remainders(u, x, 14))]
        for i, value in enumerate(out):
            w[x + i] = value

    loop(2, 30, 14, second)

    def third(x):
        out = [r for r, _ in remainders(w, x, 24)]
        at = (x - 4) // 2
        for i in range(len(out) // 2):
            pairs[at + i] = pair_rows(out[2 * i] + out[2 * i + 1])

    loop(4, 28, 24, third)

    def fourth(i):
        out = [pair_rows(k[2 * i + 2 * j, 0:32, :] + k[2 * i + 2 * j + 1, 0:32, :]) for j in range(16)]
        for j, value in enumerate(out):
            kpairs[i + j] = value

    loop(0, 16, 16, fourth)
    rk = paired(compact(range(16), kpairs, 16), pair_matrix(64)).reshape(16, 16, LANES)
    rf = paired(compact(range(12), pairs, 16), pair_matrix(0)).reshape(12, 16, LANES)
    coarse[0:2] = rk[0:2]
    coarse[2:14] = rk[2:14] + rf
    coarse[14:16] = rk[14:16]


def fine_outer(packed, x_before, x_after, g, s, k, d, u, w, inner, coarse, edge, pairs):
    xbefore, xafter = edges("box")
    theta, c1, c2 = coefficients(0)
    new_d, new_u, new_w = {}, {}, {}

    def side(x, before, after, own):
        return before(x + 3) if x < 0 else after(x - 32) if x > 31 else own(x)

    def guess_at(x):
        return side(x, lambda i: x_before[i] * xbefore, lambda i: x_after[i] * xafter, lambda i: g[i])

    def source_at(x):
        return side(x, lambda i: x_before[i + 2], lambda i: x_after[i + 3], lambda i: s[i])

    def reaction_at(x):
        return side(x, lambda i: x_before[i + 4], lambda i: x_after[i + 5], lambda i: k[i])

    def mask_at(x):
        return side(x, lambda i: x_before[7] * xbefore, lambda i: x_after[7] * xafter, lambda i: packed[7])

    def remainders(field, first, size):
        planes = [field(x) for x in range(first - 1, first + size + 1)]
        out = []
        for i, q in enumerate(blurred(planes, blur_z_full)):
            x = first + i
            r = mask_at(x) * (source_at(x) - (reaction_at(x) + SHIFT) * planes[i + 1] + q * (1.0 / 56.0))
            out.append((x, r, planes[i + 1]))
        return out

    for first in (-2, 31):
        for x, r, middle in remainders(guess_at, first, 3):
            new_d[x] = r * (1.0 / theta)
            new_u[x] = middle + new_d[x]
    for first in (-1, 30):
        for x, r, middle in remainders(lambda i: new_u[i] if i in new_u else u[i], first, 3):
            step = new_d[x] if x in new_d else d[x]
            new_w[x] = middle + (c1 * step + c2 * r)
    for at, x in enumerate((0, 1, 30, 31)):
        edge[at] = new_w[x][0:32]
    for at, first in enumerate((0, 28)):
        out = [r for _, r, _ in remainders(lambda i: new_w[i] if i in new_w else w[i], first, 4)]
        pairs[2 * at] = pair_rows(out[0] + out[1])
        pairs[2 * at + 1] = pair_rows(out[2] + out[3])
    rf = paired(compact(range(4), pairs, 16), pair_matrix(0)).reshape(4, 16, LANES)
    coarse[0:2] = inner[0:2] + rf[0:2]
    coarse[2:14] = inner[2:14]
    coarse[14:16] = inner[14:16] + rf[2:4]


def level_constants(level):
    theta, c1, c2 = coefficients(level)
    return (1.0 + c1) / theta + c2, c2 / theta


def low_half(shape):
    return iota(shape, len(shape) - 1) < 64


def masks_of(rows, lo, hi, lanes):
    before, after = edges("agg")
    xbefore, xafter = edges("box")
    shape = (rows, LANES)
    row = iota(shape, 0)
    inside = jnp.where(row < lo, before, jnp.where(row >= hi, after, 1.0))
    inside = jnp.where((iota(shape, 1) & 63) < lanes, inside, 0.0)
    return inside * jnp.where(low_half(shape), xbefore, xafter), inside


def corrections(level, planes, reactions, masks, blur_z):
    alpha, beta = level_constants(level)
    return [
        m * (f * (alpha - beta * (k + SHIFT)) + q * (beta / 56.0))
        for f, k, m, q in zip(planes[1:-1], reactions, masks, blurred(planes, blur_z))
    ]


def coarse_remainders(planes, fields, reactions, blur_z):
    return [
        f - (k + SHIFT) * e + q * (1.0 / 56.0)
        for f, k, e, q in zip(fields, reactions, planes[1:-1], blurred(planes, blur_z))
    ]


def swap(values):
    return pltpu.roll(values, 64, 1)


def coarse_inner(y_before, own, y_after, f, k, e, f2, k2, pairs, kpairs):
    _, inside = masks_of(48, 16, 32, 64)
    low = low_half((48, LANES))
    for j in range(8):
        lo = jnp.concatenate([y_before[j], own[j], y_after[j]], axis=0)
        hi = jnp.concatenate([y_before[15 - j], own[15 - j], y_after[15 - j]], axis=0)
        f[j] = jnp.where(low, lo, swap(hi)) * inside
        k[j] = jnp.where(low, swap(lo), hi)
    fields = [f[j] for j in range(8)]
    reactions = [k[j] for j in range(8)]
    value = corrections(1, fields + [swap(fields[7])], reactions[1:], [inside] * 7, blur_z_halves)
    for j in range(7):
        e[j + 1] = value[j]
    rest = coarse_remainders(value + [swap(value[6])], fields[2:], reactions[2:], blur_z_halves)
    for j in range(3):
        pairs[j] = pair_rows(rest[2 * j] + rest[2 * j + 1])
        kpairs[j] = pair_rows(reactions[2 * j + 2] + reactions[2 * j + 3])
    halve = pair_matrix_halves()
    _, inside = masks_of(24, 8, 16, 32)
    both = jnp.concatenate([compact(range(3), pairs, 24), compact(range(3), kpairs, 24)], axis=0)
    both = paired(both, halve).reshape(6, 24, LANES)
    for j in range(3):
        f2[j] = both[j] * inside
    k2[...] = both[3:6]


def coarse_outer(
    x_before, x_after, f_in, k_in, e_in, f2_in, k2_in, own1, own2, own3, f4, k4,
    pairs, kpairs,
):
    outside, inside = masks_of(48, 16, 32, 64)
    low = low_half((48, LANES))
    halve = pair_matrix_halves()

    def both(fields, reactions, rows):
        values = [compact(range(fields), pairs, rows), compact(range(reactions), kpairs, rows)]
        out = paired(jnp.concatenate(values, axis=0), halve).reshape(fields + reactions, rows, LANES)
        return [out[i] for i in range(fields)], [out[fields + i] for i in range(reactions)]

    fields, reactions = [], []
    for j in range(FAR):
        lo, hi = x_before[j], x_after[FAR - 1 - j]
        fields.append(jnp.where(low, lo, swap(hi)) * outside)
        reactions.append(jnp.where(low, swap(lo), hi))
    for j in range(2):
        fields.append(f_in[j])
        reactions.append(k_in[j])
    for j in range(7):
        kpairs[j] = pair_rows(reactions[2 * j + 2] + reactions[2 * j + 3])
    value = corrections(1, fields, reactions[1:15], [outside] * 13 + [inside], blur_z_halves)
    own1[0] = value[13][16:32]
    for j in range(1, 8):
        own1[j] = e_in[j, 16:32, :]
    rest = coarse_remainders(value + [e_in[1], e_in[2]], fields[2:], reactions[2:], blur_z_halves)
    for j in range(7):
        pairs[j] = pair_rows(rest[2 * j] + rest[2 * j + 1])
    rf, rk = both(7, 7, 24)
    outside, inside = masks_of(24, 8, 16, 32)
    fields = [rf[j] * (outside if j < 6 else inside) for j in range(7)] + [f2_in[j] for j in range(3)]
    reactions = rk + [k2_in[j] for j in range(3)]
    for p in range(4):
        kpairs[p, 0:24, :] = pair_rows(reactions[2 * p + 2] + reactions[2 * p + 3])
    value = corrections(
        2, fields + [swap(fields[9])], reactions[1:], [outside] * 5 + [inside] * 4, blur_z_part
    )
    for j in range(4):
        own2[j] = value[5 + j][8:16]
    rest = coarse_remainders(value + [swap(value[8])], fields[2:], reactions[2:], blur_z_part)
    for p in range(4):
        pairs[p, 0:24, :] = pair_rows(rest[2 * p] + rest[2 * p + 1])
    rf, rk = both(4, 4, 16)
    outside, inside = masks_of(16, 4, 8, 16)
    fields = [rf[0] * outside, rf[1] * outside, rf[2] * inside, rf[3] * inside]
    for p in range(2):
        kpairs[p, 0:16, :] = pair_rows(rk[2 * p] + rk[2 * p + 1])
    value = corrections(3, fields + [swap(fields[3])], rk[1:], [outside, inside, inside], blur_z_part)
    for j in range(2):
        own3[j] = value[1 + j][0:8]
    rest = coarse_remainders(value + [swap(value[2])], fields[2:], rk[2:], blur_z_part)
    pairs[0, 0:16, :] = pair_rows(rest[0] + rest[1])
    rf, rk = both(1, 2, 8)
    f4[...] = rf[0]
    k4[0] = rk[0]
    k4[1] = rk[1]


def unfold(own1, own2, own3, e1, e2, e3):
    for own, out, rows in ((own1, e1, slice(0, 16)), (own2, e2, slice(0, 8)), (own3, e3, slice(4, 8))):
        planes, _, lanes = out.shape
        for j in range(planes // 2):
            value = own[j]
            out[j] = value[rows, 0:lanes]
            out[planes - 1 - j] = swap(value)[rows, 0:lanes]


def pack_last(y_before, own, y_after, out):
    before, after = edges("agg")
    row = iota(own.shape, 0)
    lo = pltpu.roll(y_before[...], 6, 0) * before
    hi = pltpu.roll(y_after[...], 2, 0) * after
    out[...] = jnp.where(row < 2, lo, jnp.where(row < 4, own[...], jnp.where(row < 6, hi, 0.0)))


def last_kernel(own, x_before, x_after, k4, e4, rest):
    outside, inside = masks_of(8, 2, 4, 8)
    low = low_half(own.shape)
    inside = jnp.where(iota(own.shape, 0) < 6, inside, 0.0)
    outside = jnp.where(iota(own.shape, 0) < 6, outside, 0.0)
    middle = own[...] * inside
    fields = [
        jnp.where(low, x_before[...], x_after[...]) * outside,
        swap(jnp.where(low, x_after[...], x_before[...])) * outside,
        middle,
        swap(middle),
    ]
    value = corrections(4, fields, [k4[0], k4[1]], [outside, inside], blur_z_part)
    left = coarse_remainders(value + [swap(value[1])], [middle], [k4[1]], blur_z_part)[0]
    for out, here in ((e4, value[1]), (rest, left)):
        out[0] = here[2:4, 0:8]
        out[1] = swap(here)[2:4, 0:8]


def neighbours_of(up, down, axis):
    count = lax.axis_size(axis)
    ahead = [(i, (i + 1) % count) for i in range(count)]
    back = [(i, (i - 1) % count) for i in range(count)]
    return lax.ppermute(up, axis, ahead), lax.ppermute(down, axis, back)


VMEM = pl.BlockSpec(memory_space=pltpu.VMEM)
HBM = pl.BlockSpec(memory_space=pltpu.HBM)


def call(body, outs, ins, scratch=(), copies=0, flops=0, name=None):
    sems = [pltpu.SemaphoreType.DMA((copies,))] if copies else []
    return pl.pallas_call(
        body,
        out_shape=[jax.ShapeDtypeStruct(dims, F32) for dims in outs],
        in_specs=ins,
        out_specs=[VMEM] * len(outs),
        scratch_shapes=[s if not isinstance(s, tuple) else pltpu.VMEM(s, F32) for s in scratch] + sems,
        compiler_params=pltpu.CompilerParams(vmem_limit_bytes=40 * 1024 * 1024),
        cost_estimate=pl.CostEstimate(flops=flops, transcendentals=0, bytes_accessed=flops),
        name=name,
    )


def per_device(source, guess, reaction, flags):
    tile = (32, 8, LANES)
    flags, guess, source, reaction = (
        pltpu.with_memory_space_constraint(v, pltpu.HBM) for v in (flags, guess, source, reaction)
    )
    own, down, strip_up, strip_down = call(
        pack_rows,
        [tile, tile, (7, 32, LANES), (7, 32, LANES)],
        [HBM] * 4,
        scratch=[pltpu.SMEM((1, 1, flags.shape[2]), jnp.int32)] + [tile] * 6,
        copies=13,
        name="pack_rows",
    )(flags, guess, source, reaction)
    y_before, y_after = neighbours_of(own, down, "agg")
    packed, down = call(
        pack_planes, [(8, 40, LANES)] * 2, [VMEM] * 5, name="pack_planes"
    )(own, y_before, y_after, strip_up, strip_down)
    x_before, x_after = neighbours_of(packed, down, "box")
    big = (32, 40, LANES)
    *fields, inner = call(
        fine_inner,
        [big] * 6 + [(16, 16, LANES)],
        [VMEM] * 3 + [HBM] * 3,
        scratch=[(12, 40, LANES), (16, 32, LANES)],
        copies=3,
        flops=8000000,
        name="fine_inner",
    )(packed, y_before, y_after, guess, source, reaction)
    coarse, edge = call(
        fine_outer,
        [(16, 16, LANES), (4, 32, LANES)],
        [VMEM] * 10,
        scratch=[(4, 40, LANES)],
        name="fine_outer",
    )(packed, x_before, x_after, *fields, inner)
    iterate = jnp.concatenate([edge[0:2], fields[5][2:30, 0:32], edge[2:4]], axis=0)
    y_before, y_after = neighbours_of(coarse, coarse, "agg")
    extended = jnp.concatenate([y_before, coarse, y_after], axis=1)
    x_before, x_after = neighbours_of(extended[16 - FAR :], extended[:FAR], "box")
    plane = (48, LANES)
    inner = call(
        coarse_inner,
        [(8,) + plane] * 3 + [(3, 24, LANES)] * 2,
        [VMEM] * 3,
        scratch=[(3,) + plane] * 2,
        flops=4000000,
        name="coarse_inner",
    )(y_before, coarse, y_after)
    *owns, f4, k4 = call(
        coarse_outer,
        [(8, 16, LANES), (4, 8, LANES), (2, 8, LANES), (8, LANES), (2, 8, LANES)],
        [VMEM] * 7,
        scratch=[(7,) + plane] * 2,
        name="coarse_outer",
    )(x_before, x_after, *inner)
    e1, e2, e3 = call(
        unfold, [(16, 16, 64), (8, 8, 32), (4, 4, 16)], [VMEM] * 3, flops=2000000, name="unfold"
    )(*owns)
    y_before, y_after = neighbours_of(f4, f4, "agg")
    (last,) = call(pack_last, [(8, LANES)], [VMEM] * 3, name="pack_last")(y_before, f4, y_after)
    x_before, x_after = neighbours_of(last, last, "box")
    e4, rest = call(
        last_kernel, [(2, 2, 8), (2, 2, 8)], [VMEM] * 4, name="last"
    )(last, x_before, x_after, k4)
    return iterate, e1, e2, e3, e4, rest


def solution(mesh):
    spec = P("box", "agg", None)
    return jax.shard_map(
        per_device, mesh=mesh, in_specs=(spec,) * 4, out_specs=(spec,) * 6, check_vma=False
    )
```

```python
import functools

import jax
import jax.numpy as jnp
from jax import lax
from jax.experimental import pallas as pl
from jax.experimental.pallas import tpu as pltpu
from jax.sharding import PartitionSpec as P

F32 = jnp.float32
LANES = 128
FAR = 14


def coefficients(level_index):
    upper_edge = 1.1 * (2.0 + 0.02 * 4.0**level_index)
    lower_edge = upper_edge / 8.0
    midpoint = (upper_edge + lower_edge) / 2.0
    half_span = (upper_edge - lower_edge) / 2.0
    sigma_value = midpoint / half_span
    rho_first = 1.0 / sigma_value
    rho_second = 1.0 / (2.0 * sigma_value - rho_first)
    return (midpoint, rho_second * rho_first, 2.0 * rho_second / half_span)


def iota(shape, dim):
    return lax.broadcasted_iota(jnp.int32, shape, dim)


def edges(axis):
    here = lax.axis_index(axis)
    before = jnp.where(here > 0, 1.0, 0.0).astype(F32)
    after = jnp.where(here < lax.axis_size(axis) - 1, 1.0, 0.0).astype(F32)
    return before, after


def blurred(planes, stride):
    sums = [a + b for a, b in zip(planes[:-1], planes[1:])]
    out = []
    for low, high in zip(sums[:-1], sums[1:]):
        total = low + high
        beside = pltpu.roll(total, 1, 0) + pltpu.roll(total, total.shape[0] - 1, 0)
        out.append(blur_z((total + total) + beside, stride))
    return out


def blur_z(values, stride):
    lane = iota(values.shape, 1)
    left = jnp.where(lane < stride, 0.0, pltpu.roll(values, stride, 1))
    right = jnp.where(lane >= LANES - stride, 0.0, pltpu.roll(values, LANES - stride, 1))
    return (values + values) + (left + right)


def pair_rows(values):
    return values + pltpu.roll(values, values.shape[0] - 1, 0)


def halved(values, stride):
    return (values + pltpu.roll(values, LANES - stride, 1)) * 0.5


def even_lanes(shape):
    return (iota(shape, len(shape) - 1) & 1) == 0


def loop(first, stop, size, body):
    count = (stop - first) // size
    if count == 1:
        body(first)
        return

    def step(i, carry):
        body(first + i * size)
        return carry

    lax.fori_loop(0, count, step, 0)


def copy_all(sems, *pairs):
    copies = [pltpu.make_async_copy(a, b, sems.at[i]) for i, (a, b) in enumerate(pairs)]
    for copy in copies:
        copy.start()
    return copies


def pack_rows(
    flags, guess, source, reaction, up, down, strip_up, strip_down,
    flag_smem, guess_lo, guess_hi, source_lo, source_hi, reaction_lo, reaction_hi, sems,
):
    lo, hi = pl.ds(0, 8), pl.ds(24, 8)
    copies = copy_all(
        sems,
        (flags, flag_smem),
        (guess.at[:, lo, :], guess_lo),
        (guess.at[:, hi, :], guess_hi),
        (source.at[:, lo, :], source_lo),
        (source.at[:, hi, :], source_hi),
        (reaction.at[:, lo, :], reaction_lo),
        (reaction.at[:, hi, :], reaction_hi),
        (guess.at[29:32], strip_up.at[0:3]),
        (source.at[30:32], strip_up.at[3:5]),
        (reaction.at[30:32], strip_up.at[5:7]),
        (guess.at[0:3], strip_down.at[0:3]),
        (source.at[0:2], strip_down.at[3:5]),
        (reaction.at[0:2], strip_down.at[5:7]),
    )
    for copy in copies[:7]:
        copy.wait()
    boxes = flags.shape[2]
    lane = iota((8, LANES), 1)
    flag = jnp.zeros((8, LANES), F32)
    for i in range(boxes):
        flag = jnp.where(lane // (LANES // boxes) == i, flag_smem[0, 0, i].astype(F32), flag)
    flag = flag[None]
    row = iota(up.shape, 1)
    up[...] = jnp.where(
        row >= 5,
        guess_hi[...],
        jnp.where(
            row >= 3,
            pltpu.roll(source_hi[...], 5, 1),
            jnp.where(row >= 1, pltpu.roll(reaction_hi[...], 3, 1), flag),
        ),
    )
    down[...] = jnp.where(
        row < 3,
        guess_lo[...],
        jnp.where(
            row < 5,
            pltpu.roll(source_lo[...], 3, 1),
            jnp.where(row < 7, pltpu.roll(reaction_lo[...], 5, 1), flag),
        ),
    )
    for copy in copies[7:]:
        copy.wait()


def halo_tiles(from_before, from_after, before, after):
    row = iota(from_before.shape, 1)
    first = row < 4
    guess = jnp.where(first, from_after * after, from_before * before)
    source = jnp.where(first, pltpu.roll(from_after, 5, 1), pltpu.roll(from_before, 3, 1))
    reaction = jnp.where(first, pltpu.roll(from_after, 3, 1), pltpu.roll(from_before, 5, 1))
    return guess, source, reaction


def pack_planes(own, from_before, from_after, strip_up, strip_down, up, down):
    before, after = edges("agg")
    tile = (8, LANES)
    own_mask = jnp.broadcast_to(own[0, 0:1, :], (32, LANES))
    lo_mask = jnp.broadcast_to(from_before[0, 0:1, :] * before, tile)
    hi_mask = jnp.broadcast_to(from_after[0, 7:8, :] * after, tile)
    halo_mask = jnp.where(iota(tile, 0) < 4, hi_mask, lo_mask)
    planes = from_before.shape[0]
    for target, strip, first, local in (
        (up, strip_up, planes - 4, (1, 2, 2)),
        (down, strip_down, 0, (0, 0, 0)),
    ):
        tiles = halo_tiles(from_before[first : first + 4], from_after[first : first + 4], before, after)
        target[0:7, 0:32, :] = strip[...]
        at = 0
        for tile, start, count in zip(tiles, local, (3, 2, 2)):
            target[at : at + count, 32:40, :] = tile[start : start + count]
            at += count
        target[7, 0:32, :] = own_mask
        target[7, 32:40, :] = halo_mask


SHIFT = 8.0 / 7.0


def even_rows(ref, i, rows):
    return ref[i, pl.ds(0, rows, stride=2), :]


def fine_inner(
    packed, from_before, from_after, guess, source, reaction,
    g, s, k, d, u, w, coarse, pairs, kpairs, sems,
):
    rows = pl.ds(0, 32)
    copies = copy_all(
        sems, (guess, g.at[:, rows, :]), (source, s.at[:, rows, :]), (reaction, k.at[:, rows, :])
    )
    before, after = edges("agg")
    theta, c1, c2 = coefficients(0)

    def assemble(x):
        at = pl.ds(x, 32)
        tiles = halo_tiles(from_before[at], from_after[at], before, after)
        g[at, 32:40, :] = tiles[0]
        s[at, 32:40, :] = tiles[1]
        k[at, 32:40, :] = tiles[2]

    loop(0, 32, 32, assemble)
    for copy in copies:
        copy.wait()

    def remainders(field, x, size):
        planes = [field[x + i] for i in range(-1, size + 1)]
        mask = packed[7]
        out = []
        for i, q in enumerate(blurred(planes, 1)):
            r = mask * (s[x + i] - (k[x + i] + SHIFT) * planes[i + 1] + q * (1.0 / 56.0))
            out.append((r, planes[i + 1]))
        return out

    def first(x):
        out = remainders(g, x, 10)
        for i, (r, middle) in enumerate(out):
            step = r * (1.0 / theta)
            d[x + i] = step
            u[x + i] = middle + step

    loop(1, 31, 10, first)

    def second(x):
        out = [m + (c1 * d[x + i] + c2 * r) for i, (r, m) in enumerate(remainders(u, x, 14))]
        for i, value in enumerate(out):
            w[x + i] = value

    loop(2, 30, 14, second)

    def third(x):
        out = [r for r, _ in remainders(w, x, 24)]
        at = (x - 4) // 2
        for i in range(len(out) // 2):
            pairs[at + i] = pair_rows(out[2 * i] + out[2 * i + 1])

    loop(4, 28, 24, third)

    for i in range(16):
        kpairs[i] = pair_rows(k[2 * i, 0:32, :] + k[2 * i + 1, 0:32, :])
    even = even_lanes((16, LANES))
    for i in range(16):
        value = pltpu.roll(halved(even_rows(kpairs, i, 16), 1), 1, 1)
        if 2 <= i < 14:
            value = jnp.where(even, halved(even_rows(pairs, i - 2, 16), 1), value)
        coarse[i] = value


def fine_outer(packed, x_before, x_after, g, s, k, d, u, w, inner, coarse, edge, pairs):
    xbefore, xafter = edges("box")
    theta, c1, c2 = coefficients(0)
    new_d, new_u, new_w = {}, {}, {}

    def side(x, before, after, own):
        return before(x + 3) if x < 0 else after(x - 32) if x > 31 else own(x)

    def guess_at(x):
        return side(x, lambda i: x_before[i] * xbefore, lambda i: x_after[i] * xafter, lambda i: g[i])

    def source_at(x):
        return side(x, lambda i: x_before[i + 2], lambda i: x_after[i + 3], lambda i: s[i])

    def reaction_at(x):
        return side(x, lambda i: x_before[i + 4], lambda i: x_after[i + 5], lambda i: k[i])

    def mask_at(x):
        return side(x, lambda i: x_before[7] * xbefore, lambda i: x_after[7] * xafter, lambda i: packed[7])

    def remainders(field, first, size):
        planes = [field(x) for x in range(first - 1, first + size + 1)]
        out = []
        for i, q in enumerate(blurred(planes, 1)):
            x = first + i
            r = mask_at(x) * (source_at(x) - (reaction_at(x) + SHIFT) * planes[i + 1] + q * (1.0 / 56.0))
            out.append((x, r, planes[i + 1]))
        return out

    for first in (-2, 31):
        for x, r, middle in remainders(guess_at, first, 3):
            new_d[x] = r * (1.0 / theta)
            new_u[x] = middle + new_d[x]
    for first in (-1, 30):
        for x, r, middle in remainders(lambda i: new_u[i] if i in new_u else u[i], first, 3):
            step = new_d[x] if x in new_d else d[x]
            new_w[x] = middle + (c1 * step + c2 * r)
    for at, x in enumerate((0, 1, 30, 31)):
        edge[at] = new_w[x][0:32]
    for at, first in enumerate((0, 28)):
        out = [r for _, r, _ in remainders(lambda i: new_w[i] if i in new_w else w[i], first, 4)]
        pairs[2 * at] = pair_rows(out[0] + out[1])
        pairs[2 * at + 1] = pair_rows(out[2] + out[3])
    even = even_lanes((16, LANES))
    for at, x in enumerate((0, 1, 14, 15)):
        coarse[x] = jnp.where(even, halved(even_rows(pairs, at, 16), 1), inner[x])
    coarse[2:14] = inner[2:14]


def level_constants(level):
    theta, c1, c2 = coefficients(level)
    return (1.0 + c1) / theta + c2, c2 / theta


def masks_of(rows, lo, hi):
    before, after = edges("agg")
    xbefore, xafter = edges("box")
    shape = (rows, LANES)
    row = iota(shape, 0)
    inside = jnp.where(row < lo, before, jnp.where(row >= hi, after, 1.0))
    return inside * jnp.where(even_lanes(shape), xbefore, xafter), inside


def corrections(level, planes, reactions, masks):
    alpha, beta = level_constants(level)
    return [
        m * (f * (alpha - beta * (k + SHIFT)) + q * (beta / 56.0))
        for f, k, m, q in zip(planes[1:-1], reactions, masks, blurred(planes, 2**level))
    ]


def coarse_remainders(level, planes, fields, reactions):
    return [
        f - (k + SHIFT) * e + q * (1.0 / 56.0)
        for f, k, e, q in zip(fields, reactions, planes[1:-1], blurred(planes, 2**level))
    ]


def to_left(values):
    return pltpu.roll(values, LANES - 1, 1)


def to_right(values):
    return pltpu.roll(values, 1, 1)


def swap(values):
    return jnp.where(even_lanes(values.shape), to_left(values), to_right(values))


def folded(lo, hi):
    even = even_lanes(lo.shape)
    return jnp.where(even, lo, to_right(hi)), jnp.where(even, to_left(lo), hi)


def coarse_inner(y_before, own, y_after, f, k, e, f2, k2, pairs, kpairs):
    _, inside = masks_of(48, 16, 32)
    fields, reactions = [], []
    for j in range(8):
        lo = jnp.concatenate([y_before[j], own[j], y_after[j]], axis=0)
        hi = jnp.concatenate([y_before[15 - j], own[15 - j], y_after[15 - j]], axis=0)
        field, reaction = folded(lo, hi)
        fields.append(field * inside)
        reactions.append(reaction)
    for j in range(2):
        f[j], k[j] = fields[j], reactions[j]
    for j in range(3):
        kpairs[j] = pair_rows(reactions[2 * j + 2] + reactions[2 * j + 3])
    value = corrections(1, fields + [swap(fields[7])], reactions[1:], [inside] * 7)
    for j in range(7):
        e[j + 1] = value[j]
    rest = coarse_remainders(1, value + [swap(value[6])], fields[2:], reactions[2:])
    for j in range(3):
        pairs[j] = pair_rows(rest[2 * j] + rest[2 * j + 1])
    _, inside = masks_of(24, 8, 16)
    for j in range(3):
        f2[j] = halved(even_rows(pairs, j, 24), 2) * inside
        k2[j] = halved(even_rows(kpairs, j, 24), 2)


def coarse_outer(
    x_before, x_after, f_in, k_in, e_in, f2_in, k2_in, own1, own2, own3, f4, k4,
    pairs, kpairs,
):
    outside, inside = masks_of(48, 16, 32)
    fields, reactions = [], []
    for j in range(FAR):
        field, reaction = folded(x_before[j], x_after[FAR - 1 - j])
        fields.append(field * outside)
        reactions.append(reaction)
    for j in range(2):
        fields.append(f_in[j])
        reactions.append(k_in[j])
    for j in range(7):
        kpairs[j] = pair_rows(reactions[2 * j + 2] + reactions[2 * j + 3])
    value = corrections(1, fields, reactions[1:15], [outside] * 13 + [inside])
    own1[0] = value[13][16:32]
    for j in range(1, 8):
        own1[j] = e_in[j, 16:32, :]
    rest = coarse_remainders(1, value + [e_in[1], e_in[2]], fields[2:], reactions[2:])
    for j in range(7):
        pairs[j] = pair_rows(rest[2 * j] + rest[2 * j + 1])
    outside, inside = masks_of(24, 8, 16)
    fields = [halved(even_rows(pairs, j, 24), 2) * (outside if j < 6 else inside) for j in range(7)]
    fields += [f2_in[j] for j in range(3)]
    reactions = [halved(even_rows(kpairs, j, 24), 2) for j in range(7)] + [k2_in[j] for j in range(3)]
    for p in range(4):
        kpairs[p, 0:24, :] = pair_rows(reactions[2 * p + 2] + reactions[2 * p + 3])
    value = corrections(2, fields + [swap(fields[9])], reactions[1:], [outside] * 5 + [inside] * 4)
    for j in range(4):
        own2[j] = value[5 + j][8:16]
    rest = coarse_remainders(2, value + [swap(value[8])], fields[2:], reactions[2:])
    for p in range(4):
        pairs[p, 0:24, :] = pair_rows(rest[2 * p] + rest[2 * p + 1])
    outside, inside = masks_of(16, 4, 8)
    fields = [halved(even_rows(pairs, j, 16), 4) * (outside if j < 2 else inside) for j in range(4)]
    reactions = [halved(even_rows(kpairs, j, 16), 4) for j in range(4)]
    for p in range(2):
        kpairs[p, 0:16, :] = pair_rows(reactions[2 * p] + reactions[2 * p + 1])
    value = corrections(3, fields + [swap(fields[3])], reactions[1:], [outside, inside, inside])
    for j in range(2):
        own3[j] = value[1 + j][0:8]
    rest = coarse_remainders(3, value + [swap(value[2])], fields[2:], reactions[2:])
    pairs[0, 0:16, :] = pair_rows(rest[0] + rest[1])
    f4[...] = halved(even_rows(pairs, 0, 8), 8)
    for p in range(2):
        k4[p] = halved(even_rows(kpairs, p, 8), 8)


def unfold(own1, own2, own3, e1, e2, e3):
    rows = (slice(0, 16), slice(0, 8), slice(4, 8))
    for level, own, out, part in zip((1, 2, 3), (own1, own2, own3), (e1, e2, e3), rows):
        planes, _, lanes = out.shape
        source = iota((LANES, LANES), 0)
        target = iota((LANES, LANES), 1)
        hit = source == ((target & 63) << level) + (target >> 6)
        values = own[...].reshape(-1, LANES)
        values = jnp.dot(
            values,
            jnp.where(hit, 1.0, 0.0).astype(F32),
            precision=lax.Precision.HIGHEST,
            preferred_element_type=F32,
        ).reshape(own.shape)
        for j in range(planes // 2):
            value = values[j]
            out[j] = value[part, 0:lanes]
            out[planes - 1 - j] = pltpu.roll(value, 64, 1)[part, 0:lanes]


def pack_last(y_before, own, y_after, out):
    before, after = edges("agg")
    row = iota(own.shape, 0)
    lo = pltpu.roll(y_before[...], 6, 0) * before
    hi = pltpu.roll(y_after[...], 2, 0) * after
    out[...] = jnp.where(row < 2, lo, jnp.where(row < 4, own[...], jnp.where(row < 6, hi, 0.0)))


def last_kernel(own, x_before, x_after, k4, e4, rest):
    outside, inside = masks_of(8, 2, 4)
    even = even_lanes(own.shape)
    row = iota(own.shape, 0)
    inside = jnp.where(row < 6, inside, 0.0)
    outside = jnp.where(row < 6, outside, 0.0)
    middle = own[...] * inside
    fields = [
        jnp.where(even, x_before[...], x_after[...]) * outside,
        swap(jnp.where(even, x_after[...], x_before[...])) * outside,
        middle,
        swap(middle),
    ]
    value = corrections(4, fields, [k4[0], k4[1]], [outside, inside])
    left = coarse_remainders(4, value + [swap(value[1])], [middle], [k4[1]])[0]
    lane = iota(own.shape, 1)
    for out, here in ((e4, value[1]), (rest, left)):
        for side, folded_plane in enumerate((here, to_left(here))):
            cells = [
                jnp.where(lane == z, pltpu.roll(folded_plane, (LANES - 15 * z) % LANES, 1), 0.0)
                for z in range(8)
            ]
            while len(cells) > 1:
                cells = [a + b for a, b in zip(cells[::2], cells[1::2])]
            out[side] = cells[0][2:4, 0:8]


def neighbours_of(up, down, axis):
    count = lax.axis_size(axis)
    ahead = [(i, (i + 1) % count) for i in range(count)]
    back = [(i, (i - 1) % count) for i in range(count)]
    return lax.ppermute(up, axis, ahead), lax.ppermute(down, axis, back)


VMEM = pl.BlockSpec(memory_space=pltpu.VMEM)
HBM = pl.BlockSpec(memory_space=pltpu.HBM)


def call(body, outs, ins, scratch=(), copies=0, flops=0, name=None):
    sems = [pltpu.SemaphoreType.DMA((copies,))] if copies else []
    return pl.pallas_call(
        body,
        out_shape=[jax.ShapeDtypeStruct(dims, F32) for dims in outs],
        in_specs=ins,
        out_specs=[VMEM] * len(outs),
        scratch_shapes=[s if not isinstance(s, tuple) else pltpu.VMEM(s, F32) for s in scratch] + sems,
        compiler_params=pltpu.CompilerParams(vmem_limit_bytes=40 * 1024 * 1024),
        cost_estimate=pl.CostEstimate(flops=flops, transcendentals=0, bytes_accessed=flops),
        name=name,
    )


def per_device(source, guess, reaction, flags):
    tile = (32, 8, LANES)
    flags, guess, source, reaction = (
        pltpu.with_memory_space_constraint(v, pltpu.HBM) for v in (flags, guess, source, reaction)
    )
    own, down, strip_up, strip_down = call(
        pack_rows,
        [tile, tile, (7, 32, LANES), (7, 32, LANES)],
        [HBM] * 4,
        scratch=[pltpu.SMEM((1, 1, flags.shape[2]), jnp.int32)] + [tile] * 6,
        copies=13,
        name="pack_rows",
    )(flags, guess, source, reaction)
    y_before, y_after = neighbours_of(own, down, "agg")
    packed, down = call(
        pack_planes, [(8, 40, LANES)] * 2, [VMEM] * 5, name="pack_planes"
    )(own, y_before, y_after, strip_up, strip_down)
    x_before, x_after = neighbours_of(packed, down, "box")
    big = (32, 40, LANES)
    *fields, inner = call(
        fine_inner,
        [big] * 6 + [(16, 16, LANES)],
        [VMEM] * 3 + [HBM] * 3,
        scratch=[(12, 40, LANES), (16, 32, LANES)],
        copies=3,
        flops=8000000,
        name="fine_inner",
    )(packed, y_before, y_after, guess, source, reaction)
    coarse, edge = call(
        fine_outer,
        [(16, 16, LANES), (4, 32, LANES)],
        [VMEM] * 10,
        scratch=[(4, 40, LANES)],
        name="fine_outer",
    )(packed, x_before, x_after, *fields, inner)
    iterate = jnp.concatenate([edge[0:2], fields[5][2:30, 0:32], edge[2:4]], axis=0)
    y_before, y_after = neighbours_of(coarse, coarse, "agg")
    y_before, iterate = lax.optimization_barrier((y_before, iterate))
    extended = jnp.concatenate([y_before, coarse, y_after], axis=1)
    x_before, x_after = neighbours_of(extended[16 - FAR :], extended[:FAR], "box")
    plane = (48, LANES)
    inner = call(
        coarse_inner,
        [(2,) + plane] * 2 + [(8,) + plane] + [(3, 24, LANES)] * 2,
        [VMEM] * 3,
        scratch=[(3,) + plane] * 2,
        flops=4000000,
        name="coarse_inner",
    )(y_before, coarse, y_after)
    *owns, f4, k4 = call(
        coarse_outer,
        [(8, 16, LANES), (4, 8, LANES), (2, 8, LANES), (8, LANES), (2, 8, LANES)],
        [VMEM] * 7,
        scratch=[(7,) + plane] * 2,
        name="coarse_outer",
    )(x_before, x_after, *inner)
    e1, e2, e3 = call(
        unfold, [(16, 16, 64), (8, 8, 32), (4, 4, 16)], [VMEM] * 3, flops=2000000, name="unfold"
    )(*owns)
    y_before, y_after = neighbours_of(f4, f4, "agg")
    y_before, e1, e2, e3 = lax.optimization_barrier((y_before, e1, e2, e3))
    (last,) = call(pack_last, [(8, LANES)], [VMEM] * 3, name="pack_last")(y_before, f4, y_after)
    x_before, x_after = neighbours_of(last, last, "box")
    e4, rest = call(
        last_kernel, [(2, 2, 8), (2, 2, 8)], [VMEM] * 4, name="last"
    )(last, x_before, x_after, k4)
    return iterate, e1, e2, e3, e4, rest


def solution(mesh):
    spec = P("box", "agg", None)
    return jax.shard_map(
        per_device, mesh=mesh, in_specs=(spec,) * 4, out_specs=(spec,) * 6, check_vma=False
    )
```

```python
import functools

import jax
import jax.numpy as jnp
from jax import lax
from jax.experimental import pallas as pl
from jax.experimental.pallas import tpu as pltpu
from jax.sharding import PartitionSpec as P

F32 = jnp.float32
LANES = 128
FAR = 14


def coefficients(level_index):
    upper_edge = 1.1 * (2.0 + 0.02 * 4.0**level_index)
    lower_edge = upper_edge / 8.0
    midpoint = (upper_edge + lower_edge) / 2.0
    half_span = (upper_edge - lower_edge) / 2.0
    sigma_value = midpoint / half_span
    rho_first = 1.0 / sigma_value
    rho_second = 1.0 / (2.0 * sigma_value - rho_first)
    return (midpoint, rho_second * rho_first, 2.0 * rho_second / half_span)


def iota(shape, dim):
    return lax.broadcasted_iota(jnp.int32, shape, dim)


def edges(axis):
    here = lax.axis_index(axis)
    before = jnp.where(here > 0, 1.0, 0.0).astype(F32)
    after = jnp.where(here < lax.axis_size(axis) - 1, 1.0, 0.0).astype(F32)
    return before, after


def blurred(planes, stride):
    sums = [a + b for a, b in zip(planes[:-1], planes[1:])]
    out = []
    for low, high in zip(sums[:-1], sums[1:]):
        total = low + high
        beside = pltpu.roll(total, 1, 0) + pltpu.roll(total, total.shape[0] - 1, 0)
        out.append(blur_z((total + total) + beside, stride))
    return out


def across_of(axis):
    return ("box", 2) if axis == "agg" else ("agg", 1)


def moves_up(axis):
    name, width = across_of(axis)
    return lax.axis_index(name) // width % 2 == 0


def in_order(axis, first, second):
    up = moves_up(axis)
    return jnp.where(up, first, second), jnp.where(up, second, first)


def blur_z(values, stride):
    lane = iota(values.shape, 1)
    left = jnp.where(lane < stride, 0.0, pltpu.roll(values, stride, 1))
    right = jnp.where(lane >= LANES - stride, 0.0, pltpu.roll(values, LANES - stride, 1))
    return (values + values) + (left + right)


def pair_rows(values):
    return values + pltpu.roll(values, values.shape[0] - 1, 0)


def halved(values, stride):
    return (values + pltpu.roll(values, LANES - stride, 1)) * 0.5


def even_lanes(shape):
    return (iota(shape, len(shape) - 1) & 1) == 0


def loop(first, stop, size, body):
    count = (stop - first) // size
    if count == 1:
        body(first)
        return

    def step(i, carry):
        body(first + i * size)
        return carry

    lax.fori_loop(0, count, step, 0)


def copy_all(sems, *pairs):
    copies = [pltpu.make_async_copy(a, b, sems.at[i]) for i, (a, b) in enumerate(pairs)]
    for copy in copies:
        copy.start()
    return copies


def pack_rows(
    flags, guess, source, reaction, first, second, strip_up, strip_down,
    flag_smem, guess_lo, guess_hi, source_lo, source_hi, reaction_lo, reaction_hi, sems,
):
    lo, hi = pl.ds(0, 8), pl.ds(24, 8)
    copies = copy_all(
        sems,
        (flags, flag_smem),
        (guess.at[:, lo, :], guess_lo),
        (guess.at[:, hi, :], guess_hi),
        (source.at[:, lo, :], source_lo),
        (source.at[:, hi, :], source_hi),
        (reaction.at[:, lo, :], reaction_lo),
        (reaction.at[:, hi, :], reaction_hi),
        (guess.at[29:32], strip_up.at[0:3]),
        (source.at[30:32], strip_up.at[3:5]),
        (reaction.at[30:32], strip_up.at[5:7]),
        (guess.at[0:3], strip_down.at[0:3]),
        (source.at[0:2], strip_down.at[3:5]),
        (reaction.at[0:2], strip_down.at[5:7]),
    )
    for copy in copies[:7]:
        copy.wait()
    boxes = flags.shape[2]
    lane = iota((8, LANES), 1)
    flag = jnp.zeros((8, LANES), F32)
    for i in range(boxes):
        flag = jnp.where(lane // (LANES // boxes) == i, flag_smem[0, 0, i].astype(F32), flag)
    flag = flag[None]
    row = iota(first.shape, 1)
    up = jnp.where(
        row >= 5,
        guess_hi[...],
        jnp.where(
            row >= 3,
            pltpu.roll(source_hi[...], 5, 1),
            jnp.where(row >= 1, pltpu.roll(reaction_hi[...], 3, 1), flag),
        ),
    )
    down = jnp.where(
        row < 3,
        guess_lo[...],
        jnp.where(
            row < 5,
            pltpu.roll(source_lo[...], 3, 1),
            jnp.where(row < 7, pltpu.roll(reaction_lo[...], 5, 1), flag),
        ),
    )
    first[...], second[...] = in_order("agg", up, down)
    for copy in copies[7:]:
        copy.wait()


def halo_tiles(from_before, from_after, before, after):
    row = iota(from_before.shape, 1)
    first = row < 4
    guess = jnp.where(first, from_after * after, from_before * before)
    source = jnp.where(first, pltpu.roll(from_after, 5, 1), pltpu.roll(from_before, 3, 1))
    reaction = jnp.where(first, pltpu.roll(from_after, 3, 1), pltpu.roll(from_before, 5, 1))
    return guess, source, reaction


def flag_plane(own, lo, hi):
    tile = (8, LANES)
    halo = jnp.where(iota(tile, 0) < 4, jnp.broadcast_to(hi, tile), jnp.broadcast_to(lo, tile))
    return jnp.concatenate([jnp.broadcast_to(own, (32, LANES)), halo], axis=0)


def pack_planes(own_first, own_second, from_first, from_second, strip_up, strip_down, first, second, mask):
    before, after = edges("agg")
    own, _ = in_order("agg", own_first[0, 0:1, :], own_second[0, 0:1, :])
    from_before, from_after = in_order("agg", from_first[...], from_second[...])
    lo = from_before[0, 0:1, :] * before
    hi = from_after[0, 7:8, :] * after
    mask[...] = flag_plane(own, lo, hi)
    planes = from_before.shape[0]
    strips, tiles = [], []
    for strip, at, local in ((strip_up, planes - 4, (1, 2, 2)), (strip_down, 0, (0, 0, 0))):
        fields = halo_tiles(from_before[at : at + 4], from_after[at : at + 4], before, after)
        rows = [tile[i] for tile, start, count in zip(fields, local, (3, 2, 2)) for i in range(start, start + count)]
        row = iota(rows[0].shape, 0)
        rows[0] = jnp.where(row == 3, own, jnp.where(row == 4, lo, rows[0]))
        rows[1] = jnp.where(row == 3, hi, rows[1])
        strips.append(strip[...])
        tiles.append(rows)
    first[:, 0:32, :], second[:, 0:32, :] = in_order("box", *strips)
    for i, (up, down) in enumerate(zip(*tiles)):
        first[i, 32:40, :], second[i, 32:40, :] = in_order("box", up, down)


SHIFT = 8.0 / 7.0


def even_rows(ref, i, rows):
    return ref[i, pl.ds(0, rows, stride=2), :]


def fine_inner(
    mask_ref, from_first, from_second, guess, source, reaction,
    g, s, k, d, u, w, coarse, pairs, kpairs, sems,
):
    rows = pl.ds(0, 32)
    copies = copy_all(
        sems, (guess, g.at[:, rows, :]), (source, s.at[:, rows, :]), (reaction, k.at[:, rows, :])
    )
    before, after = edges("agg")
    theta, c1, c2 = coefficients(0)

    def assemble(x):
        at = pl.ds(x, 32)
        sides = in_order("agg", from_first[at], from_second[at])
        tiles = halo_tiles(*sides, before, after)
        g[at, 32:40, :] = tiles[0]
        s[at, 32:40, :] = tiles[1]
        k[at, 32:40, :] = tiles[2]

    loop(0, 32, 32, assemble)
    for copy in copies:
        copy.wait()

    def remainders(field, x, size):
        planes = [field[x + i] for i in range(-1, size + 1)]
        mask = mask_ref[...]
        out = []
        for i, q in enumerate(blurred(planes, 1)):
            r = mask * (s[x + i] - (k[x + i] + SHIFT) * planes[i + 1] + q * (1.0 / 56.0))
            out.append((r, planes[i + 1]))
        return out

    def first(x):
        out = remainders(g, x, 10)
        for i, (r, middle) in enumerate(out):
            step = r * (1.0 / theta)
            d[x + i] = step
            u[x + i] = middle + step

    loop(1, 31, 10, first)

    def second(x):
        out = [m + (c1 * d[x + i] + c2 * r) for i, (r, m) in enumerate(remainders(u, x, 14))]
        for i, value in enumerate(out):
            w[x + i] = value

    loop(2, 30, 14, second)

    def third(x):
        out = [r for r, _ in remainders(w, x, 24)]
        at = (x - 4) // 2
        for i in range(len(out) // 2):
            pairs[at + i] = pair_rows(out[2 * i] + out[2 * i + 1])

    loop(4, 28, 24, third)

    for i in range(16):
        kpairs[i] = pair_rows(k[2 * i, 0:32, :] + k[2 * i + 1, 0:32, :])
    even = even_lanes((16, LANES))
    for i in range(16):
        value = pltpu.roll(halved(even_rows(kpairs, i, 16), 1), 1, 1)
        if 2 <= i < 14:
            value = jnp.where(even, halved(even_rows(pairs, i - 2, 16), 1), value)
        coarse[i] = value


def fine_outer(mask_ref, from_first, from_second, g, s, k, d, u, w, inner, coarse, edge, pairs):
    xbefore, xafter = edges("box")
    x_before, x_after = in_order("box", from_first[...], from_second[...])
    mask_before, mask_after = (
        flag_plane(x[0, 35:36], x[0, 36:37], x[1, 35:36]) * edge for x, edge in ((x_before, xbefore), (x_after, xafter))
    )
    theta, c1, c2 = coefficients(0)
    new_d, new_u, new_w = {}, {}, {}

    def side(x, before, after, own):
        return before(x + 3) if x < 0 else after(x - 32) if x > 31 else own(x)

    def guess_at(x):
        return side(x, lambda i: x_before[i] * xbefore, lambda i: x_after[i] * xafter, lambda i: g[i])

    def source_at(x):
        return side(x, lambda i: x_before[i + 2], lambda i: x_after[i + 3], lambda i: s[i])

    def reaction_at(x):
        return side(x, lambda i: x_before[i + 4], lambda i: x_after[i + 5], lambda i: k[i])

    def mask_at(x):
        return side(x, lambda i: mask_before, lambda i: mask_after, lambda i: mask_ref[...])

    def remainders(field, first, size):
        planes = [field(x) for x in range(first - 1, first + size + 1)]
        out = []
        for i, q in enumerate(blurred(planes, 1)):
            x = first + i
            r = mask_at(x) * (source_at(x) - (reaction_at(x) + SHIFT) * planes[i + 1] + q * (1.0 / 56.0))
            out.append((x, r, planes[i + 1]))
        return out

    for first in (-2, 31):
        for x, r, middle in remainders(guess_at, first, 3):
            new_d[x] = r * (1.0 / theta)
            new_u[x] = middle + new_d[x]
    for first in (-1, 30):
        for x, r, middle in remainders(lambda i: new_u[i] if i in new_u else u[i], first, 3):
            step = new_d[x] if x in new_d else d[x]
            new_w[x] = middle + (c1 * step + c2 * r)
    for at, x in enumerate((0, 1, 30, 31)):
        edge[at] = new_w[x][0:32]
    for at, first in enumerate((0, 28)):
        out = [r for _, r, _ in remainders(lambda i: new_w[i] if i in new_w else w[i], first, 4)]
        pairs[2 * at] = pair_rows(out[0] + out[1])
        pairs[2 * at + 1] = pair_rows(out[2] + out[3])
    even = even_lanes((16, LANES))
    for at, x in enumerate((0, 1, 14, 15)):
        coarse[x] = jnp.where(even, halved(even_rows(pairs, at, 16), 1), inner[x])
    coarse[2:14] = inner[2:14]


def level_constants(level):
    theta, c1, c2 = coefficients(level)
    return (1.0 + c1) / theta + c2, c2 / theta


def masks_of(rows, lo, hi):
    before, after = edges("agg")
    xbefore, xafter = edges("box")
    shape = (rows, LANES)
    row = iota(shape, 0)
    inside = jnp.where(row < lo, before, jnp.where(row >= hi, after, 1.0))
    return inside * jnp.where(even_lanes(shape), xbefore, xafter), inside


def corrections(level, planes, reactions, masks):
    alpha, beta = level_constants(level)
    return [
        m * (f * (alpha - beta * (k + SHIFT)) + q * (beta / 56.0))
        for f, k, m, q in zip(planes[1:-1], reactions, masks, blurred(planes, 2**level))
    ]


def coarse_remainders(level, planes, fields, reactions):
    return [
        f - (k + SHIFT) * e + q * (1.0 / 56.0)
        for f, k, e, q in zip(fields, reactions, planes[1:-1], blurred(planes, 2**level))
    ]


def to_left(values):
    return pltpu.roll(values, LANES - 1, 1)


def to_right(values):
    return pltpu.roll(values, 1, 1)


def swap(values):
    return jnp.where(even_lanes(values.shape), to_left(values), to_right(values))


def folded(lo, hi):
    even = even_lanes(lo.shape)
    return jnp.where(even, lo, to_right(hi)), jnp.where(even, to_left(lo), hi)


def coarse_inner(y_before, own, y_after, f, k, e, f2, k2, pairs, kpairs):
    _, inside = masks_of(48, 16, 32)
    fields, reactions = [], []
    for j in range(8):
        lo = jnp.concatenate([y_before[j], own[j], y_after[j]], axis=0)
        hi = jnp.concatenate([y_before[15 - j], own[15 - j], y_after[15 - j]], axis=0)
        field, reaction = folded(lo, hi)
        fields.append(field * inside)
        reactions.append(reaction)
    for j in range(2):
        f[j], k[j] = fields[j], reactions[j]
    for j in range(3):
        kpairs[j] = pair_rows(reactions[2 * j + 2] + reactions[2 * j + 3])
    value = corrections(1, fields + [swap(fields[7])], reactions[1:], [inside] * 7)
    for j in range(7):
        e[j + 1] = value[j]
    rest = coarse_remainders(1, value + [swap(value[6])], fields[2:], reactions[2:])
    for j in range(3):
        pairs[j] = pair_rows(rest[2 * j] + rest[2 * j + 1])
    _, inside = masks_of(24, 8, 16)
    for j in range(3):
        f2[j] = halved(even_rows(pairs, j, 24), 2) * inside
        k2[j] = halved(even_rows(kpairs, j, 24), 2)


def coarse_outer(
    from_first, from_second, f_in, k_in, e_in, f2_in, k2_in, own1, own2, own3, f4, k4,
    pairs, kpairs,
):
    outside, inside = masks_of(48, 16, 32)
    fields, reactions = [], []
    x_before, x_after = in_order("box", from_first[...], from_second[...])
    for j in range(FAR):
        field, reaction = folded(x_before[j], x_after[FAR - 1 - j])
        fields.append(field * outside)
        reactions.append(reaction)
    for j in range(2):
        fields.append(f_in[j])
        reactions.append(k_in[j])
    for j in range(7):
        kpairs[j] = pair_rows(reactions[2 * j + 2] + reactions[2 * j + 3])
    value = corrections(1, fields, reactions[1:15], [outside] * 13 + [inside])
    own1[0] = value[13][16:32]
    for j in range(1, 8):
        own1[j] = e_in[j, 16:32, :]
    rest = coarse_remainders(1, value + [e_in[1], e_in[2]], fields[2:], reactions[2:])
    for j in range(7):
        pairs[j] = pair_rows(rest[2 * j] + rest[2 * j + 1])
    outside, inside = masks_of(24, 8, 16)
    fields = [halved(even_rows(pairs, j, 24), 2) * (outside if j < 6 else inside) for j in range(7)]
    fields += [f2_in[j] for j in range(3)]
    reactions = [halved(even_rows(kpairs, j, 24), 2) for j in range(7)] + [k2_in[j] for j in range(3)]
    for p in range(4):
        kpairs[p, 0:24, :] = pair_rows(reactions[2 * p + 2] + reactions[2 * p + 3])
    value = corrections(2, fields + [swap(fields[9])], reactions[1:], [outside] * 5 + [inside] * 4)
    for j in range(4):
        own2[j] = value[5 + j][8:16]
    rest = coarse_remainders(2, value + [swap(value[8])], fields[2:], reactions[2:])
    for p in range(4):
        pairs[p, 0:24, :] = pair_rows(rest[2 * p] + rest[2 * p + 1])
    outside, inside = masks_of(16, 4, 8)
    fields = [halved(even_rows(pairs, j, 16), 4) * (outside if j < 2 else inside) for j in range(4)]
    reactions = [halved(even_rows(kpairs, j, 16), 4) for j in range(4)]
    for p in range(2):
        kpairs[p, 0:16, :] = pair_rows(reactions[2 * p] + reactions[2 * p + 1])
    value = corrections(3, fields + [swap(fields[3])], reactions[1:], [outside, inside, inside])
    for j in range(2):
        own3[j] = value[1 + j][0:8]
    rest = coarse_remainders(3, value + [swap(value[2])], fields[2:], reactions[2:])
    pairs[0, 0:16, :] = pair_rows(rest[0] + rest[1])
    f4[...] = halved(even_rows(pairs, 0, 8), 8)
    for p in range(2):
        k4[p] = halved(even_rows(kpairs, p, 8), 8)


def unfold(own1, own2, own3, e1, e2, e3):
    rows = (slice(0, 16), slice(0, 8), slice(4, 8))
    for level, own, out, part in zip((1, 2, 3), (own1, own2, own3), (e1, e2, e3), rows):
        planes, _, lanes = out.shape
        source = iota((LANES, LANES), 0)
        target = iota((LANES, LANES), 1)
        hit = source == ((target & 63) << level) + (target >> 6)
        values = own[...].reshape(-1, LANES)
        values = jnp.dot(
            values,
            jnp.where(hit, 1.0, 0.0).astype(F32),
            precision=lax.Precision.HIGHEST,
            preferred_element_type=F32,
        ).reshape(own.shape)
        for j in range(planes // 2):
            value = values[j]
            out[j] = value[part, 0:lanes]
            out[planes - 1 - j] = pltpu.roll(value, 64, 1)[part, 0:lanes]


def pack_last(from_first, own, from_second, out):
    before, after = edges("agg")
    row = iota(own.shape, 0)
    y_before, y_after = in_order("agg", from_first[...], from_second[...])
    lo = pltpu.roll(y_before, 6, 0) * before
    hi = pltpu.roll(y_after, 2, 0) * after
    out[...] = jnp.where(row < 2, lo, jnp.where(row < 4, own[...], jnp.where(row < 6, hi, 0.0)))


def last_kernel(own, from_first, from_second, k4, e4, rest):
    outside, inside = masks_of(8, 2, 4)
    even = even_lanes(own.shape)
    row = iota(own.shape, 0)
    inside = jnp.where(row < 6, inside, 0.0)
    outside = jnp.where(row < 6, outside, 0.0)
    middle = own[...] * inside
    x_before, x_after = in_order("box", from_first[...], from_second[...])
    fields = [
        jnp.where(even, x_before, x_after) * outside,
        swap(jnp.where(even, x_after, x_before)) * outside,
        middle,
        swap(middle),
    ]
    value = corrections(4, fields, [k4[0], k4[1]], [outside, inside])
    left = coarse_remainders(4, value + [swap(value[1])], [middle], [k4[1]])[0]
    lane = iota(own.shape, 1)
    for out, here in ((e4, value[1]), (rest, left)):
        for side, folded_plane in enumerate((here, to_left(here))):
            cells = [
                jnp.where(lane == z, pltpu.roll(folded_plane, (LANES - 15 * z) % LANES, 1), 0.0)
                for z in range(8)
            ]
            while len(cells) > 1:
                cells = [a + b for a, b in zip(cells[::2], cells[1::2])]
            out[side] = cells[0][2:4, 0:8]


def exchanged(first, second, axis):
    names = ("box", "agg")
    along = names.index(axis)
    across, width = across_of(axis)
    sizes = [lax.axis_size(name) for name in names]
    route = []
    for source in range(sizes[0] * sizes[1]):
        at = list(divmod(source, sizes[1]))
        step = 1 if at[names.index(across)] // width % 2 == 0 else -1
        if 0 <= at[along] + step < sizes[along]:
            at[along] += step
        else:
            at[1 - along] += step * width
        route.append((source, at[0] * sizes[1] + at[1]))
    inverse = [(target, source) for source, target in route]
    return lax.ppermute(first, names, route), lax.ppermute(second, names, inverse)


VMEM = pl.BlockSpec(memory_space=pltpu.VMEM)
HBM = pl.BlockSpec(memory_space=pltpu.HBM)


def call(body, outs, ins, scratch=(), copies=0, flops=0, name=None):
    sems = [pltpu.SemaphoreType.DMA((copies,))] if copies else []
    return pl.pallas_call(
        body,
        out_shape=[jax.ShapeDtypeStruct(dims, F32) for dims in outs],
        in_specs=ins,
        out_specs=[VMEM] * len(outs),
        scratch_shapes=[s if not isinstance(s, tuple) else pltpu.VMEM(s, F32) for s in scratch] + sems,
        compiler_params=pltpu.CompilerParams(vmem_limit_bytes=40 * 1024 * 1024),
        cost_estimate=pl.CostEstimate(flops=flops, transcendentals=0, bytes_accessed=flops),
        name=name,
    )


def per_device(source, guess, reaction, flags):
    tile = (32, 8, LANES)
    flags, guess, source, reaction = (
        pltpu.with_memory_space_constraint(v, pltpu.HBM) for v in (flags, guess, source, reaction)
    )
    *packed, strip_up, strip_down = call(
        pack_rows,
        [tile, tile, (7, 32, LANES), (7, 32, LANES)],
        [HBM] * 4,
        scratch=[pltpu.SMEM((1, 1, flags.shape[2]), jnp.int32)] + [tile] * 6,
        copies=13,
        name="pack_rows",
    )(flags, guess, source, reaction)
    y_sides = exchanged(*packed, "agg")
    *packed, mask = call(
        pack_planes, [(7, 40, LANES)] * 2 + [(40, LANES)], [VMEM] * 6, name="pack_planes"
    )(*packed, *y_sides, strip_up, strip_down)
    x_sides = exchanged(*packed, "box")
    big = (32, 40, LANES)
    *fields, inner = call(
        fine_inner,
        [big] * 6 + [(16, 16, LANES)],
        [VMEM] * 3 + [HBM] * 3,
        scratch=[(12, 40, LANES), (16, 32, LANES)],
        copies=3,
        flops=8000000,
        name="fine_inner",
    )(mask, *y_sides, guess, source, reaction)
    coarse, edge = call(
        fine_outer,
        [(16, 16, LANES), (4, 32, LANES)],
        [VMEM] * 10,
        scratch=[(4, 40, LANES)],
        name="fine_outer",
    )(mask, *x_sides, *fields, inner)
    iterate = jnp.concatenate([edge[0:2], fields[5][2:30, 0:32], edge[2:4]], axis=0)
    y_first, y_second = exchanged(coarse, coarse, "agg")
    y_first, iterate = lax.optimization_barrier((y_first, iterate))
    y_before, y_after = in_order("agg", y_first, y_second)
    extended = jnp.concatenate([y_before, coarse, y_after], axis=1)
    x_sides = exchanged(*in_order("box", extended[16 - FAR :], extended[:FAR]), "box")
    plane = (48, LANES)
    inner = call(
        coarse_inner,
        [(2,) + plane] * 2 + [(8,) + plane] + [(3, 24, LANES)] * 2,
        [VMEM] * 3,
        scratch=[(3,) + plane] * 2,
        flops=4000000,
        name="coarse_inner",
    )(y_before, coarse, y_after)
    *owns, f4, k4 = call(
        coarse_outer,
        [(8, 16, LANES), (4, 8, LANES), (2, 8, LANES), (8, LANES), (2, 8, LANES)],
        [VMEM] * 7,
        scratch=[(7,) + plane] * 2,
        name="coarse_outer",
    )(*x_sides, *inner)
    e1, e2, e3 = call(
        unfold, [(16, 16, 64), (8, 8, 32), (4, 4, 16)], [VMEM] * 3, flops=2000000, name="unfold"
    )(*owns)
    y_first, y_second = exchanged(f4, f4, "agg")
    y_first, e1, e2, e3 = lax.optimization_barrier((y_first, e1, e2, e3))
    (last,) = call(pack_last, [(8, LANES)], [VMEM] * 3, name="pack_last")(y_first, f4, y_second)
    x_sides = exchanged(last, last, "box")
    e4, rest = call(
        last_kernel, [(2, 2, 8), (2, 2, 8)], [VMEM] * 4, name="last"
    )(last, *x_sides, k4)
    return iterate, e1, e2, e3, e4, rest


def solution(mesh):
    spec = P("box", "agg", None)
    return jax.shard_map(
        per_device, mesh=mesh, in_specs=(spec,) * 4, out_specs=(spec,) * 6, check_vma=False
    )
```

```python
import functools

import jax
import jax.numpy as jnp
from jax import lax
from jax.experimental import pallas as pl
from jax.experimental.pallas import tpu as pltpu
from jax.sharding import PartitionSpec as P

F32 = jnp.float32
LANES = 128
FAR = 14


def coefficients(level_index):
    upper_edge = 1.1 * (2.0 + 0.02 * 4.0**level_index)
    lower_edge = upper_edge / 8.0
    midpoint = (upper_edge + lower_edge) / 2.0
    half_span = (upper_edge - lower_edge) / 2.0
    sigma_value = midpoint / half_span
    rho_first = 1.0 / sigma_value
    rho_second = 1.0 / (2.0 * sigma_value - rho_first)
    return (midpoint, rho_second * rho_first, 2.0 * rho_second / half_span)


def iota(shape, dim):
    return lax.broadcasted_iota(jnp.int32, shape, dim)


def edges(axis):
    here = lax.axis_index(axis)
    before = jnp.where(here > 0, 1.0, 0.0).astype(F32)
    after = jnp.where(here < lax.axis_size(axis) - 1, 1.0, 0.0).astype(F32)
    return before, after


def blurred(planes, stride):
    sums = [a + b for a, b in zip(planes[:-1], planes[1:])]
    out = []
    for low, high in zip(sums[:-1], sums[1:]):
        total = low + high
        beside = pltpu.roll(total, 1, 0) + pltpu.roll(total, total.shape[0] - 1, 0)
        out.append(blur_z((total + total) + beside, stride))
    return out


def across_of(axis):
    return "box" if axis == "agg" else "agg"


def moves_up(axis):
    return lax.axis_index(across_of(axis)) % 2 == 0


def in_order(axis, first, second):
    up = moves_up(axis)
    return jnp.where(up, first, second), jnp.where(up, second, first)


def blur_z(values, stride):
    lane = iota(values.shape, 1)
    left = jnp.where(lane < stride, 0.0, pltpu.roll(values, stride, 1))
    right = jnp.where(lane >= LANES - stride, 0.0, pltpu.roll(values, LANES - stride, 1))
    return (values + values) + (left + right)


def pair_rows(values):
    return values + pltpu.roll(values, values.shape[0] - 1, 0)


def halved(values, stride):
    return (values + pltpu.roll(values, LANES - stride, 1)) * 0.5


def even_lanes(shape):
    return (iota(shape, len(shape) - 1) & 1) == 0


def loop(first, stop, size, body):
    count = (stop - first) // size
    if count == 1:
        body(first)
        return

    def step(i, carry):
        body(first + i * size)
        return carry

    lax.fori_loop(0, count, step, 0)


def copy_all(sems, *pairs):
    copies = [pltpu.make_async_copy(a, b, sems.at[i]) for i, (a, b) in enumerate(pairs)]
    for copy in copies:
        copy.start()
    return copies


def pack_rows(
    flags, guess, source, reaction, first, second, strip_up, strip_down,
    flag_smem, guess_lo, guess_hi, source_lo, source_hi, reaction_lo, reaction_hi, sems,
):
    lo, hi = pl.ds(0, 8), pl.ds(24, 8)
    copies = copy_all(
        sems,
        (flags, flag_smem),
        (guess.at[:, lo, :], guess_lo),
        (guess.at[:, hi, :], guess_hi),
        (source.at[:, lo, :], source_lo),
        (source.at[:, hi, :], source_hi),
        (reaction.at[:, lo, :], reaction_lo),
        (reaction.at[:, hi, :], reaction_hi),
        (guess.at[29:32], strip_up.at[0:3]),
        (source.at[30:32], strip_up.at[3:5]),
        (reaction.at[30:32], strip_up.at[5:7]),
        (guess.at[0:3], strip_down.at[0:3]),
        (source.at[0:2], strip_down.at[3:5]),
        (reaction.at[0:2], strip_down.at[5:7]),
    )
    for copy in copies[:7]:
        copy.wait()
    boxes = flags.shape[2]
    lane = iota((8, LANES), 1)
    flag = jnp.zeros((8, LANES), F32)
    for i in range(boxes):
        flag = jnp.where(lane // (LANES // boxes) == i, flag_smem[0, 0, i].astype(F32), flag)
    flag = flag[None]
    row = iota(first.shape, 1)
    up = jnp.where(
        row >= 5,
        guess_hi[...],
        jnp.where(
            row >= 3,
            pltpu.roll(source_hi[...], 5, 1),
            jnp.where(row >= 1, pltpu.roll(reaction_hi[...], 3, 1), flag),
        ),
    )
    down = jnp.where(
        row < 3,
        guess_lo[...],
        jnp.where(
            row < 5,
            pltpu.roll(source_lo[...], 3, 1),
            jnp.where(row < 7, pltpu.roll(reaction_lo[...], 5, 1), flag),
        ),
    )
    first[...], second[...] = in_order("agg", up, down)
    for copy in copies[7:]:
        copy.wait()


def halo_tiles(from_before, from_after, before, after):
    row = iota(from_before.shape, 1)
    first = row < 4
    guess = jnp.where(first, from_after * after, from_before * before)
    source = jnp.where(first, pltpu.roll(from_after, 5, 1), pltpu.roll(from_before, 3, 1))
    reaction = jnp.where(first, pltpu.roll(from_after, 3, 1), pltpu.roll(from_before, 5, 1))
    return guess, source, reaction


def flag_plane(own, lo, hi):
    tile = (8, LANES)
    halo = jnp.where(iota(tile, 0) < 4, jnp.broadcast_to(hi, tile), jnp.broadcast_to(lo, tile))
    return jnp.concatenate([jnp.broadcast_to(own, (32, LANES)), halo], axis=0)


def pack_planes(own_first, own_second, from_first, from_second, strip_up, strip_down, first, second, mask):
    before, after = edges("agg")
    own, _ = in_order("agg", own_first[0, 0:1, :], own_second[0, 0:1, :])
    from_before, from_after = in_order("agg", from_first[...], from_second[...])
    lo = from_before[0, 0:1, :] * before
    hi = from_after[0, 7:8, :] * after
    mask[...] = flag_plane(own, lo, hi)
    planes = from_before.shape[0]
    strips, tiles = [], []
    for strip, at, local in ((strip_up, planes - 4, (1, 2, 2)), (strip_down, 0, (0, 0, 0))):
        fields = halo_tiles(from_before[at : at + 4], from_after[at : at + 4], before, after)
        rows = [tile[i] for tile, start, count in zip(fields, local, (3, 2, 2)) for i in range(start, start + count)]
        row = iota(rows[0].shape, 0)
        rows[0] = jnp.where(row == 3, own, jnp.where(row == 4, lo, rows[0]))
        rows[1] = jnp.where(row == 3, hi, rows[1])
        strips.append(strip[...])
        tiles.append(rows)
    first[:, 0:32, :], second[:, 0:32, :] = in_order("box", *strips)
    for i, (up, down) in enumerate(zip(*tiles)):
        first[i, 32:40, :], second[i, 32:40, :] = in_order("box", up, down)


SHIFT = 8.0 / 7.0


def even_rows(ref, i, rows):
    return ref[i, pl.ds(0, rows, stride=2), :]


def fine_inner(
    mask_ref, from_first, from_second, guess, source, reaction,
    g, s, k, d, u, w, coarse, pairs, kpairs, sems,
):
    rows = pl.ds(0, 32)
    copies = copy_all(
        sems, (guess, g.at[:, rows, :]), (source, s.at[:, rows, :]), (reaction, k.at[:, rows, :])
    )
    before, after = edges("agg")
    theta, c1, c2 = coefficients(0)

    def assemble(x):
        at = pl.ds(x, 32)
        sides = in_order("agg", from_first[at], from_second[at])
        tiles = halo_tiles(*sides, before, after)
        g[at, 32:40, :] = tiles[0]
        s[at, 32:40, :] = tiles[1]
        k[at, 32:40, :] = tiles[2]

    loop(0, 32, 32, assemble)
    for copy in copies:
        copy.wait()

    def remainders(field, x, size):
        planes = [field[x + i] for i in range(-1, size + 1)]
        mask = mask_ref[...]
        out = []
        for i, q in enumerate(blurred(planes, 1)):
            r = mask * (s[x + i] - (k[x + i] + SHIFT) * planes[i + 1] + q * (1.0 / 56.0))
            out.append((r, planes[i + 1]))
        return out

    def first(x):
        out = remainders(g, x, 10)
        for i, (r, middle) in enumerate(out):
            step = r * (1.0 / theta)
            d[x + i] = step
            u[x + i] = middle + step

    loop(1, 31, 10, first)

    def second(x):
        out = [m + (c1 * d[x + i] + c2 * r) for i, (r, m) in enumerate(remainders(u, x, 14))]
        for i, value in enumerate(out):
            w[x + i] = value

    loop(2, 30, 14, second)

    def third(x):
        out = [r for r, _ in remainders(w, x, 24)]
        at = (x - 4) // 2
        for i in range(len(out) // 2):
            pairs[at + i] = pair_rows(out[2 * i] + out[2 * i + 1])

    loop(4, 28, 24, third)

    for i in range(16):
        kpairs[i] = pair_rows(k[2 * i, 0:32, :] + k[2 * i + 1, 0:32, :])
    even = even_lanes((16, LANES))
    for i in range(16):
        value = pltpu.roll(halved(even_rows(kpairs, i, 16), 1), 1, 1)
        if 2 <= i < 14:
            value = jnp.where(even, halved(even_rows(pairs, i - 2, 16), 1), value)
        coarse[i] = value


def fine_outer(mask_ref, from_first, from_second, g, s, k, d, u, w, inner, coarse, edge, pairs):
    xbefore, xafter = edges("box")
    x_before, x_after = in_order("box", from_first[...], from_second[...])
    mask_before, mask_after = (
        flag_plane(x[0, 35:36], x[0, 36:37], x[1, 35:36]) * edge for x, edge in ((x_before, xbefore), (x_after, xafter))
    )
    theta, c1, c2 = coefficients(0)
    new_d, new_u, new_w = {}, {}, {}

    def side(x, before, after, own):
        return before(x + 3) if x < 0 else after(x - 32) if x > 31 else own(x)

    def guess_at(x):
        return side(x, lambda i: x_before[i] * xbefore, lambda i: x_after[i] * xafter, lambda i: g[i])

    def source_at(x):
        return side(x, lambda i: x_before[i + 2], lambda i: x_after[i + 3], lambda i: s[i])

    def reaction_at(x):
        return side(x, lambda i: x_before[i + 4], lambda i: x_after[i + 5], lambda i: k[i])

    def mask_at(x):
        return side(x, lambda i: mask_before, lambda i: mask_after, lambda i: mask_ref[...])

    def remainders(field, first, size):
        planes = [field(x) for x in range(first - 1, first + size + 1)]
        out = []
        for i, q in enumerate(blurred(planes, 1)):
            x = first + i
            r = mask_at(x) * (source_at(x) - (reaction_at(x) + SHIFT) * planes[i + 1] + q * (1.0 / 56.0))
            out.append((x, r, planes[i + 1]))
        return out

    for first in (-2, 31):
        for x, r, middle in remainders(guess_at, first, 3):
            new_d[x] = r * (1.0 / theta)
            new_u[x] = middle + new_d[x]
    for first in (-1, 30):
        for x, r, middle in remainders(lambda i: new_u[i] if i in new_u else u[i], first, 3):
            step = new_d[x] if x in new_d else d[x]
            new_w[x] = middle + (c1 * step + c2 * r)
    for at, x in enumerate((0, 1, 30, 31)):
        edge[at] = new_w[x][0:32]
    for at, first in enumerate((0, 28)):
        out = [r for _, r, _ in remainders(lambda i: new_w[i] if i in new_w else w[i], first, 4)]
        pairs[2 * at] = pair_rows(out[0] + out[1])
        pairs[2 * at + 1] = pair_rows(out[2] + out[3])
    even = even_lanes((16, LANES))
    for at, x in enumerate((0, 1, 14, 15)):
        coarse[x] = jnp.where(even, halved(even_rows(pairs, at, 16), 1), inner[x])
    coarse[2:14] = inner[2:14]


def level_constants(level):
    theta, c1, c2 = coefficients(level)
    return (1.0 + c1) / theta + c2, c2 / theta


def masks_of(rows, lo, hi):
    before, after = edges("agg")
    xbefore, xafter = edges("box")
    shape = (rows, LANES)
    row = iota(shape, 0)
    inside = jnp.where(row < lo, before, jnp.where(row >= hi, after, 1.0))
    return inside * jnp.where(even_lanes(shape), xbefore, xafter), inside


def corrections(level, planes, reactions, masks):
    alpha, beta = level_constants(level)
    return [
        m * (f * (alpha - beta * (k + SHIFT)) + q * (beta / 56.0))
        for f, k, m, q in zip(planes[1:-1], reactions, masks, blurred(planes, 2**level))
    ]


def coarse_remainders(level, planes, fields, reactions):
    return [
        f - (k + SHIFT) * e + q * (1.0 / 56.0)
        for f, k, e, q in zip(fields, reactions, planes[1:-1], blurred(planes, 2**level))
    ]


def to_left(values):
    return pltpu.roll(values, LANES - 1, 1)


def to_right(values):
    return pltpu.roll(values, 1, 1)


def swap(values):
    return jnp.where(even_lanes(values.shape), to_left(values), to_right(values))


def folded(lo, hi):
    even = even_lanes(lo.shape)
    return jnp.where(even, lo, to_right(hi)), jnp.where(even, to_left(lo), hi)


def coarse_inner(y_before, own, y_after, f, k, e, f2, k2, pairs, kpairs):
    _, inside = masks_of(48, 16, 32)
    fields, reactions = [], []
    for j in range(8):
        lo = jnp.concatenate([y_before[j], own[j], y_after[j]], axis=0)
        hi = jnp.concatenate([y_before[15 - j], own[15 - j], y_after[15 - j]], axis=0)
        field, reaction = folded(lo, hi)
        fields.append(field * inside)
        reactions.append(reaction)
    for j in range(2):
        f[j], k[j] = fields[j], reactions[j]
    for j in range(3):
        kpairs[j] = pair_rows(reactions[2 * j + 2] + reactions[2 * j + 3])
    value = corrections(1, fields + [swap(fields[7])], reactions[1:], [inside] * 7)
    for j in range(7):
        e[j + 1] = value[j]
    rest = coarse_remainders(1, value + [swap(value[6])], fields[2:], reactions[2:])
    for j in range(3):
        pairs[j] = pair_rows(rest[2 * j] + rest[2 * j + 1])
    _, inside = masks_of(24, 8, 16)
    for j in range(3):
        f2[j] = halved(even_rows(pairs, j, 24), 2) * inside
        k2[j] = halved(even_rows(kpairs, j, 24), 2)


def coarse_outer(
    from_first, from_second, f_in, k_in, e_in, f2_in, k2_in, own1, own2, own3, f4, k4,
    pairs, kpairs,
):
    outside, inside = masks_of(48, 16, 32)
    fields, reactions = [], []
    x_before, x_after = in_order("box", from_first[...], from_second[...])
    for j in range(FAR):
        field, reaction = folded(x_before[j], x_after[FAR - 1 - j])
        fields.append(field * outside)
        reactions.append(reaction)
    for j in range(2):
        fields.append(f_in[j])
        reactions.append(k_in[j])
    for j in range(7):
        kpairs[j] = pair_rows(reactions[2 * j + 2] + reactions[2 * j + 3])
    value = corrections(1, fields, reactions[1:15], [outside] * 13 + [inside])
    own1[0] = value[13][16:32]
    for j in range(1, 8):
        own1[j] = e_in[j, 16:32, :]
    rest = coarse_remainders(1, value + [e_in[1], e_in[2]], fields[2:], reactions[2:])
    for j in range(7):
        pairs[j] = pair_rows(rest[2 * j] + rest[2 * j + 1])
    outside, inside = masks_of(24, 8, 16)
    fields = [halved(even_rows(pairs, j, 24), 2) * (outside if j < 6 else inside) for j in range(7)]
    fields += [f2_in[j] for j in range(3)]
    reactions = [halved(even_rows(kpairs, j, 24), 2) for j in range(7)] + [k2_in[j] for j in range(3)]
    for p in range(4):
        kpairs[p, 0:24, :] = pair_rows(reactions[2 * p + 2] + reactions[2 * p + 3])
    value = corrections(2, fields + [swap(fields[9])], reactions[1:], [outside] * 5 + [inside] * 4)
    for j in range(4):
        own2[j] = value[5 + j][8:16]
    rest = coarse_remainders(2, value + [swap(value[8])], fields[2:], reactions[2:])
    for p in range(4):
        pairs[p, 0:24, :] = pair_rows(rest[2 * p] + rest[2 * p + 1])
    outside, inside = masks_of(16, 4, 8)
    fields = [halved(even_rows(pairs, j, 16), 4) * (outside if j < 2 else inside) for j in range(4)]
    reactions = [halved(even_rows(kpairs, j, 16), 4) for j in range(4)]
    for p in range(2):
        kpairs[p, 0:16, :] = pair_rows(reactions[2 * p] + reactions[2 * p + 1])
    value = corrections(3, fields + [swap(fields[3])], reactions[1:], [outside, inside, inside])
    for j in range(2):
        own3[j] = value[1 + j][0:8]
    rest = coarse_remainders(3, value + [swap(value[2])], fields[2:], reactions[2:])
    pairs[0, 0:16, :] = pair_rows(rest[0] + rest[1])
    f4[...] = halved(even_rows(pairs, 0, 8), 8)
    for p in range(2):
        k4[p] = halved(even_rows(kpairs, p, 8), 8)


def unfold(own1, own2, own3, e1, e2, e3):
    rows = (slice(0, 16), slice(0, 8), slice(4, 8))
    for level, own, out, part in zip((1, 2, 3), (own1, own2, own3), (e1, e2, e3), rows):
        planes, _, lanes = out.shape
        source = iota((LANES, LANES), 0)
        target = iota((LANES, LANES), 1)
        hit = source == ((target & 63) << level) + (target >> 6)
        values = own[...].reshape(-1, LANES)
        values = jnp.dot(
            values,
            jnp.where(hit, 1.0, 0.0).astype(F32),
            precision=lax.Precision.HIGHEST,
            preferred_element_type=F32,
        ).reshape(own.shape)
        for j in range(planes // 2):
            value = values[j]
            out[j] = value[part, 0:lanes]
            out[planes - 1 - j] = pltpu.roll(value, 64, 1)[part, 0:lanes]


def pack_last(from_first, own, from_second, out):
    before, after = edges("agg")
    row = iota(own.shape, 0)
    y_before, y_after = in_order("agg", from_first[...], from_second[...])
    lo = pltpu.roll(y_before, 6, 0) * before
    hi = pltpu.roll(y_after, 2, 0) * after
    out[...] = jnp.where(row < 2, lo, jnp.where(row < 4, own[...], jnp.where(row < 6, hi, 0.0)))


def last_kernel(own, from_first, from_second, k4, e4, rest):
    outside, inside = masks_of(8, 2, 4)
    even = even_lanes(own.shape)
    row = iota(own.shape, 0)
    inside = jnp.where(row < 6, inside, 0.0)
    outside = jnp.where(row < 6, outside, 0.0)
    middle = own[...] * inside
    x_before, x_after = in_order("box", from_first[...], from_second[...])
    fields = [
        jnp.where(even, x_before, x_after) * outside,
        swap(jnp.where(even, x_after, x_before)) * outside,
        middle,
        swap(middle),
    ]
    value = corrections(4, fields, [k4[0], k4[1]], [outside, inside])
    left = coarse_remainders(4, value + [swap(value[1])], [middle], [k4[1]])[0]
    lane = iota(own.shape, 1)
    for out, here in ((e4, value[1]), (rest, left)):
        for side, folded_plane in enumerate((here, to_left(here))):
            cells = [
                jnp.where(lane == z, pltpu.roll(folded_plane, (LANES - 15 * z) % LANES, 1), 0.0)
                for z in range(8)
            ]
            while len(cells) > 1:
                cells = [a + b for a, b in zip(cells[::2], cells[1::2])]
            out[side] = cells[0][2:4, 0:8]


def exchanged(first, second, axis):
    names = ("box", "agg")
    along = names.index(axis)
    sizes = [lax.axis_size(name) for name in names]
    route = []
    for source in range(sizes[0] * sizes[1]):
        at = list(divmod(source, sizes[1]))
        step = 1 if at[1 - along] % 2 == 0 else -1
        if 0 <= at[along] + step < sizes[along]:
            at[along] += step
        else:
            at[1 - along] += step
        route.append((source, at[0] * sizes[1] + at[1]))
    inverse = [(target, source) for source, target in route]
    return lax.ppermute(first, names, route), lax.ppermute(second, names, inverse)


VMEM = pl.BlockSpec(memory_space=pltpu.VMEM)
HBM = pl.BlockSpec(memory_space=pltpu.HBM)


def call(body, outs, ins, scratch=(), copies=0, flops=0, name=None):
    sems = [pltpu.SemaphoreType.DMA((copies,))] if copies else []
    return pl.pallas_call(
        body,
        out_shape=[jax.ShapeDtypeStruct(dims, F32) for dims in outs],
        in_specs=ins,
        out_specs=[VMEM] * len(outs),
        scratch_shapes=[s if not isinstance(s, tuple) else pltpu.VMEM(s, F32) for s in scratch] + sems,
        compiler_params=pltpu.CompilerParams(vmem_limit_bytes=40 * 1024 * 1024),
        cost_estimate=pl.CostEstimate(flops=flops, transcendentals=0, bytes_accessed=flops),
        name=name,
    )


def per_device(source, guess, reaction, flags):
    tile = (32, 8, LANES)
    flags, guess, source, reaction = (
        pltpu.with_memory_space_constraint(v, pltpu.HBM) for v in (flags, guess, source, reaction)
    )
    *packed, strip_up, strip_down = call(
        pack_rows,
        [tile, tile, (7, 32, LANES), (7, 32, LANES)],
        [HBM] * 4,
        scratch=[pltpu.SMEM((1, 1, flags.shape[2]), jnp.int32)] + [tile] * 6,
        copies=13,
        name="pack_rows",
    )(flags, guess, source, reaction)
    y_sides = exchanged(*packed, "agg")
    *packed, mask = call(
        pack_planes, [(7, 40, LANES)] * 2 + [(40, LANES)], [VMEM] * 6, name="pack_planes"
    )(*packed, *y_sides, strip_up, strip_down)
    x_sides = exchanged(*packed, "box")
    big = (32, 40, LANES)
    *fields, inner = call(
        fine_inner,
        [big] * 6 + [(16, 16, LANES)],
        [VMEM] * 3 + [HBM] * 3,
        scratch=[(12, 40, LANES), (16, 32, LANES)],
        copies=3,
        flops=8000000,
        name="fine_inner",
    )(mask, *y_sides, guess, source, reaction)
    coarse, edge = call(
        fine_outer,
        [(16, 16, LANES), (4, 32, LANES)],
        [VMEM] * 10,
        scratch=[(4, 40, LANES)],
        name="fine_outer",
    )(mask, *x_sides, *fields, inner)
    iterate = jnp.concatenate([edge[0:2], fields[5][2:30, 0:32], edge[2:4]], axis=0)
    y_first, y_second = exchanged(coarse, coarse, "agg")
    y_first, iterate = lax.optimization_barrier((y_first, iterate))
    y_before, y_after = in_order("agg", y_first, y_second)
    extended = jnp.concatenate([y_before, coarse, y_after], axis=1)
    x_sides = exchanged(*in_order("box", extended[16 - FAR :], extended[:FAR]), "box")
    plane = (48, LANES)
    inner = call(
        coarse_inner,
        [(2,) + plane] * 2 + [(8,) + plane] + [(3, 24, LANES)] * 2,
        [VMEM] * 3,
        scratch=[(3,) + plane] * 2,
        flops=4000000,
        name="coarse_inner",
    )(y_before, coarse, y_after)
    *owns, f4, k4 = call(
        coarse_outer,
        [(8, 16, LANES), (4, 8, LANES), (2, 8, LANES), (8, LANES), (2, 8, LANES)],
        [VMEM] * 7,
        scratch=[(7,) + plane] * 2,
        name="coarse_outer",
    )(*x_sides, *inner)
    e1, e2, e3 = call(
        unfold, [(16, 16, 64), (8, 8, 32), (4, 4, 16)], [VMEM] * 3, flops=2000000, name="unfold"
    )(*owns)
    y_first, y_second = exchanged(f4, f4, "agg")
    y_first, e1, e2, e3 = lax.optimization_barrier((y_first, e1, e2, e3))
    (last,) = call(pack_last, [(8, LANES)], [VMEM] * 3, name="pack_last")(y_first, f4, y_second)
    x_sides = exchanged(last, last, "box")
    e4, rest = call(
        last_kernel, [(2, 2, 8), (2, 2, 8)], [VMEM] * 4, name="last"
    )(last, *x_sides, k4)
    return iterate, e1, e2, e3, e4, rest


def solution(mesh):
    spec = P("box", "agg", None)
    return jax.shard_map(
        per_device, mesh=mesh, in_specs=(spec,) * 4, out_specs=(spec,) * 6, check_vma=False
    )
```

```python
import functools

import jax
import jax.numpy as jnp
from jax import lax
from jax.experimental import pallas as pl
from jax.experimental.pallas import tpu as pltpu
from jax.sharding import PartitionSpec as P

F32 = jnp.float32
LANES = 128
FAR = 14


def coefficients(level_index):
    upper_edge = 1.1 * (2.0 + 0.02 * 4.0**level_index)
    lower_edge = upper_edge / 8.0
    midpoint = (upper_edge + lower_edge) / 2.0
    half_span = (upper_edge - lower_edge) / 2.0
    sigma_value = midpoint / half_span
    rho_first = 1.0 / sigma_value
    rho_second = 1.0 / (2.0 * sigma_value - rho_first)
    return (midpoint, rho_second * rho_first, 2.0 * rho_second / half_span)


def iota(shape, dim):
    return lax.broadcasted_iota(jnp.int32, shape, dim)


def edges(axis):
    here = lax.axis_index(axis)
    before = jnp.where(here > 0, 1.0, 0.0).astype(F32)
    after = jnp.where(here < lax.axis_size(axis) - 1, 1.0, 0.0).astype(F32)
    return before, after


def blurred(planes, stride):
    sums = [a + b for a, b in zip(planes[:-1], planes[1:])]
    out = []
    for low, high in zip(sums[:-1], sums[1:]):
        total = low + high
        beside = pltpu.roll(total, 1, 0) + pltpu.roll(total, total.shape[0] - 1, 0)
        out.append(blur_z((total + total) + beside, stride))
    return out


def across_of(axis):
    return "box" if axis == "agg" else "agg"


def moves_up(axis):
    return lax.axis_index(across_of(axis)) % 2 == 0


def in_order(axis, first, second):
    up = moves_up(axis)
    return jnp.where(up, first, second), jnp.where(up, second, first)


def blur_z(values, stride):
    lane = iota(values.shape, 1)
    left = jnp.where(lane < stride, 0.0, pltpu.roll(values, stride, 1))
    right = jnp.where(lane >= LANES - stride, 0.0, pltpu.roll(values, LANES - stride, 1))
    return (values + values) + (left + right)


def pair_rows(values):
    return values + pltpu.roll(values, values.shape[0] - 1, 0)


def halved(values, stride):
    return (values + pltpu.roll(values, LANES - stride, 1)) * 0.5


def even_lanes(shape):
    return (iota(shape, len(shape) - 1) & 1) == 0


def loop(first, stop, size, body):
    count = (stop - first) // size
    if count == 1:
        body(first)
        return

    def step(i, carry):
        body(first + i * size)
        return carry

    lax.fori_loop(0, count, step, 0)


def copy_all(sems, *pairs):
    copies = [pltpu.make_async_copy(a, b, sems.at[i]) for i, (a, b) in enumerate(pairs)]
    for copy in copies:
        copy.start()
    return copies


def pack_rows(
    flags, guess, source, reaction, first, second,
    flag_smem, guess_lo, guess_hi, source_lo, source_hi, reaction_lo, reaction_hi, sems,
):
    lo, hi = pl.ds(0, 8), pl.ds(24, 8)
    copies = copy_all(
        sems,
        (flags, flag_smem),
        (guess.at[:, lo, :], guess_lo),
        (guess.at[:, hi, :], guess_hi),
        (source.at[:, lo, :], source_lo),
        (source.at[:, hi, :], source_hi),
        (reaction.at[:, lo, :], reaction_lo),
        (reaction.at[:, hi, :], reaction_hi),
    )
    for copy in copies:
        copy.wait()
    boxes = flags.shape[2]
    lane = iota((8, LANES), 1)
    flag = jnp.zeros((8, LANES), F32)
    for i in range(boxes):
        flag = jnp.where(lane // (LANES // boxes) == i, flag_smem[0, 0, i].astype(F32), flag)
    flag = flag[None]
    row = iota(first.shape, 1)
    up = jnp.where(
        row >= 5,
        guess_hi[...],
        jnp.where(
            row >= 3,
            pltpu.roll(source_hi[...], 5, 1),
            jnp.where(row >= 1, pltpu.roll(reaction_hi[...], 3, 1), flag),
        ),
    )
    down = jnp.where(
        row < 3,
        guess_lo[...],
        jnp.where(
            row < 5,
            pltpu.roll(source_lo[...], 3, 1),
            jnp.where(row < 7, pltpu.roll(reaction_lo[...], 5, 1), flag),
        ),
    )
    first[...], second[...] = in_order("agg", up, down)


def load_strips(after, guess, source, reaction, strip_up, strip_down, sems):
    copies = copy_all(
        sems,
        (guess.at[29:32], strip_up.at[0:3]),
        (source.at[30:32], strip_up.at[3:5]),
        (reaction.at[30:32], strip_up.at[5:7]),
        (guess.at[0:3], strip_down.at[0:3]),
        (source.at[0:2], strip_down.at[3:5]),
        (reaction.at[0:2], strip_down.at[5:7]),
    )
    for copy in copies:
        copy.wait()


def halo_tiles(from_before, from_after, before, after):
    row = iota(from_before.shape, 1)
    first = row < 4
    guess = jnp.where(first, from_after * after, from_before * before)
    source = jnp.where(first, pltpu.roll(from_after, 5, 1), pltpu.roll(from_before, 3, 1))
    reaction = jnp.where(first, pltpu.roll(from_after, 3, 1), pltpu.roll(from_before, 5, 1))
    return guess, source, reaction


def flag_plane(own, lo, hi):
    tile = (8, LANES)
    halo = jnp.where(iota(tile, 0) < 4, jnp.broadcast_to(hi, tile), jnp.broadcast_to(lo, tile))
    return jnp.concatenate([jnp.broadcast_to(own, (32, LANES)), halo], axis=0)


def pack_planes(own_first, own_second, from_first, from_second, strip_up, strip_down, first, second, mask):
    before, after = edges("agg")
    own, _ = in_order("agg", own_first[0, 0:1, :], own_second[0, 0:1, :])
    from_before, from_after = in_order("agg", from_first[...], from_second[...])
    lo = from_before[0, 0:1, :] * before
    hi = from_after[0, 7:8, :] * after
    mask[...] = flag_plane(own, lo, hi)
    planes = from_before.shape[0]
    strips, tiles = [], []
    for strip, at, local in ((strip_up, planes - 4, (1, 2, 2)), (strip_down, 0, (0, 0, 0))):
        fields = halo_tiles(from_before[at : at + 4], from_after[at : at + 4], before, after)
        rows = [tile[i] for tile, start, count in zip(fields, local, (3, 2, 2)) for i in range(start, start + count)]
        row = iota(rows[0].shape, 0)
        rows[0] = jnp.where(row == 3, own, jnp.where(row == 4, lo, rows[0]))
        rows[1] = jnp.where(row == 3, hi, rows[1])
        strips.append(strip[...])
        tiles.append(rows)
    first[:, 0:32, :], second[:, 0:32, :] = in_order("box", *strips)
    for i, (up, down) in enumerate(zip(*tiles)):
        first[i, 32:40, :], second[i, 32:40, :] = in_order("box", up, down)


SHIFT = 8.0 / 7.0


def even_rows(ref, i, rows):
    return ref[i, pl.ds(0, rows, stride=2), :]


def fine_inner(
    mask_ref, from_first, from_second, guess, source, reaction,
    g, s, k, d, u, w, coarse, pairs, kpairs, sems,
):
    rows = pl.ds(0, 32)
    copies = copy_all(
        sems, (guess, g.at[:, rows, :]), (source, s.at[:, rows, :]), (reaction, k.at[:, rows, :])
    )
    before, after = edges("agg")
    theta, c1, c2 = coefficients(0)

    def assemble(x):
        at = pl.ds(x, 32)
        sides = in_order("agg", from_first[at], from_second[at])
        tiles = halo_tiles(*sides, before, after)
        g[at, 32:40, :] = tiles[0]
        s[at, 32:40, :] = tiles[1]
        k[at, 32:40, :] = tiles[2]

    loop(0, 32, 32, assemble)
    for copy in copies:
        copy.wait()

    def remainders(field, x, size):
        planes = [field[x + i] for i in range(-1, size + 1)]
        mask = mask_ref[...]
        out = []
        for i, q in enumerate(blurred(planes, 1)):
            r = mask * (s[x + i] - (k[x + i] + SHIFT) * planes[i + 1] + q * (1.0 / 56.0))
            out.append((r, planes[i + 1]))
        return out

    def first(x):
        out = remainders(g, x, 10)
        for i, (r, middle) in enumerate(out):
            step = r * (1.0 / theta)
            d[x + i] = step
            u[x + i] = middle + step

    loop(1, 31, 10, first)

    def second(x):
        out = [m + (c1 * d[x + i] + c2 * r) for i, (r, m) in enumerate(remainders(u, x, 14))]
        for i, value in enumerate(out):
            w[x + i] = value

    loop(2, 30, 14, second)

    def third(x):
        out = [r for r, _ in remainders(w, x, 24)]
        at = (x - 4) // 2
        for i in range(len(out) // 2):
            pairs[at + i] = pair_rows(out[2 * i] + out[2 * i + 1])

    loop(4, 28, 24, third)

    for i in range(16):
        kpairs[i] = pair_rows(k[2 * i, 0:32, :] + k[2 * i + 1, 0:32, :])
    even = even_lanes((16, LANES))
    for i in range(16):
        value = pltpu.roll(halved(even_rows(kpairs, i, 16), 1), 1, 1)
        if 2 <= i < 14:
            value = jnp.where(even, halved(even_rows(pairs, i - 2, 16), 1), value)
        coarse[i] = value


def fine_outer(mask_ref, from_first, from_second, g, s, k, d, u, w, inner, coarse, edge, pairs):
    xbefore, xafter = edges("box")
    x_before, x_after = in_order("box", from_first[...], from_second[...])
    mask_before, mask_after = (
        flag_plane(x[0, 35:36], x[0, 36:37], x[1, 35:36]) * edge for x, edge in ((x_before, xbefore), (x_after, xafter))
    )
    theta, c1, c2 = coefficients(0)
    new_d, new_u, new_w = {}, {}, {}

    def side(x, before, after, own):
        return before(x + 3) if x < 0 else after(x - 32) if x > 31 else own(x)

    def guess_at(x):
        return side(x, lambda i: x_before[i] * xbefore, lambda i: x_after[i] * xafter, lambda i: g[i])

    def source_at(x):
        return side(x, lambda i: x_before[i + 2], lambda i: x_after[i + 3], lambda i: s[i])

    def reaction_at(x):
        return side(x, lambda i: x_before[i + 4], lambda i: x_after[i + 5], lambda i: k[i])

    def mask_at(x):
        return side(x, lambda i: mask_before, lambda i: mask_after, lambda i: mask_ref[...])

    def remainders(field, first, size):
        planes = [field(x) for x in range(first - 1, first + size + 1)]
        out = []
        for i, q in enumerate(blurred(planes, 1)):
            x = first + i
            r = mask_at(x) * (source_at(x) - (reaction_at(x) + SHIFT) * planes[i + 1] + q * (1.0 / 56.0))
            out.append((x, r, planes[i + 1]))
        return out

    for first in (-2, 31):
        for x, r, middle in remainders(guess_at, first, 3):
            new_d[x] = r * (1.0 / theta)
            new_u[x] = middle + new_d[x]
    for first in (-1, 30):
        for x, r, middle in remainders(lambda i: new_u[i] if i in new_u else u[i], first, 3):
            step = new_d[x] if x in new_d else d[x]
            new_w[x] = middle + (c1 * step + c2 * r)
    for at, x in enumerate((0, 1, 30, 31)):
        edge[at] = new_w[x][0:32]
    for at, first in enumerate((0, 28)):
        out = [r for _, r, _ in remainders(lambda i: new_w[i] if i in new_w else w[i], first, 4)]
        pairs[2 * at] = pair_rows(out[0] + out[1])
        pairs[2 * at + 1] = pair_rows(out[2] + out[3])
    even = even_lanes((16, LANES))
    for at, x in enumerate((0, 1, 14, 15)):
        coarse[x] = jnp.where(even, halved(even_rows(pairs, at, 16), 1), inner[x])
    coarse[2:14] = inner[2:14]


def level_constants(level):
    theta, c1, c2 = coefficients(level)
    return (1.0 + c1) / theta + c2, c2 / theta


def masks_of(rows, lo, hi):
    before, after = edges("agg")
    xbefore, xafter = edges("box")
    shape = (rows, LANES)
    row = iota(shape, 0)
    inside = jnp.where(row < lo, before, jnp.where(row >= hi, after, 1.0))
    return inside * jnp.where(even_lanes(shape), xbefore, xafter), inside


def corrections(level, planes, reactions, masks):
    alpha, beta = level_constants(level)
    return [
        m * (f * (alpha - beta * (k + SHIFT)) + q * (beta / 56.0))
        for f, k, m, q in zip(planes[1:-1], reactions, masks, blurred(planes, 2**level))
    ]


def coarse_remainders(level, planes, fields, reactions):
    return [
        f - (k + SHIFT) * e + q * (1.0 / 56.0)
        for f, k, e, q in zip(fields, reactions, planes[1:-1], blurred(planes, 2**level))
    ]


def to_left(values):
    return pltpu.roll(values, LANES - 1, 1)


def to_right(values):
    return pltpu.roll(values, 1, 1)


def swap(values):
    return jnp.where(even_lanes(values.shape), to_left(values), to_right(values))


def folded(lo, hi):
    even = even_lanes(lo.shape)
    return jnp.where(even, lo, to_right(hi)), jnp.where(even, to_left(lo), hi)


def coarse_inner(y_before, own, y_after, f, k, e, f2, k2, pairs, kpairs):
    _, inside = masks_of(48, 16, 32)
    fields, reactions = [], []
    for j in range(8):
        lo = jnp.concatenate([y_before[j], own[j], y_after[j]], axis=0)
        hi = jnp.concatenate([y_before[15 - j], own[15 - j], y_after[15 - j]], axis=0)
        field, reaction = folded(lo, hi)
        fields.append(field * inside)
        reactions.append(reaction)
    for j in range(2):
        f[j], k[j] = fields[j], reactions[j]
    for j in range(3):
        kpairs[j] = pair_rows(reactions[2 * j + 2] + reactions[2 * j + 3])
    value = corrections(1, fields + [swap(fields[7])], reactions[1:], [inside] * 7)
    for j in range(7):
        e[j + 1] = value[j]
    rest = coarse_remainders(1, value + [swap(value[6])], fields[2:], reactions[2:])
    for j in range(3):
        pairs[j] = pair_rows(rest[2 * j] + rest[2 * j + 1])
    _, inside = masks_of(24, 8, 16)
    for j in range(3):
        f2[j] = halved(even_rows(pairs, j, 24), 2) * inside
        k2[j] = halved(even_rows(kpairs, j, 24), 2)


def coarse_outer(
    from_first, from_second, f_in, k_in, e_in, f2_in, k2_in, own1, own2, own3, f4, k4,
    pairs, kpairs,
):
    outside, inside = masks_of(48, 16, 32)
    fields, reactions = [], []
    x_before, x_after = in_order("box", from_first[...], from_second[...])
    for j in range(FAR):
        field, reaction = folded(x_before[j], x_after[FAR - 1 - j])
        fields.append(field * outside)
        reactions.append(reaction)
    for j in range(2):
        fields.append(f_in[j])
        reactions.append(k_in[j])
    for j in range(7):
        kpairs[j] = pair_rows(reactions[2 * j + 2] + reactions[2 * j + 3])
    value = corrections(1, fields, reactions[1:15], [outside] * 13 + [inside])
    own1[0] = value[13][16:32]
    for j in range(1, 8):
        own1[j] = e_in[j, 16:32, :]
    rest = coarse_remainders(1, value + [e_in[1], e_in[2]], fields[2:], reactions[2:])
    for j in range(7):
        pairs[j] = pair_rows(rest[2 * j] + rest[2 * j + 1])
    outside, inside = masks_of(24, 8, 16)
    fields = [halved(even_rows(pairs, j, 24), 2) * (outside if j < 6 else inside) for j in range(7)]
    fields += [f2_in[j] for j in range(3)]
    reactions = [halved(even_rows(kpairs, j, 24), 2) for j in range(7)] + [k2_in[j] for j in range(3)]
    for p in range(4):
        kpairs[p, 0:24, :] = pair_rows(reactions[2 * p + 2] + reactions[2 * p + 3])
    value = corrections(2, fields + [swap(fields[9])], reactions[1:], [outside] * 5 + [inside] * 4)
    for j in range(4):
        own2[j] = value[5 + j][8:16]
    rest = coarse_remainders(2, value + [swap(value[8])], fields[2:], reactions[2:])
    for p in range(4):
        pairs[p, 0:24, :] = pair_rows(rest[2 * p] + rest[2 * p + 1])
    outside, inside = masks_of(16, 4, 8)
    fields = [halved(even_rows(pairs, j, 16), 4) * (outside if j < 2 else inside) for j in range(4)]
    reactions = [halved(even_rows(kpairs, j, 16), 4) for j in range(4)]
    for p in range(2):
        kpairs[p, 0:16, :] = pair_rows(reactions[2 * p] + reactions[2 * p + 1])
    value = corrections(3, fields + [swap(fields[3])], reactions[1:], [outside, inside, inside])
    for j in range(2):
        own3[j] = value[1 + j][0:8]
    rest = coarse_remainders(3, value + [swap(value[2])], fields[2:], reactions[2:])
    pairs[0, 0:16, :] = pair_rows(rest[0] + rest[1])
    f4[...] = halved(even_rows(pairs, 0, 8), 8)
    for p in range(2):
        k4[p] = halved(even_rows(kpairs, p, 8), 8)


def unfold(own1, own2, own3, e1, e2, e3):
    rows = (slice(0, 16), slice(0, 8), slice(4, 8))
    for level, own, out, part in zip((1, 2, 3), (own1, own2, own3), (e1, e2, e3), rows):
        planes, _, lanes = out.shape
        source = iota((LANES, LANES), 0)
        target = iota((LANES, LANES), 1)
        hit = source == ((target & 63) << level) + (target >> 6)
        values = own[...].reshape(-1, LANES)
        values = jnp.dot(
            values,
            jnp.where(hit, 1.0, 0.0).astype(F32),
            precision=lax.Precision.HIGHEST,
            preferred_element_type=F32,
        ).reshape(own.shape)
        for j in range(planes // 2):
            value = values[j]
            out[j] = value[part, 0:lanes]
            out[planes - 1 - j] = pltpu.roll(value, 64, 1)[part, 0:lanes]


def pack_last(from_first, own, from_second, out):
    before, after = edges("agg")
    row = iota(own.shape, 0)
    y_before, y_after = in_order("agg", from_first[...], from_second[...])
    lo = pltpu.roll(y_before, 6, 0) * before
    hi = pltpu.roll(y_after, 2, 0) * after
    out[...] = jnp.where(row < 2, lo, jnp.where(row < 4, own[...], jnp.where(row < 6, hi, 0.0)))


def last_kernel(own, from_first, from_second, k4, e4, rest):
    outside, inside = masks_of(8, 2, 4)
    even = even_lanes(own.shape)
    row = iota(own.shape, 0)
    inside = jnp.where(row < 6, inside, 0.0)
    outside = jnp.where(row < 6, outside, 0.0)
    middle = own[...] * inside
    x_before, x_after = in_order("box", from_first[...], from_second[...])
    fields = [
        jnp.where(even, x_before, x_after) * outside,
        swap(jnp.where(even, x_after, x_before)) * outside,
        middle,
        swap(middle),
    ]
    value = corrections(4, fields, [k4[0], k4[1]], [outside, inside])
    left = coarse_remainders(4, value + [swap(value[1])], [middle], [k4[1]])[0]
    lane = iota(own.shape, 1)
    for out, here in ((e4, value[1]), (rest, left)):
        for side, folded_plane in enumerate((here, to_left(here))):
            cells = [
                jnp.where(lane == z, pltpu.roll(folded_plane, (LANES - 15 * z) % LANES, 1), 0.0)
                for z in range(8)
            ]
            while len(cells) > 1:
                cells = [a + b for a, b in zip(cells[::2], cells[1::2])]
            out[side] = cells[0][2:4, 0:8]


def exchanged(first, second, axis):
    names = ("box", "agg")
    along = names.index(axis)
    sizes = [lax.axis_size(name) for name in names]
    route = []
    for source in range(sizes[0] * sizes[1]):
        at = list(divmod(source, sizes[1]))
        step = 1 if at[1 - along] % 2 == 0 else -1
        if 0 <= at[along] + step < sizes[along]:
            at[along] += step
        else:
            at[1 - along] += step
        route.append((source, at[0] * sizes[1] + at[1]))
    inverse = [(target, source) for source, target in route]
    return lax.ppermute(first, names, route), lax.ppermute(second, names, inverse)


VMEM = pl.BlockSpec(memory_space=pltpu.VMEM)
HBM = pl.BlockSpec(memory_space=pltpu.HBM)


def call(body, outs, ins, scratch=(), copies=0, flops=0, name=None):
    sems = [pltpu.SemaphoreType.DMA((copies,))] if copies else []
    return pl.pallas_call(
        body,
        out_shape=[jax.ShapeDtypeStruct(dims, F32) for dims in outs],
        in_specs=ins,
        out_specs=[VMEM] * len(outs),
        scratch_shapes=[s if not isinstance(s, tuple) else pltpu.VMEM(s, F32) for s in scratch] + sems,
        compiler_params=pltpu.CompilerParams(vmem_limit_bytes=40 * 1024 * 1024),
        cost_estimate=pl.CostEstimate(flops=flops, transcendentals=0, bytes_accessed=flops),
        name=name,
    )


def per_device(source, guess, reaction, flags):
    tile = (32, 8, LANES)
    flags, guess, source, reaction = (
        pltpu.with_memory_space_constraint(v, pltpu.HBM) for v in (flags, guess, source, reaction)
    )
    packed = call(
        pack_rows,
        [tile, tile],
        [HBM] * 4,
        scratch=[pltpu.SMEM((1, 1, flags.shape[2]), jnp.int32)] + [tile] * 6,
        copies=7,
        name="pack_rows",
    )(flags, guess, source, reaction)
    strip_up, strip_down = call(
        load_strips, [(7, 32, LANES)] * 2, [VMEM] + [HBM] * 3, copies=6, name="load_strips"
    )(packed[0], guess, source, reaction)
    y_sides = exchanged(*packed, "agg")
    *packed, mask = call(
        pack_planes, [(7, 40, LANES)] * 2 + [(40, LANES)], [VMEM] * 6, name="pack_planes"
    )(*packed, *y_sides, strip_up, strip_down)
    x_sides = exchanged(*packed, "box")
    big = (32, 40, LANES)
    *fields, inner = call(
        fine_inner,
        [big] * 6 + [(16, 16, LANES)],
        [VMEM] * 3 + [HBM] * 3,
        scratch=[(12, 40, LANES), (16, 32, LANES)],
        copies=3,
        flops=8000000,
        name="fine_inner",
    )(mask, *y_sides, guess, source, reaction)
    coarse, edge = call(
        fine_outer,
        [(16, 16, LANES), (4, 32, LANES)],
        [VMEM] * 10,
        scratch=[(4, 40, LANES)],
        name="fine_outer",
    )(mask, *x_sides, *fields, inner)
    iterate = jnp.concatenate([edge[0:2], fields[5][2:30, 0:32], edge[2:4]], axis=0)
    y_first, y_second = exchanged(coarse, coarse, "agg")
    y_first, iterate = lax.optimization_barrier((y_first, iterate))
    y_before, y_after = in_order("agg", y_first, y_second)
    extended = jnp.concatenate([y_before, coarse, y_after], axis=1)
    x_sides = exchanged(*in_order("box", extended[16 - FAR :], extended[:FAR]), "box")
    plane = (48, LANES)
    inner = call(
        coarse_inner,
        [(2,) + plane] * 2 + [(8,) + plane] + [(3, 24, LANES)] * 2,
        [VMEM] * 3,
        scratch=[(3,) + plane] * 2,
        flops=4000000,
        name="coarse_inner",
    )(y_before, coarse, y_after)
    *owns, f4, k4 = call(
        coarse_outer,
        [(8, 16, LANES), (4, 8, LANES), (2, 8, LANES), (8, LANES), (2, 8, LANES)],
        [VMEM] * 7,
        scratch=[(7,) + plane] * 2,
        name="coarse_outer",
    )(*x_sides, *inner)
    e1, e2, e3 = call(
        unfold, [(16, 16, 64), (8, 8, 32), (4, 4, 16)], [VMEM] * 3, flops=2000000, name="unfold"
    )(*owns)
    y_first, y_second = exchanged(f4, f4, "agg")
    y_first, e1, e2, e3 = lax.optimization_barrier((y_first, e1, e2, e3))
    (last,) = call(pack_last, [(8, LANES)], [VMEM] * 3, name="pack_last")(y_first, f4, y_second)
    x_sides = exchanged(last, last, "box")
    e4, rest = call(
        last_kernel, [(2, 2, 8), (2, 2, 8)], [VMEM] * 4, name="last"
    )(last, *x_sides, k4)
    return iterate, e1, e2, e3, e4, rest


def solution(mesh):
    spec = P("box", "agg", None)
    return jax.shard_map(
        per_device, mesh=mesh, in_specs=(spec,) * 4, out_specs=(spec,) * 6, check_vma=False
    )
```

```python
import functools

import jax
import jax.numpy as jnp
from jax import lax
from jax.experimental import pallas as pl
from jax.experimental.pallas import tpu as pltpu
from jax.sharding import PartitionSpec as P

F32 = jnp.float32
LANES = 128
FAR = 14


def coefficients(level_index):
    upper_edge = 1.1 * (2.0 + 0.02 * 4.0**level_index)
    lower_edge = upper_edge / 8.0
    midpoint = (upper_edge + lower_edge) / 2.0
    half_span = (upper_edge - lower_edge) / 2.0
    sigma_value = midpoint / half_span
    rho_first = 1.0 / sigma_value
    rho_second = 1.0 / (2.0 * sigma_value - rho_first)
    return (midpoint, rho_second * rho_first, 2.0 * rho_second / half_span)


def iota(shape, dim):
    return lax.broadcasted_iota(jnp.int32, shape, dim)


def edges(axis):
    here = lax.axis_index(axis)
    before = jnp.where(here > 0, 1.0, 0.0).astype(F32)
    after = jnp.where(here < lax.axis_size(axis) - 1, 1.0, 0.0).astype(F32)
    return before, after


def blurred(planes, stride):
    sums = [a + b for a, b in zip(planes[:-1], planes[1:])]
    out = []
    for low, high in zip(sums[:-1], sums[1:]):
        total = low + high
        beside = pltpu.roll(total, 1, 0) + pltpu.roll(total, total.shape[0] - 1, 0)
        out.append(blur_z((total + total) + beside, stride))
    return out


def across_of(axis):
    return "box" if axis == "agg" else "agg"


def moves_up(axis):
    return lax.axis_index(across_of(axis)) // (2 if axis == "box" else 1) % 2 == 0


def in_order(axis, first, second):
    up = moves_up(axis)
    return jnp.where(up, first, second), jnp.where(up, second, first)


def blur_z(values, stride):
    lane = iota(values.shape, 1)
    left = jnp.where(lane < stride, 0.0, pltpu.roll(values, stride, 1))
    right = jnp.where(lane >= LANES - stride, 0.0, pltpu.roll(values, LANES - stride, 1))
    return (values + values) + (left + right)


def pair_rows(values):
    return values + pltpu.roll(values, values.shape[0] - 1, 0)


def halved(values, stride):
    return (values + pltpu.roll(values, LANES - stride, 1)) * 0.5


def even_lanes(shape):
    return (iota(shape, len(shape) - 1) & 1) == 0


def loop(first, stop, size, body):
    count = (stop - first) // size
    if count == 1:
        body(first)
        return

    def step(i, carry):
        body(first + i * size)
        return carry

    lax.fori_loop(0, count, step, 0)


def copy_all(sems, *pairs):
    copies = [pltpu.make_async_copy(a, b, sems.at[i]) for i, (a, b) in enumerate(pairs)]
    for copy in copies:
        copy.start()
    return copies


def pack_rows(
    flags, guess, source, reaction, first, second,
    flag_smem, guess_lo, guess_hi, source_lo, source_hi, reaction_lo, reaction_hi, sems,
):
    lo, hi = pl.ds(0, 8), pl.ds(24, 8)
    copies = copy_all(
        sems,
        (flags, flag_smem),
        (guess.at[:, lo, :], guess_lo),
        (guess.at[:, hi, :], guess_hi),
        (source.at[:, lo, :], source_lo),
        (source.at[:, hi, :], source_hi),
        (reaction.at[:, lo, :], reaction_lo),
        (reaction.at[:, hi, :], reaction_hi),
    )
    for copy in copies:
        copy.wait()
    boxes = flags.shape[2]
    lane = iota((8, LANES), 1)
    flag = jnp.zeros((8, LANES), F32)
    for i in range(boxes):
        flag = jnp.where(lane // (LANES // boxes) == i, flag_smem[0, 0, i].astype(F32), flag)
    flag = flag[None]
    row = iota(first.shape, 1)
    up = jnp.where(
        row >= 5,
        guess_hi[...],
        jnp.where(
            row >= 3,
            pltpu.roll(source_hi[...], 5, 1),
            jnp.where(row >= 1, pltpu.roll(reaction_hi[...], 3, 1), flag),
        ),
    )
    down = jnp.where(
        row < 3,
        guess_lo[...],
        jnp.where(
            row < 5,
            pltpu.roll(source_lo[...], 3, 1),
            jnp.where(row < 7, pltpu.roll(reaction_lo[...], 5, 1), flag),
        ),
    )
    first[...], second[...] = in_order("agg", up, down)


def load_strips(after, guess, source, reaction, strip_up, strip_down, sems):
    copies = copy_all(
        sems,
        (guess.at[29:32], strip_up.at[0:3]),
        (source.at[30:32], strip_up.at[3:5]),
        (reaction.at[30:32], strip_up.at[5:7]),
        (guess.at[0:3], strip_down.at[0:3]),
        (source.at[0:2], strip_down.at[3:5]),
        (reaction.at[0:2], strip_down.at[5:7]),
    )
    for copy in copies:
        copy.wait()


def halo_tiles(from_before, from_after, before, after):
    row = iota(from_before.shape, 1)
    first = row < 4
    guess = jnp.where(first, from_after * after, from_before * before)
    source = jnp.where(first, pltpu.roll(from_after, 5, 1), pltpu.roll(from_before, 3, 1))
    reaction = jnp.where(first, pltpu.roll(from_after, 3, 1), pltpu.roll(from_before, 5, 1))
    return guess, source, reaction


def flag_plane(own, lo, hi):
    tile = (8, LANES)
    halo = jnp.where(iota(tile, 0) < 4, jnp.broadcast_to(hi, tile), jnp.broadcast_to(lo, tile))
    return jnp.concatenate([jnp.broadcast_to(own, (32, LANES)), halo], axis=0)


def pack_planes(own_first, own_second, from_first, from_second, strip_up, strip_down, first, second, mask):
    before, after = edges("agg")
    own, _ = in_order("agg", own_first[0, 0:1, :], own_second[0, 0:1, :])
    from_before, from_after = in_order("agg", from_first[...], from_second[...])
    lo = from_before[0, 0:1, :] * before
    hi = from_after[0, 7:8, :] * after
    mask[...] = flag_plane(own, lo, hi)
    planes = from_before.shape[0]
    strips, tiles = [], []
    for strip, at, local in ((strip_up, planes - 4, (1, 2, 2)), (strip_down, 0, (0, 0, 0))):
        fields = halo_tiles(from_before[at : at + 4], from_after[at : at + 4], before, after)
        rows = [tile[i] for tile, start, count in zip(fields, local, (3, 2, 2)) for i in range(start, start + count)]
        row = iota(rows[0].shape, 0)
        rows[0] = jnp.where(row == 3, own, jnp.where(row == 4, lo, rows[0]))
        rows[1] = jnp.where(row == 3, hi, rows[1])
        strips.append(strip[...])
        tiles.append(rows)
    first[:, 0:32, :], second[:, 0:32, :] = in_order("box", *strips)
    for i, (up, down) in enumerate(zip(*tiles)):
        first[i, 32:40, :], second[i, 32:40, :] = in_order("box", up, down)


SHIFT = 8.0 / 7.0


def even_rows(ref, i, rows):
    return ref[i, pl.ds(0, rows, stride=2), :]


def fine_inner(
    mask_ref, from_first, from_second, guess, source, reaction,
    g, s, k, d, u, w, coarse, pairs, kpairs, sems,
):
    rows = pl.ds(0, 32)
    copies = copy_all(
        sems, (guess, g.at[:, rows, :]), (source, s.at[:, rows, :]), (reaction, k.at[:, rows, :])
    )
    before, after = edges("agg")
    theta, c1, c2 = coefficients(0)

    def assemble(x):
        at = pl.ds(x, 32)
        sides = in_order("agg", from_first[at], from_second[at])
        tiles = halo_tiles(*sides, before, after)
        g[at, 32:40, :] = tiles[0]
        s[at, 32:40, :] = tiles[1]
        k[at, 32:40, :] = tiles[2]

    loop(0, 32, 32, assemble)
    for copy in copies:
        copy.wait()

    def remainders(field, x, size):
        planes = [field[x + i] for i in range(-1, size + 1)]
        mask = mask_ref[...]
        out = []
        for i, q in enumerate(blurred(planes, 1)):
            r = mask * (s[x + i] - (k[x + i] + SHIFT) * planes[i + 1] + q * (1.0 / 56.0))
            out.append((r, planes[i + 1]))
        return out

    def first(x):
        out = remainders(g, x, 10)
        for i, (r, middle) in enumerate(out):
            step = r * (1.0 / theta)
            d[x + i] = step
            u[x + i] = middle + step

    loop(1, 31, 10, first)

    def second(x):
        out = [m + (c1 * d[x + i] + c2 * r) for i, (r, m) in enumerate(remainders(u, x, 14))]
        for i, value in enumerate(out):
            w[x + i] = value

    loop(2, 30, 14, second)

    def third(x):
        out = [r for r, _ in remainders(w, x, 24)]
        at = (x - 4) // 2
        for i in range(len(out) // 2):
            pairs[at + i] = pair_rows(out[2 * i] + out[2 * i + 1])

    loop(4, 28, 24, third)

    for i in range(16):
        kpairs[i] = pair_rows(k[2 * i, 0:32, :] + k[2 * i + 1, 0:32, :])
    even = even_lanes((16, LANES))
    for i in range(16):
        value = pltpu.roll(halved(even_rows(kpairs, i, 16), 1), 1, 1)
        if 2 <= i < 14:
            value = jnp.where(even, halved(even_rows(pairs, i - 2, 16), 1), value)
        coarse[i] = value


def fine_outer(mask_ref, from_first, from_second, g, s, k, d, u, w, inner, coarse, edge, pairs):
    xbefore, xafter = edges("box")
    x_before, x_after = in_order("box", from_first[...], from_second[...])
    mask_before, mask_after = (
        flag_plane(x[0, 35:36], x[0, 36:37], x[1, 35:36]) * edge for x, edge in ((x_before, xbefore), (x_after, xafter))
    )
    theta, c1, c2 = coefficients(0)
    new_d, new_u, new_w = {}, {}, {}

    def side(x, before, after, own):
        return before(x + 3) if x < 0 else after(x - 32) if x > 31 else own(x)

    def guess_at(x):
        return side(x, lambda i: x_before[i] * xbefore, lambda i: x_after[i] * xafter, lambda i: g[i])

    def source_at(x):
        return side(x, lambda i: x_before[i + 2], lambda i: x_after[i + 3], lambda i: s[i])

    def reaction_at(x):
        return side(x, lambda i: x_before[i + 4], lambda i: x_after[i + 5], lambda i: k[i])

    def mask_at(x):
        return side(x, lambda i: mask_before, lambda i: mask_after, lambda i: mask_ref[...])

    def remainders(field, first, size):
        planes = [field(x) for x in range(first - 1, first + size + 1)]
        out = []
        for i, q in enumerate(blurred(planes, 1)):
            x = first + i
            r = mask_at(x) * (source_at(x) - (reaction_at(x) + SHIFT) * planes[i + 1] + q * (1.0 / 56.0))
            out.append((x, r, planes[i + 1]))
        return out

    for first in (-2, 31):
        for x, r, middle in remainders(guess_at, first, 3):
            new_d[x] = r * (1.0 / theta)
            new_u[x] = middle + new_d[x]
    for first in (-1, 30):
        for x, r, middle in remainders(lambda i: new_u[i] if i in new_u else u[i], first, 3):
            step = new_d[x] if x in new_d else d[x]
            new_w[x] = middle + (c1 * step + c2 * r)
    for at, x in enumerate((0, 1, 30, 31)):
        edge[at] = new_w[x][0:32]
    for at, first in enumerate((0, 28)):
        out = [r for _, r, _ in remainders(lambda i: new_w[i] if i in new_w else w[i], first, 4)]
        pairs[2 * at] = pair_rows(out[0] + out[1])
        pairs[2 * at + 1] = pair_rows(out[2] + out[3])
    even = even_lanes((16, LANES))
    for at, x in enumerate((0, 1, 14, 15)):
        coarse[x] = jnp.where(even, halved(even_rows(pairs, at, 16), 1), inner[x])
    coarse[2:14] = inner[2:14]


def level_constants(level):
    theta, c1, c2 = coefficients(level)
    return (1.0 + c1) / theta + c2, c2 / theta


def masks_of(rows, lo, hi):
    before, after = edges("agg")
    xbefore, xafter = edges("box")
    shape = (rows, LANES)
    row = iota(shape, 0)
    inside = jnp.where(row < lo, before, jnp.where(row >= hi, after, 1.0))
    return inside * jnp.where(even_lanes(shape), xbefore, xafter), inside


def corrections(level, planes, reactions, masks):
    alpha, beta = level_constants(level)
    return [
        m * (f * (alpha - beta * (k + SHIFT)) + q * (beta / 56.0))
        for f, k, m, q in zip(planes[1:-1], reactions, masks, blurred(planes, 2**level))
    ]


def coarse_remainders(level, planes, fields, reactions):
    return [
        f - (k + SHIFT) * e + q * (1.0 / 56.0)
        for f, k, e, q in zip(fields, reactions, planes[1:-1], blurred(planes, 2**level))
    ]


def to_left(values):
    return pltpu.roll(values, LANES - 1, 1)


def to_right(values):
    return pltpu.roll(values, 1, 1)


def swap(values):
    return jnp.where(even_lanes(values.shape), to_left(values), to_right(values))


def folded(lo, hi):
    even = even_lanes(lo.shape)
    return jnp.where(even, lo, to_right(hi)), jnp.where(even, to_left(lo), hi)


def coarse_inner(y_before, own, y_after, f, k, e, f2, k2, pairs, kpairs):
    _, inside = masks_of(48, 16, 32)
    fields, reactions = [], []
    for j in range(8):
        lo = jnp.concatenate([y_before[j], own[j], y_after[j]], axis=0)
        hi = jnp.concatenate([y_before[15 - j], own[15 - j], y_after[15 - j]], axis=0)
        field, reaction = folded(lo, hi)
        fields.append(field * inside)
        reactions.append(reaction)
    for j in range(2):
        f[j], k[j] = fields[j], reactions[j]
    for j in range(3):
        kpairs[j] = pair_rows(reactions[2 * j + 2] + reactions[2 * j + 3])
    value = corrections(1, fields + [swap(fields[7])], reactions[1:], [inside] * 7)
    for j in range(7):
        e[j + 1] = value[j]
    rest = coarse_remainders(1, value + [swap(value[6])], fields[2:], reactions[2:])
    for j in range(3):
        pairs[j] = pair_rows(rest[2 * j] + rest[2 * j + 1])
    _, inside = masks_of(24, 8, 16)
    for j in range(3):
        f2[j] = halved(even_rows(pairs, j, 24), 2) * inside
        k2[j] = halved(even_rows(kpairs, j, 24), 2)


def coarse_outer(
    from_first, from_second, f_in, k_in, e_in, f2_in, k2_in, own1, own2, own3, f4, k4,
    pairs, kpairs,
):
    outside, inside = masks_of(48, 16, 32)
    fields, reactions = [], []
    x_before, x_after = in_order("box", from_first[...], from_second[...])
    for j in range(FAR):
        field, reaction = folded(x_before[j], x_after[FAR - 1 - j])
        fields.append(field * outside)
        reactions.append(reaction)
    for j in range(2):
        fields.append(f_in[j])
        reactions.append(k_in[j])
    for j in range(7):
        kpairs[j] = pair_rows(reactions[2 * j + 2] + reactions[2 * j + 3])
    value = corrections(1, fields, reactions[1:15], [outside] * 13 + [inside])
    own1[0] = value[13][16:32]
    for j in range(1, 8):
        own1[j] = e_in[j, 16:32, :]
    rest = coarse_remainders(1, value + [e_in[1], e_in[2]], fields[2:], reactions[2:])
    for j in range(7):
        pairs[j] = pair_rows(rest[2 * j] + rest[2 * j + 1])
    outside, inside = masks_of(24, 8, 16)
    fields = [halved(even_rows(pairs, j, 24), 2) * (outside if j < 6 else inside) for j in range(7)]
    fields += [f2_in[j] for j in range(3)]
    reactions = [halved(even_rows(kpairs, j, 24), 2) for j in range(7)] + [k2_in[j] for j in range(3)]
    for p in range(4):
        kpairs[p, 0:24, :] = pair_rows(reactions[2 * p + 2] + reactions[2 * p + 3])
    value = corrections(2, fields + [swap(fields[9])], reactions[1:], [outside] * 5 + [inside] * 4)
    for j in range(4):
        own2[j] = value[5 + j][8:16]
    rest = coarse_remainders(2, value + [swap(value[8])], fields[2:], reactions[2:])
    for p in range(4):
        pairs[p, 0:24, :] = pair_rows(rest[2 * p] + rest[2 * p + 1])
    outside, inside = masks_of(16, 4, 8)
    fields = [halved(even_rows(pairs, j, 16), 4) * (outside if j < 2 else inside) for j in range(4)]
    reactions = [halved(even_rows(kpairs, j, 16), 4) for j in range(4)]
    for p in range(2):
        kpairs[p, 0:16, :] = pair_rows(reactions[2 * p] + reactions[2 * p + 1])
    value = corrections(3, fields + [swap(fields[3])], reactions[1:], [outside, inside, inside])
    for j in range(2):
        own3[j] = value[1 + j][0:8]
    rest = coarse_remainders(3, value + [swap(value[2])], fields[2:], reactions[2:])
    pairs[0, 0:16, :] = pair_rows(rest[0] + rest[1])
    f4[...] = halved(even_rows(pairs, 0, 8), 8)
    for p in range(2):
        k4[p] = halved(even_rows(kpairs, p, 8), 8)


def unfold(own1, own2, own3, e1, e2, e3):
    rows = (slice(0, 16), slice(0, 8), slice(4, 8))
    for level, own, out, part in zip((1, 2, 3), (own1, own2, own3), (e1, e2, e3), rows):
        planes, _, lanes = out.shape
        source = iota((LANES, LANES), 0)
        target = iota((LANES, LANES), 1)
        hit = source == ((target & 63) << level) + (target >> 6)
        values = own[...].reshape(-1, LANES)
        values = jnp.dot(
            values,
            jnp.where(hit, 1.0, 0.0).astype(F32),
            precision=lax.Precision.HIGHEST,
            preferred_element_type=F32,
        ).reshape(own.shape)
        for j in range(planes // 2):
            value = values[j]
            out[j] = value[part, 0:lanes]
            out[planes - 1 - j] = pltpu.roll(value, 64, 1)[part, 0:lanes]


def pack_last(from_first, own, from_second, out):
    before, after = edges("agg")
    row = iota(own.shape, 0)
    y_before, y_after = in_order("agg", from_first[...], from_second[...])
    lo = pltpu.roll(y_before, 6, 0) * before
    hi = pltpu.roll(y_after, 2, 0) * after
    out[...] = jnp.where(row < 2, lo, jnp.where(row < 4, own[...], jnp.where(row < 6, hi, 0.0)))


def last_kernel(own, from_first, from_second, k4, e4, rest):
    outside, inside = masks_of(8, 2, 4)
    even = even_lanes(own.shape)
    row = iota(own.shape, 0)
    inside = jnp.where(row < 6, inside, 0.0)
    outside = jnp.where(row < 6, outside, 0.0)
    middle = own[...] * inside
    x_before, x_after = in_order("box", from_first[...], from_second[...])
    fields = [
        jnp.where(even, x_before, x_after) * outside,
        swap(jnp.where(even, x_after, x_before)) * outside,
        middle,
        swap(middle),
    ]
    value = corrections(4, fields, [k4[0], k4[1]], [outside, inside])
    left = coarse_remainders(4, value + [swap(value[1])], [middle], [k4[1]])[0]
    lane = iota(own.shape, 1)
    for out, here in ((e4, value[1]), (rest, left)):
        for side, folded_plane in enumerate((here, to_left(here))):
            cells = [
                jnp.where(lane == z, pltpu.roll(folded_plane, (LANES - 15 * z) % LANES, 1), 0.0)
                for z in range(8)
            ]
            while len(cells) > 1:
                cells = [a + b for a, b in zip(cells[::2], cells[1::2])]
            out[side] = cells[0][2:4, 0:8]


def exchanged(first, second, axis):
    names = ("box", "agg")
    along = names.index(axis)
    sizes = [lax.axis_size(name) for name in names]
    route = []
    for source in range(sizes[0] * sizes[1]):
        at = list(divmod(source, sizes[1]))
        width = 2 if axis == "box" else 1
        step = 1 if at[1 - along] // width % 2 == 0 else -1
        if 0 <= at[along] + step < sizes[along]:
            at[along] += step
        else:
            at[1 - along] += step * width
        route.append((source, at[0] * sizes[1] + at[1]))
    inverse = [(target, source) for source, target in route]
    return lax.ppermute(first, names, route), lax.ppermute(second, names, inverse)


VMEM = pl.BlockSpec(memory_space=pltpu.VMEM)
HBM = pl.BlockSpec(memory_space=pltpu.HBM)


def call(body, outs, ins, scratch=(), copies=0, flops=0, name=None):
    sems = [pltpu.SemaphoreType.DMA((copies,))] if copies else []
    return pl.pallas_call(
        body,
        out_shape=[jax.ShapeDtypeStruct(dims, F32) for dims in outs],
        in_specs=ins,
        out_specs=[VMEM] * len(outs),
        scratch_shapes=[s if not isinstance(s, tuple) else pltpu.VMEM(s, F32) for s in scratch] + sems,
        compiler_params=pltpu.CompilerParams(vmem_limit_bytes=40 * 1024 * 1024),
        cost_estimate=pl.CostEstimate(flops=flops, transcendentals=0, bytes_accessed=flops),
        name=name,
    )


def per_device(source, guess, reaction, flags):
    tile = (32, 8, LANES)
    flags, guess, source, reaction = (
        pltpu.with_memory_space_constraint(v, pltpu.HBM) for v in (flags, guess, source, reaction)
    )
    packed = call(
        pack_rows,
        [tile, tile],
        [HBM] * 4,
        scratch=[pltpu.SMEM((1, 1, flags.shape[2]), jnp.int32)] + [tile] * 6,
        copies=7,
        name="pack_rows",
    )(flags, guess, source, reaction)
    strip_up, strip_down = call(
        load_strips, [(7, 32, LANES)] * 2, [VMEM] + [HBM] * 3, copies=6, name="load_strips"
    )(packed[0], guess, source, reaction)
    y_sides = exchanged(*packed, "agg")
    *packed, mask = call(
        pack_planes, [(7, 40, LANES)] * 2 + [(40, LANES)], [VMEM] * 6, name="pack_planes"
    )(*packed, *y_sides, strip_up, strip_down)
    x_sides = exchanged(*packed, "box")
    big = (32, 40, LANES)
    *fields, inner = call(
        fine_inner,
        [big] * 6 + [(16, 16, LANES)],
        [VMEM] * 3 + [HBM] * 3,
        scratch=[(12, 40, LANES), (16, 32, LANES)],
        copies=3,
        flops=8000000,
        name="fine_inner",
    )(mask, *y_sides, guess, source, reaction)
    coarse, edge = call(
        fine_outer,
        [(16, 16, LANES), (4, 32, LANES)],
        [VMEM] * 10,
        scratch=[(4, 40, LANES)],
        name="fine_outer",
    )(mask, *x_sides, *fields, inner)
    iterate = jnp.concatenate([edge[0:2], fields[5][2:30, 0:32], edge[2:4]], axis=0)
    y_first, y_second = exchanged(coarse, coarse, "agg")
    y_first, iterate = lax.optimization_barrier((y_first, iterate))
    y_before, y_after = in_order("agg", y_first, y_second)
    extended = jnp.concatenate([y_before, coarse, y_after], axis=1)
    x_sides = exchanged(*in_order("box", extended[16 - FAR :], extended[:FAR]), "box")
    plane = (48, LANES)
    inner = call(
        coarse_inner,
        [(2,) + plane] * 2 + [(8,) + plane] + [(3, 24, LANES)] * 2,
        [VMEM] * 3,
        scratch=[(3,) + plane] * 2,
        flops=4000000,
        name="coarse_inner",
    )(y_before, coarse, y_after)
    *owns, f4, k4 = call(
        coarse_outer,
        [(8, 16, LANES), (4, 8, LANES), (2, 8, LANES), (8, LANES), (2, 8, LANES)],
        [VMEM] * 7,
        scratch=[(7,) + plane] * 2,
        name="coarse_outer",
    )(*x_sides, *inner)
    e1, e2, e3 = call(
        unfold, [(16, 16, 64), (8, 8, 32), (4, 4, 16)], [VMEM] * 3, flops=2000000, name="unfold"
    )(*owns)
    y_first, y_second = exchanged(f4, f4, "agg")
    y_first, e1, e2, e3 = lax.optimization_barrier((y_first, e1, e2, e3))
    (last,) = call(pack_last, [(8, LANES)], [VMEM] * 3, name="pack_last")(y_first, f4, y_second)
    x_sides = exchanged(last, last, "box")
    e4, rest = call(
        last_kernel, [(2, 2, 8), (2, 2, 8)], [VMEM] * 4, name="last"
    )(last, *x_sides, k4)
    return iterate, e1, e2, e3, e4, rest


def solution(mesh):
    spec = P("box", "agg", None)
    return jax.shard_map(
        per_device, mesh=mesh, in_specs=(spec,) * 4, out_specs=(spec,) * 6, check_vma=False
    )
```
